32 devices in a mesh: sim: 8 (over y, x, core), ana: 4 (over z).
Axes of the slice: x: 2, y: 2, z: 4, core: 2. Of those that a mesh axis runs over, the one named last changes fastest.
Arguments:
- initial_disp: float32 [256, 512, 128], P('ana', 'sim'), may hold values from -24 to 24
- initial_vel: float32 [256, 512, 128], P('ana', 'sim'), may hold values from -2 to 2
- stiffness: float32 [512, 128], P('sim'), may hold values from 0.05 to 0.35
- basis: float32 [512, 128, 512], P(('sim', 'ana')), may hold values from -5 to 5
- rotation: float32 [768, 512], replicated, may hold values from -0.21875 to 0.21875
Outputs:
- basis_out: float32 [512, 128, 512], P(('sim', 'ana'))
- coords: float32 [512, 256], replicated
The draws below stay inside these ranges and needn't reach their ends.
All inputs are finite; a program needn't handle non-finite values.
Results may differ from the reference program's by a relative error of at most 0.000054.
Values sent between devices are 32-bit elements; how exact they have to be, the bound alone decides.
No kernel may reach another device: no remote copies, remote signals or barrier semaphores. Data moves between devices by JAX's collectives and lax.ppermute only.
A program may use at most 64 MiB of HBM per device.

```python
import math
import jax
import jax.numpy as jnp
from jax import lax

M = 256
K = 512
KA = 768
NY = 128
STEPS = 4
NX = 512


def shared_basis(key):
    basis_key = jax.random.fold_in(key, 7)
    return jnp.clip(jax.random.normal(basis_key, (NX, NY, K), jnp.float32), -5.0, 5.0)


def draw_basis(key, part):
    return shared_basis(key)


def draw_initial_disp(key, part):
    basis_draw = shared_basis(key)
    leading_modes = jnp.transpose(basis_draw[:, :, :M], (2, 0, 1))
    member_noise = jnp.clip(jax.random.normal(jax.random.fold_in(key, 8), (M, NX, NY), jnp.float32), -5.0, 5.0)
    common = jnp.clip(jax.random.normal(jax.random.fold_in(key, 9), (NX, NY), jnp.float32), -5.0, 5.0)
    line_ramp = 1.0 + 2.0 * jnp.arange(NX, dtype=jnp.float32) / max(NX - 1, 1)
    return line_ramp[None, :, None] * (0.5 * leading_modes + 0.5 * common[None] + 0.5 * member_noise)


def level_of(stream_key, dims, split, smallest, high):
    level = 1.0
    for axis_at, shards_of in split:
        heights = jax.random.uniform(jax.random.fold_in(jax.random.fold_in(stream_key, 6), axis_at), (shards_of,), jnp.float32, smallest / len(split), high / len(split))
        level = level * jnp.repeat(jnp.exp(heights), dims[axis_at] // shards_of).reshape((-1,) + (1,) * (len(dims) - 1 - axis_at))
    return level


def gaussian(stream_key, dims, deviation, bound, cuts=(), kind=jnp.bfloat16):
    drawn = jax.random.normal(stream_key, dims, jnp.float32) * deviation
    if len(cuts) > 0:
        drawn = level_of(stream_key, dims, cuts, -0.22, 0.18) * drawn
    return jnp.clip(drawn, min=-bound, max=bound).astype(kind)


def setup_inputs(seed: int = 0) -> dict:
    keys = jax.random.split(jax.random.key(seed), 6)
    return {
        "initial_disp": draw_initial_disp(jax.random.fold_in(keys[5], 71), 0),
        "initial_vel": gaussian(keys[1], (M, NX, NY), 0.3, 2.0, ((0, 4), (1, 8)), jnp.float32),
        "stiffness": jnp.clip(0.05 + 0.29999999 * jax.random.uniform(keys[2], (NX, NY), jnp.float32) ** level_of(keys[2], (NX, NY), ((0, 8),), -0.2, 0.2), 0.05, 0.35),
        "basis": draw_basis(jax.random.fold_in(keys[5], 71), 0),
        "rotation": gaussian(keys[4], (KA, K), KA ** -0.5, 0.21875, (), jnp.float32),
    }


epsilon = 1e-06

def accelerate(displace, stiffness):
    padded = jnp.pad(displace, ((0, 0), (1, 1), (1, 1)))
    laplace = padded[:, 2:, 1:-1] + padded[:, :-2, 1:-1] + padded[:, 1:-1, 2:] + padded[:, 1:-1, :-2] - 4.0 * displace
    return stiffness[None] * (laplace - 0.5 * displace * displace * displace / (1.0 + displace * displace))

def contract(left, right, left_dim, right_dim):
    return lax.dot_general(left.astype(jnp.float32), right.astype(jnp.float32), (((left_dim,), (right_dim,)), ((), ())), precision=lax.Precision.HIGHEST, preferred_element_type=jnp.float32)

def reference(initial_disp, initial_vel, stiffness, basis, rotation):
    displace = initial_disp
    velocity = initial_vel
    for step_index in range(STEPS):
        velocity = velocity + accelerate(displace, stiffness)
        displace = displace + velocity
    row_count = NX * NY
    col_scale = jnp.sqrt(lax.optimization_barrier(jnp.sum(displace * displace, axis=(1, 2))) / row_count + epsilon)
    panel_rows = (displace / col_scale[:, None, None]).reshape(M, row_count)
    basis_rows = basis.reshape(row_count, K)
    coefficients = contract(basis_rows, panel_rows, 0, 1) / row_count
    remainder = panel_rows - contract(coefficients, basis_rows, 0, 1)
    gram_matrix = contract(remainder, remainder, 1, 1) / row_count
    factor = jnp.linalg.cholesky(gram_matrix)
    fresh_basis = jax.scipy.linalg.solve_triangular(factor, remainder, lower=True)
    top_rows = rotation[:K]
    bottom_rows = rotation[K:]
    basis_out = contract(basis_rows, top_rows, 1, 0) + contract(fresh_basis, bottom_rows, 0, 0)
    coords = (contract(top_rows, coefficients, 0, 0) + contract(bottom_rows, factor, 0, 1)) * math.sqrt(K)
    return (basis_out.reshape(NX, NY, K), coords)
```

```python
import math

import jax
import jax.numpy as jnp
from jax import lax
from jax.sharding import PartitionSpec as P

STEPS = 4
EPS = 1e-06
HI = lax.Precision.HIGHEST


def xor_permute(value, axis, mask):
    size = lax.axis_size(axis)
    return lax.ppermute(value, axis, [(i, i ^ mask) for i in range(size)])


def block_of(value, index, size):
    return lax.dynamic_slice_in_dim(value, index * size, size, axis=0)


def reduce_all(value):
    sim = lax.axis_index("sim")
    chips = lax.axis_size("sim") // 2
    core, chip = sim % 2, sim // 2
    half = value.shape[0] // 2
    got = xor_permute(block_of(value, 1 - core, half), "sim", 1)
    part = block_of(value, core, half) + got
    piece = half // chips
    got = [xor_permute(block_of(part, chip ^ k, piece), "sim", 2 * k) for k in range(1, chips)]
    total = block_of(part, chip, piece)
    for g in got:
        total = total + g
    got = [xor_permute(total, "ana", k) for k in range(1, lax.axis_size("ana"))]
    ana = lax.axis_index("ana")
    stack = jnp.stack([total] + got)
    total = stack[0 ^ ana]
    for k in range(1, lax.axis_size("ana")):
        total = total + stack[k ^ ana]
    got = [total] + [xor_permute(total, "sim", 2 * k) for k in range(1, chips)]
    stack = jnp.stack(got)
    part = jnp.concatenate([stack[chip ^ k] for k in range(chips)], axis=0)
    other = xor_permute(part, "sim", 1)
    low = jnp.where(core == 0, part, other)
    high = jnp.where(core == 0, other, part)
    return jnp.concatenate([low, high], axis=0)


def accelerate(displace, stiffness):
    inner = displace[:, 1:-1]
    padded = jnp.pad(inner, ((0, 0), (0, 0), (1, 1)))
    laplace = displace[:, 2:] + displace[:, :-2] + padded[:, :, 2:] + padded[:, :, :-2] - 4.0 * inner
    return stiffness[None] * (laplace - 0.5 * inner * inner * inner / (1.0 + inner * inner))


def pack_symmetric(value):
    n = value.shape[0] // 128
    tiles = [value[128 * i:128 * (i + 1), 128 * j:128 * (j + 1)] for i in range(n) for j in range(i, n)]
    flat = jnp.concatenate(tiles, axis=0)
    half = flat.shape[0] // 2
    return jnp.concatenate([flat[:half], flat[half:]], axis=1)


def unpack_symmetric(packed, n):
    flat = jnp.concatenate([packed[:, :128], packed[:, 128:]], axis=0)
    n = n // 128
    tiles = {}
    at = 0
    for i in range(n):
        for j in range(i, n):
            tiles[i, j] = flat[128 * at:128 * (at + 1)]
            tiles[j, i] = tiles[i, j].T
            at += 1
    return jnp.concatenate([jnp.concatenate([tiles[i, j] for j in range(n)], axis=1) for i in range(n)], axis=0)


def dot(left, right, dims):
    return lax.dot_general(left, right, (dims, ((), ())), precision=HI, preferred_element_type=jnp.float32)


def per_device(initial_disp, initial_vel, stiffness, basis, rotation):
    ranks = lax.axis_size("ana")
    sims = lax.axis_size("sim")
    ana = lax.axis_index("ana")
    lines, width, rank = basis.shape
    rows = lines * width
    count = rows * sims * ranks
    members = initial_disp.shape[0]
    w = STEPS

    up = [(i, i + 1) for i in range(sims - 1)]
    down = [(j, i) for i, j in up]

    def edge(start, stop):
        parts = [initial_disp[:, start:stop], initial_vel[:, start:stop], stiffness[None, start:stop]]
        return jnp.concatenate(parts, axis=0)

    block = initial_disp.shape[1]
    before = lax.ppermute(edge(block - w, block), "sim", up)
    after = lax.ppermute(edge(0, w), "sim", down)

    basis_rows = basis.reshape(rows, rank)
    own = pack_symmetric(dot(basis_rows, basis_rows, ((0,), (0,))))
    basis_gram = unpack_symmetric(reduce_all(own), rank) / count

    def joined(value, first, last):
        return jnp.concatenate([before[first:last], value, after[first:last]], axis=1)

    displace = joined(initial_disp, 0, members)
    velocity = joined(initial_vel, members, 2 * members)[:, 1:-1]
    stiff = joined(stiffness[None], 2 * members, 2 * members + 1)[0, 1:-1]
    for step in range(STEPS):
        velocity = velocity + accelerate(displace, stiff)
        displace = displace[:, 1:-1] + velocity
        velocity = velocity[:, 1:-1]
        stiff = stiff[1:-1]

    def lines_of(k):
        return lax.dynamic_slice_in_dim(displace, (ana ^ k) * lines, lines, axis=1)

    arrived = jnp.zeros((members * ranks, lines, width), jnp.float32)
    for k in range(ranks):
        piece = lines_of(k)
        if k:
            piece = xor_permute(piece, "ana", k)
        arrived = lax.dynamic_update_slice_in_dim(arrived, piece, (ana ^ k) * members, axis=0)
    snaps = arrived.reshape(members * ranks, rows)
    total_members = members * ranks
    cross = dot(basis_rows, snaps, ((0,), (1,)))
    inner = dot(snaps, snaps, ((1,), (1,)))
    packed = reduce_all(jnp.concatenate([cross, pack_symmetric(inner)], axis=0))
    cross, inner = packed[:rank], unpack_symmetric(packed[rank:], total_members)
    scale = jnp.sqrt(jnp.diagonal(inner) / count + EPS)
    coefficients = cross / (count * scale)[None, :]
    inner = inner / count / (scale[:, None] * scale[None, :])
    correct = 2.0 * coefficients - dot(basis_gram, coefficients, ((1,), (0,)))
    gram = inner - dot(coefficients, correct, ((0,), (0,)))
    factor = jnp.linalg.cholesky(gram)
    top_rows = rotation[:rank]
    bottom_rows = rotation[rank:]
    mix = jax.scipy.linalg.solve_triangular(factor, bottom_rows, lower=True, trans=1)
    weights = top_rows - dot(coefficients, mix, ((1,), (0,)))
    basis_out = dot(basis_rows, weights, ((1,), (0,))) + dot(snaps, mix / scale[:, None], ((0,), (0,)))
    coords = (dot(top_rows, coefficients, ((0,), (0,))) + dot(bottom_rows, factor, ((0,), (1,)))) * math.sqrt(rank)
    return (basis_out.reshape(basis.shape), coords)


def solution(mesh):
    in_specs = (
        P("ana", "sim", None),
        P("ana", "sim", None),
        P("sim", None),
        P(("sim", "ana"), None, None),
        P(),
    )
    out_specs = (P(("sim", "ana"), None, None), P())
    return jax.shard_map(
        per_device, mesh=mesh, in_specs=in_specs, out_specs=out_specs, check_vma=False
    )
```

```python
import functools
import math

import jax
import jax.numpy as jnp
from jax import lax
from jax.experimental import pallas as pl
from jax.experimental.pallas import tpu as pltpu
from jax.sharding import PartitionSpec as P

STEPS = 4
EPS = 1e-06
MIB = 1024 * 1024
HI = lax.Precision.HIGHEST
SCALARS = pl.BlockSpec(memory_space=pltpu.SMEM)


def mm(left, right, dims, precision=HI):
    return lax.dot_general(left, right, (dims, ((), ())), precision=precision, preferred_element_type=jnp.float32)


def shape(*dims, dtype=jnp.float32):
    return jax.ShapeDtypeStruct(dims, dtype)


def params(mib):
    return pltpu.CompilerParams(vmem_limit_bytes=mib * MIB)


def xor_permute(value, axis, mask):
    size = lax.axis_size(axis)
    return lax.ppermute(value, axis, [(i, i ^ mask) for i in range(size)])


def to_lines_kernel(disp_ref, vel_ref, stiff_ref, disp_out, vel_out, last_ref, first_ref):
    lines, group, _ = disp_out.shape
    for line in range(lines):
        disp_out[line] = disp_ref[pl.ds(line, group, stride=lines), :]
        vel_out[line] = vel_ref[pl.ds(line, group, stride=lines), :]
    w = STEPS
    for ref, start in ((last_ref, lines - w), (first_ref, 0)):
        for i in range(w):
            ref[i] = disp_ref[pl.ds(start + i, group, stride=lines), :]
            ref[w + i] = vel_ref[pl.ds(start + i, group, stride=lines), :]
        ref[2 * w] = jnp.zeros_like(ref[2 * w])
        ref[2 * w, :w, :] = stiff_ref[start:start + w, :]


def to_lines(disp, vel, stiff):
    members, lines, width = disp.shape
    group = 16
    w = STEPS
    flat = pl.BlockSpec((group * lines, width), lambda i: (i, 0))
    out = pl.BlockSpec((lines, group, width), lambda i: (0, i, 0))
    edge = pl.BlockSpec((2 * w + 1, group, width), lambda i: (0, i, 0))
    return pl.pallas_call(
        to_lines_kernel,
        grid=(members // group,),
        in_specs=[flat, flat, pl.BlockSpec((lines, width), lambda i: (0, 0))],
        out_specs=[out, out, edge, edge],
        out_shape=[shape(lines, members, width)] * 2 + [shape(2 * w + 1, members, width)] * 2,
        compiler_params=params(32),
        name="to_lines",
    )(disp.reshape(members * lines, width), vel.reshape(members * lines, width), stiff)


def evolve_kernel(index_ref, disp_ref, vel_ref, stiff_ref, before_ref, after_ref, *rest, masks, size):
    outs, (disp_pad, vel_pad, stiff_pad) = rest[:len(masks)], rest[len(masks):]
    lines, members, width = disp_ref.shape
    w = STEPS
    blocks = lines // size
    lane = lax.broadcasted_iota(jnp.int32, (8, width), 1)
    for mask, out in zip(masks, outs):
        block = index_ref[0] ^ mask
        start = block * size
        disp_pad[w:w + size] = disp_ref[pl.ds(start, size)]
        vel_pad[w:w + size] = vel_ref[pl.ds(start, size)]
        stiff_pad[8:8 + size, :] = stiff_ref[pl.ds(pl.multiple_of(start, 8), size), :]

        @pl.when(block == 0)
        def _():
            disp_pad[:w] = before_ref[:w]
            vel_pad[:w] = before_ref[w:2 * w]
            stiff_pad[8 - w:8, :] = before_ref[2 * w, :w, :]

        @pl.when(block > 0)
        def _():
            low = jnp.maximum(start - w, 0)
            disp_pad[:w] = disp_ref[pl.ds(low, w)]
            vel_pad[:w] = vel_ref[pl.ds(low, w)]
            stiff_pad[:8, :] = stiff_ref[pl.ds(pl.multiple_of(jnp.maximum(start - 8, 0), 8), 8), :]

        @pl.when(block == blocks - 1)
        def _():
            disp_pad[w + size:] = after_ref[:w]
            vel_pad[w + size:] = after_ref[w:2 * w]
            stiff_pad[8 + size:8 + size + w, :] = after_ref[2 * w, :w, :]

        @pl.when(block < blocks - 1)
        def _():
            high = jnp.minimum(start + size, lines - 8)
            disp_pad[w + size:] = disp_ref[pl.ds(high, w)]
            vel_pad[w + size:] = vel_ref[pl.ds(high, w)]
            stiff_pad[8 + size:, :] = stiff_ref[pl.ds(pl.multiple_of(high, 8), 8), :]

        def group_step(g, carry):
            at = pl.ds(pl.multiple_of(g * 8, 8), 8)
            disp = {i: disp_pad[i, at, :] for i in range(size + 2 * w)}
            vel = {i: vel_pad[i, at, :] for i in range(1, size + 2 * w - 1)}
            for step in range(1, w + 1):
                new = {}
                for i in range(step, size + 2 * w - step):
                    u = disp[i]
                    right = jnp.where(lane == width - 1, 0.0, pltpu.roll(u, width - 1, 1))
                    left = jnp.where(lane == 0, 0.0, pltpu.roll(u, 1, 1))
                    laplace = disp[i + 1] + disp[i - 1] + right + left - 4.0 * u
                    square = u * u
                    stiff = jnp.broadcast_to(stiff_pad[8 - w + i:8 - w + i + 1, :], (8, width))
                    vel[i] = vel[i] + stiff * (laplace - 0.5 * u * (square / (1.0 + square)))
                    new[i] = u + vel[i]
                disp = new
            for i in range(size):
                out[i, at, :] = disp[w + i]
            return carry

        lax.fori_loop(0, members // 8, group_step, 0)


def evolve(index, disp, vel, stiff, before, after, masks, size):
    lines, members, width = disp.shape
    w = STEPS
    return pl.pallas_call(
        functools.partial(evolve_kernel, masks=masks, size=size),
        in_specs=[SCALARS] + [pl.BlockSpec(memory_space=pltpu.VMEM)] * 5,
        out_shape=[shape(size, members, width)] * len(masks),
        scratch_shapes=[pltpu.VMEM((size + 2 * w, members, width), jnp.float32)] * 2
        + [pltpu.VMEM((size + 16, width), jnp.float32)],
        compiler_params=params(32),
        name="evolve" + "".join(str(m) for m in masks),
    )(index, disp, vel, stiff, before, after)


def products_kernel(index_ref, basis_ref, *rest):
    pieces, (send_ref, keep_ref, snap_ref, sum_ref) = rest[:-4], rest[-4:]
    lines, members, width = pieces[0].shape
    rank = basis_ref.shape[-1]
    step = pl.program_id(0)
    for k, piece in enumerate(pieces):
        at = pl.multiple_of((index_ref[0] ^ k) * members, members)
        for line in range(lines):
            snap_ref[pl.ds(at, members), line * width:(line + 1) * width] = piece[line]

    @pl.when(step == 0)
    def _():
        sum_ref[...] = jnp.zeros_like(sum_ref)

    snap = snap_ref[...]
    rows = basis_ref[...].reshape(lines * width, rank)
    sum_ref[:, :rank] += mm(snap, rows, ((1,), (0,)))
    sum_ref[:, rank:] += mm(snap, snap, ((1,), (1,)))

    @pl.when(step == pl.num_programs(0) - 1)
    def _():
        half = keep_ref.shape[0]
        core = index_ref[1]
        keep_ref[...] = sum_ref[pl.ds(pl.multiple_of(core * half, half), half), :]
        send_ref[...] = sum_ref[pl.ds(pl.multiple_of((1 - core) * half, half), half), :]


def products(index, basis, pieces):
    lines, width, rank = basis.shape
    members = pieces[0].shape[1]
    total = members * len(pieces)
    block = 2
    half = pl.BlockSpec((total // 2, rank + total), lambda i: (0, 0))
    return pl.pallas_call(
        products_kernel,
        grid=(lines // block,),
        in_specs=[SCALARS, pl.BlockSpec((block, width, rank), lambda i: (i, 0, 0))]
        + [pl.BlockSpec((block, members, width), lambda i: (i, 0, 0))] * len(pieces),
        out_specs=[half, half],
        out_shape=[shape(total // 2, rank + total)] * 2,
        scratch_shapes=[pltpu.VMEM((total, block * width), jnp.float32), pltpu.VMEM((total, rank + total), jnp.float32)],
        compiler_params=params(32),
        name="products",
    )(index, basis, *pieces)


def split_kernel(index_ref, keep_ref, got_ref, *outs):
    rows = outs[0].shape[0]
    for k, out in enumerate(outs):
        at = pl.ds(pl.multiple_of((index_ref[2] ^ k) * rows, rows), rows)
        out[...] = keep_ref[at, :] + got_ref[at, :]


def split(index, keep, got, chips):
    rows, cols = keep.shape
    return pl.pallas_call(
        split_kernel,
        in_specs=[SCALARS] + [pl.BlockSpec(memory_space=pltpu.VMEM)] * 2,
        out_shape=[shape(rows // chips, cols)] * chips,
        compiler_params=params(16),
        name="split",
    )(index, keep, got)


def tree_sum(values):
    while len(values) > 1:
        values = [a + b for a, b in zip(values[::2], values[1::2])]
    return values[0]


def chip_scatter(index, send, keep):
    chips = lax.axis_size("sim") // 2
    got = xor_permute(send, "sim", 1)
    pieces = split(index, keep, got, chips)
    return tree_sum([pieces[0]] + [xor_permute(pieces[k], "sim", 2 * k) for k in range(1, chips)])


def ana_sum(value):
    return tree_sum([value] + [xor_permute(value, "ana", k) for k in range(1, lax.axis_size("ana"))])


def chip_gather(value):
    chips = lax.axis_size("sim") // 2
    mine = jnp.concatenate([value] + [xor_permute(value, "sim", 2 * k) for k in range(1, chips)], axis=0)
    return mine, xor_permute(mine, "sim", 1)


PANEL = 32

def eliminate(work_ref, members):
    tiles = work_ref.shape[1] // 128
    groups = PANEL // 8
    sub = lax.broadcasted_iota(jnp.int32, (8, 128), 0)

    def panel_step(k, carry):
        start = pl.multiple_of(k * PANEL, PANEL)
        at = pl.multiple_of((k * PANEL) // 128 * 128, 128)
        diag = work_ref[pl.ds(start, PANEL), pl.ds(at, 128)]
        diag = pltpu.roll(diag, (128 - (k * PANEL) % 128) % 128, 1)
        rows = work_ref[pl.ds(start, PANEL), :]
        x = [[rows[8 * g:8 * g + 8, 128 * t:128 * t + 128] for t in range(tiles)] + [diag[8 * g:8 * g + 8]]
             for g in range(groups)]
        for b in range(groups):
            cols = {g: [jnp.broadcast_to(x[g][tiles][:, 8 * b + j:8 * b + j + 1], (8, 128)) for j in range(8)]
                    for g in range(b, groups)}
            pivots = jnp.ones((8, 128), jnp.float32)
            for r in range(8):
                pivot = jnp.broadcast_to(cols[b][r][r:r + 1], (8, 128))
                pivots = jnp.where(sub == r, pivot, pivots)
                inverse = 1.0 / pivot
                raw = [jnp.broadcast_to(v[r:r + 1], (8, 128)) for v in x[b]]
                craw = [jnp.broadcast_to(cols[b][j][r:r + 1], (8, 128)) if j > r else None for j in range(8)]
                for g in range(b, groups):
                    coef = cols[g][r] * inverse
                    if g == b:
                        coef = jnp.where(sub > r, coef, 0.0)
                    x[g] = [v - coef * w for v, w in zip(x[g], raw)]
                    cols[g] = [cols[g][j] - coef * craw[j] if j > r else cols[g][j] for j in range(8)]
            x[b] = [v * lax.rsqrt(pivots) for v in x[b]]
        done = jnp.concatenate([jnp.concatenate(v[:tiles], axis=1) for v in x], axis=0)
        lane = lax.broadcasted_iota(jnp.int32, (PANEL, members), 1)
        lower = jnp.where(lane >= start + PANEL, done[:, :members], 0.0)
        work_ref[...] = work_ref[...] - mm(lower, done, ((0,), (0,)))
        work_ref[pl.ds(start, PANEL), :] = done
        return carry

    lax.fori_loop(0, members // PANEL, panel_step, 0)


def ordered(index_ref, mine_ref, other_ref, out_ref, chips):
    half = mine_ref.shape[0]
    rows = half // chips
    for k in range(chips):
        at = (index_ref[2] ^ k) * rows
        piece = slice(k * rows, (k + 1) * rows)
        out_ref[pl.ds(pl.multiple_of(index_ref[1] * half + at, rows), rows), :] = mine_ref[piece, :]
        out_ref[pl.ds(pl.multiple_of((1 - index_ref[1]) * half + at, rows), rows), :] = other_ref[piece, :]


def solve_kernel(index_ref, sums_ref, sums2_ref, gram_ref, gram2_ref, rot_ref, w_ref, coords_ref,
                 work_ref, all_ref, basis_ref, *, count, chips):
    members, rank = coords_ref.shape
    ordered(index_ref, sums_ref, sums2_ref, all_ref, chips)
    ordered(index_ref, gram_ref, gram2_ref, basis_ref, chips)
    row = lax.broadcasted_iota(jnp.int32, (members, members), 0)
    col = lax.broadcasted_iota(jnp.int32, (members, members), 1)
    eye = row == col
    inner = all_ref[:, rank:]
    diag = jnp.where(eye, inner, 0.0)
    across = lax.rsqrt(jnp.sum(diag, axis=0, keepdims=True) / count + EPS)
    along = lax.rsqrt(jnp.sum(diag, axis=1, keepdims=True) / count + EPS)
    coef = all_ref[:, :rank] * (along / count)
    correct = 2.0 * coef - mm(coef, basis_ref[...], ((1,), (0,))) / count
    work_ref[:, :members] = inner * (along / count) * across - mm(correct, coef, ((1,), (1,)))
    work_ref[:, members:] = jnp.where(eye, 1.0, 0.0)
    eliminate(work_ref, members)
    top, bottom = rot_ref[:rank, :], rot_ref[rank:, :]
    upper = jnp.where(row <= col, work_ref[:, :members], 0.0)
    mix = mm(work_ref[:, members:], bottom, ((0,), (0,)))
    w_ref[:rank, :] = top - mm(coef, mix, ((0,), (0,)))
    w_ref[rank:, :] = mix * along
    coords_ref[...] = (mm(coef, top, ((1,), (0,))) + mm(upper, bottom, ((0,), (0,)))) * math.sqrt(rank)


def solve(index, sums, gram, rotation, count, chips):
    rank = gram[0].shape[1]
    members = rotation.shape[0] - rank
    return pl.pallas_call(
        functools.partial(solve_kernel, count=float(count), chips=chips),
        in_specs=[SCALARS] + [pl.BlockSpec(memory_space=pltpu.VMEM)] * 5,
        out_shape=(shape(members + rank, rank), shape(members, rank)),
        scratch_shapes=[pltpu.VMEM((members, 2 * members), jnp.float32),
                        pltpu.VMEM((members, rank + members), jnp.float32),
                        pltpu.VMEM((rank, rank), jnp.float32)],
        compiler_params=params(40),
        name="solve",
    )(index, *sums, *gram, rotation)


def rotate_kernel(index_ref, weights_ref, basis_ref, *rest):
    pieces, (out_ref, snap_ref) = rest[:-2], rest[-2:]
    lines, members, width = pieces[0].shape
    rank = basis_ref.shape[-1]
    for k, piece in enumerate(pieces):
        at = pl.multiple_of((index_ref[0] ^ k) * members, members)
        for line in range(lines):
            snap_ref[pl.ds(at, members), line * width:(line + 1) * width] = piece[line]
    rows = basis_ref[...].reshape(lines * width, rank)
    out = mm(rows, weights_ref[:rank, :], ((1,), (0,))) + mm(snap_ref[...], weights_ref[rank:, :], ((0,), (0,)))
    out_ref[...] = out.reshape(out_ref.shape)


def rotate(index, weights, basis, pieces):
    lines, width, rank = basis.shape
    members = pieces[0].shape[1]
    block = 2
    rows = pl.BlockSpec((block, width, rank), lambda i: (i, 0, 0))
    return pl.pallas_call(
        rotate_kernel,
        grid=(lines // block,),
        in_specs=[SCALARS, pl.BlockSpec(weights.shape, lambda i: (0, 0)), rows]
        + [pl.BlockSpec((block, members, width), lambda i: (i, 0, 0))] * len(pieces),
        out_specs=rows,
        out_shape=shape(lines, width, rank),
        scratch_shapes=[pltpu.VMEM((members * len(pieces), block * width), jnp.float32)],
        compiler_params=params(32),
        name="rotate",
    )(index, weights, basis, *pieces)


def per_device(initial_disp, initial_vel, stiffness, basis, rotation):
    ranks, sims = lax.axis_size("ana"), lax.axis_size("sim")
    ana, sim = lax.axis_index("ana"), lax.axis_index("sim")
    lines, width, rank = basis.shape
    count = lines * width * sims * ranks
    chips = sims // 2
    core = sim % 2
    index = jnp.stack([ana, core, sim // 2]).astype(jnp.int32)

    disp, vel, last, first = to_lines(initial_disp, initial_vel, stiffness)
    up = [(i, i + 1) for i in range(sims - 1)]
    before = lax.ppermute(last, "sim", up)
    after = lax.ppermute(first, "sim", [(j, i) for i, j in up])

    rows = basis.reshape(lines * width, rank)
    gram = mm(rows, rows, ((0,), (0,)))
    half = rank // 2
    keep = lax.dynamic_slice_in_dim(gram, core * half, half, axis=0)
    send = lax.dynamic_slice_in_dim(gram, (1 - core) * half, half, axis=0)
    gram = chip_scatter(index, send, keep)

    far = tuple(range(ranks // 2, ranks))
    near = tuple(range(ranks // 2))
    pieces = {}
    for masks in (far, near):
        found = evolve(index, disp, vel, stiffness, before, after, masks, lines)
        for mask, piece in zip(masks, found):
            pieces[mask] = xor_permute(piece, "ana", mask) if mask else piece
    pieces = [pieces[k] for k in range(ranks)]

    send, keep = products(index, basis, pieces)
    sums = chip_gather(ana_sum(chip_scatter(index, send, keep)))
    gram = chip_gather(ana_sum(gram))
    weights, coords = solve(index, sums, gram, rotation, count, chips)
    return rotate(index, weights, basis, pieces), coords.T


def solution(mesh):
    in_specs = (
        P("ana", "sim", None),
        P("ana", "sim", None),
        P("sim", None),
        P(("sim", "ana"), None, None),
        P(),
    )
    out_specs = (P(("sim", "ana"), None, None), P())
    return jax.shard_map(
        per_device, mesh=mesh, in_specs=in_specs, out_specs=out_specs, check_vma=False
    )
```

```python
import functools
import math

import jax
import jax.numpy as jnp
from jax import lax
from jax.experimental import pallas as pl
from jax.experimental.pallas import tpu as pltpu
from jax.sharding import PartitionSpec as P

STEPS = 4
EPS = 1e-06
MIB = 1024 * 1024
HI = lax.Precision.HIGHEST
FIRST = 4
SCALARS = pl.BlockSpec(memory_space=pltpu.SMEM)


def mm(left, right, dims, precision=HI):
    return lax.dot_general(left, right, (dims, ((), ())), precision=precision, preferred_element_type=jnp.float32)


def shape(*dims, dtype=jnp.float32):
    return jax.ShapeDtypeStruct(dims, dtype)


def params(mib):
    return pltpu.CompilerParams(vmem_limit_bytes=mib * MIB)


def in_hbm(value):
    return pltpu.with_memory_space_constraint(value, pltpu.HBM)


def halves(value):
    high = value.astype(jnp.bfloat16)
    return high, (value - high.astype(jnp.float32)).astype(jnp.bfloat16)


def mm3(left, right, dims):
    (lh, ll), (rh, rl) = left, right
    return mm(lh, rh, dims, None) + (mm(lh, rl, dims, None) + mm(ll, rh, dims, None))


def xor_permute(value, axis, mask):
    size = lax.axis_size(axis)
    return lax.ppermute(value, axis, [(i, i ^ mask) for i in range(size)])


def to_lines_kernel(disp_ref, vel_ref, stiff_ref, disp_out, vel_out, last_ref, first_ref):
    lines, group, _ = disp_out.shape
    for line in range(lines):
        disp_out[line] = disp_ref[pl.ds(line, group, stride=lines), :]
        vel_out[line] = vel_ref[pl.ds(line, group, stride=lines), :]
    w = STEPS
    for ref, start in ((last_ref, lines - w), (first_ref, 0)):
        for i in range(w):
            ref[i] = disp_ref[pl.ds(start + i, group, stride=lines), :]
            ref[w + i] = vel_ref[pl.ds(start + i, group, stride=lines), :]
        ref[2 * w] = jnp.zeros_like(ref[2 * w])
        ref[2 * w, :w, :] = stiff_ref[start:start + w, :]


def to_lines(disp, vel, stiff):
    members, lines, width = disp.shape
    group = 16
    w = STEPS
    flat = pl.BlockSpec((group * lines, width), lambda i: (i, 0))
    out = pl.BlockSpec((lines, group, width), lambda i: (0, i, 0))
    edge = pl.BlockSpec((2 * w + 1, group, width), lambda i: (0, i, 0))
    return pl.pallas_call(
        to_lines_kernel,
        grid=(members // group,),
        in_specs=[flat, flat, pl.BlockSpec((lines, width), lambda i: (0, 0))],
        out_specs=[out, out, edge, edge],
        out_shape=[shape(lines, members, width)] * 2 + [shape(2 * w + 1, members, width)] * 2,
        compiler_params=params(32),
        name="to_lines",
    )(in_hbm(disp.reshape(members * lines, width)), in_hbm(vel.reshape(members * lines, width)), stiff)


def evolve_kernel(index_ref, disp_ref, vel_ref, stiff_ref, before_ref, after_ref, out, disp_pad, vel_pad, stiff_pad, *, slot):
    size = out.shape[0]
    lines, members, width = disp_ref.shape
    w = STEPS
    blocks = lines // size
    lane = lax.broadcasted_iota(jnp.int32, (8, width), 1)
    block = index_ref[0] ^ index_ref[FIRST + slot]
    start = block * size
    disp_pad[w:w + size] = disp_ref[pl.ds(start, size)]
    vel_pad[w:w + size] = vel_ref[pl.ds(start, size)]
    stiff_pad[8:8 + size, :] = stiff_ref[pl.ds(pl.multiple_of(start, 8), size), :]

    @pl.when(block == 0)
    def _():
        disp_pad[:w] = before_ref[:w]
        vel_pad[:w] = before_ref[w:2 * w]
        stiff_pad[8 - w:8, :] = before_ref[2 * w, :w, :]

    @pl.when(block > 0)
    def _():
        low = jnp.maximum(start - w, 0)
        disp_pad[:w] = disp_ref[pl.ds(low, w)]
        vel_pad[:w] = vel_ref[pl.ds(low, w)]
        stiff_pad[:8, :] = stiff_ref[pl.ds(pl.multiple_of(jnp.maximum(start - 8, 0), 8), 8), :]

    @pl.when(block == blocks - 1)
    def _():
        disp_pad[w + size:] = after_ref[:w]
        vel_pad[w + size:] = after_ref[w:2 * w]
        stiff_pad[8 + size:8 + size + w, :] = after_ref[2 * w, :w, :]

    @pl.when(block < blocks - 1)
    def _():
        high = jnp.minimum(start + size, lines - 8)
        disp_pad[w + size:] = disp_ref[pl.ds(high, w)]
        vel_pad[w + size:] = vel_ref[pl.ds(high, w)]
        stiff_pad[8 + size:, :] = stiff_ref[pl.ds(pl.multiple_of(high, 8), 8), :]

    def group_step(g, carry):
        at = pl.ds(pl.multiple_of(g * 8, 8), 8)
        disp = {i: disp_pad[i, at, :] for i in range(size + 2 * w)}
        vel = {i: vel_pad[i, at, :] for i in range(1, size + 2 * w - 1)}
        for step in range(1, w + 1):
            new = {}
            for i in range(step, size + 2 * w - step):
                u = disp[i]
                right = jnp.where(lane == width - 1, 0.0, pltpu.roll(u, width - 1, 1))
                left = jnp.where(lane == 0, 0.0, pltpu.roll(u, 1, 1))
                around = (disp[i + 1] + disp[i - 1]) + (right + left)
                stiff = jnp.broadcast_to(stiff_pad[8 - w + i:8 - w + i + 1, :], (8, width))
                vel[i] = vel[i] + stiff * (around + u * (0.5 * pl.reciprocal(1.0 + u * u) - 4.5))
                new[i] = u + vel[i]
            disp = new
        for i in range(size):
            out[i, at, :] = disp[w + i]
        return carry

    lax.fori_loop(0, members // 8, group_step, 0)


def evolve(index, disp, vel, stiff, before, after, slot, size):
    lines, members, width = disp.shape
    w = STEPS
    return pl.pallas_call(
        functools.partial(evolve_kernel, slot=slot),
        in_specs=[SCALARS] + [pl.BlockSpec(memory_space=pltpu.VMEM)] * 5,
        out_shape=shape(size, members, width),
        scratch_shapes=[pltpu.VMEM((size + 2 * w, members, width), jnp.float32)] * 2
        + [pltpu.VMEM((size + 16, width), jnp.float32)],
        compiler_params=params(16),
        name="evolve%d" % slot,
    )(index, disp, vel, stiff, before, after)


def basis_gram_kernel(index_ref, basis_ref, send_ref, keep_ref, sum_ref, mixed_ref):
    lines, width, rank = basis_ref.shape
    step = pl.program_id(0)

    @pl.when(step == 0)
    def _():
        sum_ref[...] = jnp.zeros_like(sum_ref)
        mixed_ref[...] = jnp.zeros_like(mixed_ref)

    high, low = halves(basis_ref[...].reshape(lines * width, rank))
    sum_ref[...] += mm(high, high, ((0,), (0,)), None)
    mixed_ref[...] += mm(high, low, ((0,), (0,)), None)

    @pl.when(step == pl.num_programs(0) - 1)
    def _():
        sum_ref[...] += mixed_ref[...] + mixed_ref[...].T
        half = keep_ref.shape[0]
        core = index_ref[1]
        keep_ref[...] = sum_ref[pl.ds(pl.multiple_of(core * half, half), half), :]
        send_ref[...] = sum_ref[pl.ds(pl.multiple_of((1 - core) * half, half), half), :]


def basis_gram(index, basis):
    lines, width, rank = basis.shape
    block = 2
    half = pl.BlockSpec((rank // 2, rank), lambda i: (0, 0))
    return pl.pallas_call(
        basis_gram_kernel,
        grid=(lines // block,),
        in_specs=[SCALARS, pl.BlockSpec((block, width, rank), lambda i: (i, 0, 0))],
        out_specs=[half, half],
        out_shape=[shape(rank // 2, rank)] * 2,
        scratch_shapes=[pltpu.VMEM((rank, rank), jnp.float32)] * 2,
        compiler_params=params(24),
        name="basis_gram",
    )(index, in_hbm(basis))


def products_kernel(index_ref, basis_ref, *rest):
    pieces, (send_ref, keep_ref, snap_ref, sum_ref) = rest[:-4], rest[-4:]
    lines, members, width = pieces[0].shape
    rank = basis_ref.shape[-1]
    step = pl.program_id(0)
    for k, piece in enumerate(pieces):
        at = pl.multiple_of((index_ref[0] ^ index_ref[FIRST + k]) * members, members)
        for line in range(lines):
            snap_ref[pl.ds(at, members), line * width:(line + 1) * width] = piece[line]

    @pl.when(step == 0)
    def _():
        sum_ref[...] = jnp.zeros_like(sum_ref)

    snap = snap_ref[...]
    rows = basis_ref[...].reshape(lines * width, rank)
    sum_ref[:, :rank] += mm3(halves(snap), halves(rows), ((1,), (0,)))
    sum_ref[:, rank:] += mm(snap, snap, ((1,), (1,)))

    @pl.when(step == pl.num_programs(0) - 1)
    def _():
        half = keep_ref.shape[0]
        core = index_ref[1]
        keep_ref[...] = sum_ref[pl.ds(pl.multiple_of(core * half, half), half), :]
        send_ref[...] = sum_ref[pl.ds(pl.multiple_of((1 - core) * half, half), half), :]


def products(index, basis, pieces):
    lines, width, rank = basis.shape
    members = pieces[0].shape[1]
    total = members * len(pieces)
    block = 2
    half = pl.BlockSpec((total // 2, rank + total), lambda i: (0, 0))
    return pl.pallas_call(
        products_kernel,
        grid=(lines // block,),
        in_specs=[SCALARS, pl.BlockSpec((block, width, rank), lambda i: (i, 0, 0))]
        + [pl.BlockSpec((block, members, width), lambda i: (i, 0, 0))] * len(pieces),
        out_specs=[half, half],
        out_shape=[shape(total // 2, rank + total)] * 2,
        scratch_shapes=[pltpu.VMEM((total, block * width), jnp.float32), pltpu.VMEM((total, rank + total), jnp.float32)],
        compiler_params=params(32),
        name="products",
    )(index, in_hbm(basis), *pieces)


def split_kernel(index_ref, keep_ref, got_ref, *outs):
    rows = outs[0].shape[0]
    for k, out in enumerate(outs):
        at = pl.ds(pl.multiple_of((index_ref[2] ^ k) * rows, rows), rows)
        out[...] = keep_ref[at, :] + got_ref[at, :]


def split(index, keep, got, chips):
    rows, cols = keep.shape
    return pl.pallas_call(
        split_kernel,
        in_specs=[SCALARS] + [pl.BlockSpec(memory_space=pltpu.VMEM)] * 2,
        out_shape=[shape(rows // chips, cols)] * chips,
        compiler_params=params(16),
        name="split",
    )(index, keep, got)


def tree_sum(values):
    while len(values) > 1:
        values = [a + b for a, b in zip(values[::2], values[1::2])]
    return values[0]


def chip_scatter(index, send, keep):
    chips = lax.axis_size("sim") // 2
    got = xor_permute(send, "sim", 1)
    pieces = split(index, keep, got, chips)
    return tree_sum([pieces[0]] + [xor_permute(pieces[k], "sim", 2 * k) for k in range(1, chips)])


def ana_sum(value):
    return tree_sum([value] + [xor_permute(value, "ana", k) for k in range(1, lax.axis_size("ana"))])


def ana_sum_halved(value):
    ranks = lax.axis_size("ana")
    top = lax.axis_index("ana") // (ranks // 2)
    half = value.shape[0] // 2
    send = lax.dynamic_slice_in_dim(value, (1 - top) * half, half, axis=0)
    total = lax.dynamic_slice_in_dim(value, top * half, half, axis=0) + xor_permute(send, "ana", ranks // 2)
    bit = 1
    while bit < ranks // 2:
        total = total + xor_permute(total, "ana", bit)
        bit *= 2
    return jnp.concatenate([total, xor_permute(total, "ana", ranks // 2)], axis=0)


def chip_gather(value):
    chips = lax.axis_size("sim") // 2
    mine = jnp.concatenate([value] + [xor_permute(value, "sim", 2 * k) for k in range(1, chips)], axis=0)
    return mine, xor_permute(mine, "sim", 1)


PANEL = 32

def eliminate(work_ref, members):
    tiles = work_ref.shape[1] // 128
    groups = PANEL // 8
    sub = lax.broadcasted_iota(jnp.int32, (8, 128), 0)

    def panel_step(k, carry):
        start = pl.multiple_of(k * PANEL, PANEL)
        at = pl.multiple_of((k * PANEL) // 128 * 128, 128)
        diag = work_ref[pl.ds(start, PANEL), pl.ds(at, 128)]
        diag = pltpu.roll(diag, (128 - (k * PANEL) % 128) % 128, 1)
        rows = work_ref[pl.ds(start, PANEL), :]
        x = [[rows[8 * g:8 * g + 8, 128 * t:128 * t + 128] for t in range(tiles)] + [diag[8 * g:8 * g + 8]]
             for g in range(groups)]
        for b in range(groups):
            cols = {g: [jnp.broadcast_to(x[g][tiles][:, 8 * b + j:8 * b + j + 1], (8, 128)) for j in range(8)]
                    for g in range(b, groups)}
            pivots = jnp.ones((8, 128), jnp.float32)
            for r in range(8):
                pivot = jnp.broadcast_to(cols[b][r][r:r + 1], (8, 128))
                pivots = jnp.where(sub == r, pivot, pivots)
                inverse = 1.0 / pivot
                raw = [jnp.broadcast_to(v[r:r + 1], (8, 128)) for v in x[b]]
                craw = [jnp.broadcast_to(cols[b][j][r:r + 1], (8, 128)) if j > r else None for j in range(8)]
                for g in range(b, groups):
                    coef = cols[g][r] * inverse
                    if g == b:
                        coef = jnp.where(sub > r, coef, 0.0)
                    x[g] = [v - coef * w for v, w in zip(x[g], raw)]
                    cols[g] = [cols[g][j] - coef * craw[j] if j > r else cols[g][j] for j in range(8)]
            x[b] = [v * lax.rsqrt(pivots) for v in x[b]]
        done = jnp.concatenate([jnp.concatenate(v[:tiles], axis=1) for v in x], axis=0)
        lane = lax.broadcasted_iota(jnp.int32, (PANEL, members), 1)
        lower = jnp.where(lane >= start + PANEL, done[:, :members], 0.0)
        work_ref[...] = work_ref[...] - mm(lower, done, ((0,), (0,)))
        work_ref[pl.ds(start, PANEL), :] = done
        return carry

    lax.fori_loop(0, members // PANEL, panel_step, 0)


def ordered(index_ref, mine_ref, other_ref, out_ref, chips, parts):
    half = mine_ref.shape[0]
    rows = half // chips // parts
    for k in range(chips * parts):
        at = (index_ref[2] ^ (k // parts)) * (rows * parts)
        if parts > 1:
            at = at + (index_ref[3] ^ (k % parts)) * rows
        piece = slice(k * rows, (k + 1) * rows)
        out_ref[pl.ds(pl.multiple_of(index_ref[1] * half + at, rows), rows), :] = mine_ref[piece, :]
        out_ref[pl.ds(pl.multiple_of((1 - index_ref[1]) * half + at, rows), rows), :] = other_ref[piece, :]


def solve_kernel(index_ref, sums_ref, sums2_ref, gram_ref, gram2_ref, rot_ref, high_ref, low_ref, coords_ref,
                 work_ref, all_ref, basis_ref, *, count, chips):
    rank, members = coords_ref.shape
    ordered(index_ref, sums_ref, sums2_ref, all_ref, chips, 1)
    ordered(index_ref, gram_ref, gram2_ref, basis_ref, chips, 2)
    row = lax.broadcasted_iota(jnp.int32, (members, members), 0)
    col = lax.broadcasted_iota(jnp.int32, (members, members), 1)
    eye = row == col
    inner = all_ref[:, rank:]
    diag = jnp.where(eye, inner, 0.0)
    across = lax.rsqrt(jnp.sum(diag, axis=0, keepdims=True) / count + EPS)
    along = lax.rsqrt(jnp.sum(diag, axis=1, keepdims=True) / count + EPS)
    coef = all_ref[:, :rank] * (along / count)
    correct = 2.0 * coef - mm(coef, basis_ref[...], ((1,), (0,))) / count
    work_ref[:, :members] = inner * (along / count) * across - mm(correct, coef, ((1,), (1,)))
    work_ref[:, members:] = jnp.where(eye, 1.0, 0.0)
    eliminate(work_ref, members)
    top, bottom = rot_ref[:rank, :], rot_ref[rank:, :]
    upper = jnp.where(row <= col, work_ref[:, :members], 0.0)
    mix = mm(work_ref[:, members:], bottom, ((0,), (0,)))
    high_ref[:rank, :], low_ref[:rank, :] = halves(top - mm(coef, mix, ((0,), (0,))))
    high_ref[rank:, :], low_ref[rank:, :] = halves(mix * along)
    coords = (mm(coef, top, ((1,), (0,))) + mm(upper, bottom, ((0,), (0,)))) * math.sqrt(rank)
    coords_ref[...] = coords.T


def solve(index, sums, gram, rotation, count, chips):
    rank = gram[0].shape[1]
    members = rotation.shape[0] - rank
    return pl.pallas_call(
        functools.partial(solve_kernel, count=float(count), chips=chips),
        in_specs=[SCALARS] + [pl.BlockSpec(memory_space=pltpu.VMEM)] * 5,
        out_shape=[shape(members + rank, rank, dtype=jnp.bfloat16)] * 2 + [shape(rank, members)],
        scratch_shapes=[pltpu.VMEM((members, 2 * members), jnp.float32),
                        pltpu.VMEM((members, rank + members), jnp.float32),
                        pltpu.VMEM((rank, rank), jnp.float32)],
        compiler_params=params(40),
        name="solve",
    )(index, *sums, *gram, rotation)


def rotate_kernel(index_ref, high_ref, low_ref, basis_ref, *rest):
    pieces, (out_ref, snap_ref) = rest[:-2], rest[-2:]
    lines, members, width = pieces[0].shape
    rank = basis_ref.shape[-1]
    for k, piece in enumerate(pieces):
        at = pl.multiple_of((index_ref[0] ^ index_ref[FIRST + k]) * members, members)
        for line in range(lines):
            snap_ref[pl.ds(at, members), line * width:(line + 1) * width] = piece[line]
    rows = basis_ref[...].reshape(lines * width, rank)
    out = mm3(halves(rows), (high_ref[:rank, :], low_ref[:rank, :]), ((1,), (0,)))
    out = out + mm3(halves(snap_ref[...].T), (high_ref[rank:, :], low_ref[rank:, :]), ((1,), (0,)))
    out_ref[...] = out.reshape(out_ref.shape)


def rotate(index, high, low, basis, pieces):
    lines, width, rank = basis.shape
    members = pieces[0].shape[1]
    block = 2
    rows = pl.BlockSpec((block, width, rank), lambda i: (i, 0, 0))
    return pl.pallas_call(
        rotate_kernel,
        grid=(lines // block,),
        in_specs=[SCALARS] + [pl.BlockSpec(high.shape, lambda i: (0, 0))] * 2 + [rows]
        + [pl.BlockSpec((block, members, width), lambda i: (i, 0, 0))] * len(pieces),
        out_specs=rows,
        out_shape=shape(lines, width, rank),
        scratch_shapes=[pltpu.VMEM((members * len(pieces), block * width), jnp.float32)],
        compiler_params=params(32),
        name="rotate",
    )(index, high, low, in_hbm(basis), *pieces)


def per_device(initial_disp, initial_vel, stiffness, basis, rotation):
    ranks, sims = lax.axis_size("ana"), lax.axis_size("sim")
    ana, sim = lax.axis_index("ana"), lax.axis_index("sim")
    lines, width, rank = basis.shape
    count = lines * width * sims * ranks
    chips = sims // 2
    core = sim % 2
    near, far = list(range(1, ranks // 2)), list(range(ranks // 2, ranks))
    orders = (near + far[::-1] + [0], far[::-1] + near + [0])
    masks = jnp.where(core == 0, jnp.array(orders[0]), jnp.array(orders[1]))
    first_index = jnp.stack([ana, core, sim // 2, ana // (ranks // 2)])
    index = jnp.concatenate([first_index, masks]).astype(jnp.int32)

    disp, vel, last, first = to_lines(initial_disp, initial_vel, stiffness)
    up = [(i, i + 1) for i in range(sims - 1)]
    before = lax.ppermute(last, "sim", up)
    after = lax.ppermute(first, "sim", [(j, i) for i, j in up])

    basis_late, _ = lax.optimization_barrier((basis, last[0, 0, 0]))
    send, keep = basis_gram(index, basis_late)
    before, after, send = lax.optimization_barrier((before, after, send))

    pieces = []
    for slot in range(ranks):
        piece = evolve(index, disp, vel, stiffness, before, after, slot, lines)
        if slot < ranks - 1:
            pairs = [(s * ranks + a, s * ranks + (a ^ orders[s % 2][slot])) for s in range(sims) for a in range(ranks)]
            piece = lax.ppermute(piece, ("sim", "ana"), pairs)
        pieces.append(piece)
    pieces[-1], send = lax.optimization_barrier((pieces[-1], send))
    gram = chip_scatter(index, send, keep)
    gram = chip_gather(ana_sum_halved(gram))
    pieces, gram = lax.optimization_barrier((pieces, gram))

    send, keep = products(index, basis, pieces)
    sums = chip_gather(ana_sum(chip_scatter(index, send, keep)))
    high, low, coords = solve(index, sums, gram, rotation, count, chips)
    return rotate(index, high, low, basis, pieces), coords


def solution(mesh):
    in_specs = (
        P("ana", "sim", None),
        P("ana", "sim", None),
        P("sim", None),
        P(("sim", "ana"), None, None),
        P(),
    )
    out_specs = (P(("sim", "ana"), None, None), P())
    return jax.shard_map(
        per_device, mesh=mesh, in_specs=in_specs, out_specs=out_specs, check_vma=False
    )
```

```python
import functools
import math

import jax
import jax.numpy as jnp
from jax import lax
from jax.experimental import pallas as pl
from jax.experimental.pallas import tpu as pltpu
from jax.sharding import PartitionSpec as P

STEPS = 4
EPS = 1e-06
MIB = 1024 * 1024
HI = lax.Precision.HIGHEST
FIRST = 4
SCALARS = pl.BlockSpec(memory_space=pltpu.SMEM)


def mm(left, right, dims, precision=HI):
    return lax.dot_general(left, right, (dims, ((), ())), precision=precision, preferred_element_type=jnp.float32)


def shape(*dims, dtype=jnp.float32):
    return jax.ShapeDtypeStruct(dims, dtype)


def params(mib):
    return pltpu.CompilerParams(vmem_limit_bytes=mib * MIB)


def in_hbm(value):
    return pltpu.with_memory_space_constraint(value, pltpu.HBM)


def halves(value):
    high = value.astype(jnp.bfloat16)
    return high, (value - high.astype(jnp.float32)).astype(jnp.bfloat16)


def mm3(left, right, dims):
    (lh, ll), (rh, rl) = left, right
    return mm(lh, rh, dims, None) + (mm(lh, rl, dims, None) + mm(ll, rh, dims, None))


def xor_permute(value, axis, mask):
    size = lax.axis_size(axis)
    return lax.ppermute(value, axis, [(i, i ^ mask) for i in range(size)])


def to_lines_kernel(disp_ref, vel_ref, stiff_ref, disp_out, vel_out, last_ref, first_ref):
    lines, group, _ = disp_out.shape
    for line in range(lines):
        disp_out[line] = disp_ref[pl.ds(line, group, stride=lines), :]
        vel_out[line] = vel_ref[pl.ds(line, group, stride=lines), :]
    w = STEPS
    for ref, start in ((last_ref, lines - w), (first_ref, 0)):
        for i in range(w):
            ref[i] = disp_ref[pl.ds(start + i, group, stride=lines), :]
            ref[w + i] = vel_ref[pl.ds(start + i, group, stride=lines), :]
        ref[2 * w] = jnp.zeros_like(ref[2 * w])
        ref[2 * w, :w, :] = stiff_ref[start:start + w, :]


def to_lines(disp, vel, stiff):
    members, lines, width = disp.shape
    group = 16
    w = STEPS
    flat = pl.BlockSpec((group * lines, width), lambda i: (i, 0))
    out = pl.BlockSpec((lines, group, width), lambda i: (0, i, 0))
    edge = pl.BlockSpec((2 * w + 1, group, width), lambda i: (0, i, 0))
    return pl.pallas_call(
        to_lines_kernel,
        grid=(members // group,),
        in_specs=[flat, flat, pl.BlockSpec((lines, width), lambda i: (0, 0))],
        out_specs=[out, out, edge, edge],
        out_shape=[shape(lines, members, width)] * 2 + [shape(2 * w + 1, members, width)] * 2,
        compiler_params=params(32),
        name="to_lines",
    )(in_hbm(disp.reshape(members * lines, width)), in_hbm(vel.reshape(members * lines, width)), stiff)


def evolve_kernel(index_ref, disp_ref, vel_ref, stiff_ref, before_ref, after_ref, out, disp_pad, vel_pad, stiff_pad, *, slot):
    size = out.shape[0]
    lines, members, width = disp_ref.shape
    w = STEPS
    blocks = lines // size
    lane = lax.broadcasted_iota(jnp.int32, (8, width), 1)
    block = index_ref[0] ^ index_ref[FIRST + slot]
    start = block * size
    disp_pad[w:w + size] = disp_ref[pl.ds(start, size)]
    vel_pad[w:w + size] = vel_ref[pl.ds(start, size)]
    stiff_pad[8:8 + size, :] = stiff_ref[pl.ds(pl.multiple_of(start, 8), size), :]

    @pl.when(block == 0)
    def _():
        disp_pad[:w] = before_ref[:w]
        vel_pad[:w] = before_ref[w:2 * w]
        stiff_pad[8 - w:8, :] = before_ref[2 * w, :w, :]

    @pl.when(block > 0)
    def _():
        low = jnp.maximum(start - w, 0)
        disp_pad[:w] = disp_ref[pl.ds(low, w)]
        vel_pad[:w] = vel_ref[pl.ds(low, w)]
        stiff_pad[:8, :] = stiff_ref[pl.ds(pl.multiple_of(jnp.maximum(start - 8, 0), 8), 8), :]

    @pl.when(block == blocks - 1)
    def _():
        disp_pad[w + size:] = after_ref[:w]
        vel_pad[w + size:] = after_ref[w:2 * w]
        stiff_pad[8 + size:8 + size + w, :] = after_ref[2 * w, :w, :]

    @pl.when(block < blocks - 1)
    def _():
        high = jnp.minimum(start + size, lines - 8)
        disp_pad[w + size:] = disp_ref[pl.ds(high, w)]
        vel_pad[w + size:] = vel_ref[pl.ds(high, w)]
        stiff_pad[8 + size:, :] = stiff_ref[pl.ds(pl.multiple_of(high, 8), 8), :]

    def group_step(g, carry):
        at = pl.ds(pl.multiple_of(g * 8, 8), 8)
        disp = {i: disp_pad[i, at, :] for i in range(size + 2 * w)}
        vel = {i: vel_pad[i, at, :] for i in range(1, size + 2 * w - 1)}
        for step in range(1, w + 1):
            new = {}
            for i in range(step, size + 2 * w - step):
                u = disp[i]
                right = jnp.where(lane == width - 1, 0.0, pltpu.roll(u, width - 1, 1))
                left = jnp.where(lane == 0, 0.0, pltpu.roll(u, 1, 1))
                around = (disp[i + 1] + disp[i - 1]) + (right + left)
                stiff = jnp.broadcast_to(stiff_pad[8 - w + i:8 - w + i + 1, :], (8, width))
                vel[i] = vel[i] + stiff * (around + u * (0.5 * pl.reciprocal(1.0 + u * u) - 4.5))
                new[i] = u + vel[i]
            disp = new
        for i in range(size):
            out[i, at, :] = disp[w + i]
        return carry

    lax.fori_loop(0, members // 8, group_step, 0)


def evolve(index, disp, vel, stiff, before, after, slot, size):
    lines, members, width = disp.shape
    w = STEPS
    return pl.pallas_call(
        functools.partial(evolve_kernel, slot=slot),
        in_specs=[SCALARS] + [pl.BlockSpec(memory_space=pltpu.VMEM)] * 5,
        out_shape=pltpu.HBM((size, members, width), jnp.float32),
        out_specs=pl.BlockSpec((size, members, width), lambda: (0, 0, 0)),
        scratch_shapes=[pltpu.VMEM((size + 2 * w, members, width), jnp.float32)] * 2
        + [pltpu.VMEM((size + 16, width), jnp.float32)],
        compiler_params=params(16),
        name="evolve%d" % slot,
    )(index, disp, vel, stiff, before, after)


def basis_gram_kernel(index_ref, basis_ref, send_ref, keep_ref, sum_ref, mixed_ref):
    lines, width, rank = basis_ref.shape
    step = pl.program_id(0)

    @pl.when(step == 0)
    def _():
        sum_ref[...] = jnp.zeros_like(sum_ref)
        mixed_ref[...] = jnp.zeros_like(mixed_ref)

    high, low = halves(basis_ref[...].reshape(lines * width, rank))
    sum_ref[...] += mm(high, high, ((0,), (0,)), None)
    mixed_ref[...] += mm(high, low, ((0,), (0,)), None)

    @pl.when(step == pl.num_programs(0) - 1)
    def _():
        sum_ref[...] += mixed_ref[...] + mixed_ref[...].T
        half = keep_ref.shape[0]
        core = index_ref[1]
        keep_ref[...] = sum_ref[pl.ds(pl.multiple_of(core * half, half), half), :]
        send_ref[...] = sum_ref[pl.ds(pl.multiple_of((1 - core) * half, half), half), :]


def basis_gram(index, basis):
    lines, width, rank = basis.shape
    block = 4
    half = pl.BlockSpec((rank // 2, rank), lambda i: (0, 0))
    return pl.pallas_call(
        basis_gram_kernel,
        grid=(lines // block,),
        in_specs=[SCALARS, pl.BlockSpec((block, width, rank), lambda i: (i, 0, 0))],
        out_specs=[half, half],
        out_shape=[shape(rank // 2, rank)] * 2,
        scratch_shapes=[pltpu.VMEM((rank, rank), jnp.float32)] * 2,
        compiler_params=params(24),
        name="basis_gram",
    )(index, in_hbm(basis))


def products_kernel(index_ref, basis_ref, *rest):
    pieces, (send_ref, keep_ref, snap_ref, sum_ref) = rest[:-4], rest[-4:]
    lines, members, width = pieces[0].shape
    rank = basis_ref.shape[-1]
    step = pl.program_id(0)
    for k, piece in enumerate(pieces):
        at = pl.multiple_of((index_ref[0] ^ index_ref[FIRST + k]) * members, members)
        for line in range(lines):
            snap_ref[pl.ds(at, members), line * width:(line + 1) * width] = piece[line]

    @pl.when(step == 0)
    def _():
        sum_ref[...] = jnp.zeros_like(sum_ref)

    snap = snap_ref[...]
    rows = basis_ref[...].reshape(lines * width, rank)
    sum_ref[:, :rank] += mm3(halves(snap), halves(rows), ((1,), (0,)))
    sum_ref[:, rank:] += mm(snap, snap, ((1,), (1,)))

    @pl.when(step == pl.num_programs(0) - 1)
    def _():
        half = keep_ref.shape[0]
        core = index_ref[1]
        keep_ref[...] = sum_ref[pl.ds(pl.multiple_of(core * half, half), half), :]
        send_ref[...] = sum_ref[pl.ds(pl.multiple_of((1 - core) * half, half), half), :]


def products(index, basis, pieces):
    lines, width, rank = basis.shape
    members = pieces[0].shape[1]
    total = members * len(pieces)
    block = 4
    half = pl.BlockSpec((total // 2, rank + total), lambda i: (0, 0))
    return pl.pallas_call(
        products_kernel,
        grid=(lines // block,),
        in_specs=[SCALARS, pl.BlockSpec((block, width, rank), lambda i: (i, 0, 0))]
        + [pl.BlockSpec((block, members, width), lambda i: (i, 0, 0))] * len(pieces),
        out_specs=[half, half],
        out_shape=[shape(total // 2, rank + total)] * 2,
        scratch_shapes=[pltpu.VMEM((total, block * width), jnp.float32), pltpu.VMEM((total, rank + total), jnp.float32)],
        compiler_params=params(32),
        name="products",
    )(index, in_hbm(basis), *pieces)


def split_kernel(index_ref, keep_ref, got_ref, *outs):
    rows = outs[0].shape[0]
    for k, out in enumerate(outs):
        at = pl.ds(pl.multiple_of((index_ref[2] ^ k) * rows, rows), rows)
        out[...] = keep_ref[at, :] + got_ref[at, :]


def split(index, keep, got, chips):
    rows, cols = keep.shape
    return pl.pallas_call(
        split_kernel,
        in_specs=[SCALARS] + [pl.BlockSpec(memory_space=pltpu.VMEM)] * 2,
        out_shape=[shape(rows // chips, cols)] * chips,
        compiler_params=params(16),
        name="split",
    )(index, keep, got)


def tree_sum(values):
    while len(values) > 1:
        values = [a + b for a, b in zip(values[::2], values[1::2])]
    return values[0]


def exchange_chips(pieces, limit):
    found = []
    for k in range(1, len(pieces)):
        piece = pieces[k]
        if k > limit:
            piece, found[k - limit - 1] = lax.optimization_barrier((piece, found[k - limit - 1]))
        found.append(xor_permute(piece, "sim", 2 * k))
    return found


def chip_scatter(index, send, keep, limit):
    chips = lax.axis_size("sim") // 2
    got = xor_permute(send, "sim", 1)
    pieces = split(index, keep, got, chips)
    return tree_sum([pieces[0]] + exchange_chips(pieces, limit))


def ana_sum(value):
    return tree_sum([value] + [xor_permute(value, "ana", k) for k in range(1, lax.axis_size("ana"))])


def ana_sum_halved(value):
    ranks = lax.axis_size("ana")
    top = lax.axis_index("ana") // (ranks // 2)
    half = value.shape[0] // 2
    send = lax.dynamic_slice_in_dim(value, (1 - top) * half, half, axis=0)
    total = lax.dynamic_slice_in_dim(value, top * half, half, axis=0) + xor_permute(send, "ana", ranks // 2)
    bit = 1
    while bit < ranks // 2:
        total = total + xor_permute(total, "ana", bit)
        bit *= 2
    return jnp.concatenate([total, xor_permute(total, "ana", ranks // 2)], axis=0)


def chip_gather(value, limit):
    chips = lax.axis_size("sim") // 2
    mine = jnp.concatenate([value] + exchange_chips([value] * chips, limit), axis=0)
    return mine, xor_permute(mine, "sim", 1)


PANEL = 32

def eliminate(work_ref, members):
    tiles = work_ref.shape[1] // 128
    groups = PANEL // 8
    sub = lax.broadcasted_iota(jnp.int32, (8, 128), 0)

    def panel_step(k, carry):
        start = pl.multiple_of(k * PANEL, PANEL)
        at = pl.multiple_of((k * PANEL) // 128 * 128, 128)
        diag = work_ref[pl.ds(start, PANEL), pl.ds(at, 128)]
        diag = pltpu.roll(diag, (128 - (k * PANEL) % 128) % 128, 1)
        rows = work_ref[pl.ds(start, PANEL), :]
        x = [[rows[8 * g:8 * g + 8, 128 * t:128 * t + 128] for t in range(tiles)] + [diag[8 * g:8 * g + 8]]
             for g in range(groups)]
        for b in range(groups):
            cols = {g: [jnp.broadcast_to(x[g][tiles][:, 8 * b + j:8 * b + j + 1], (8, 128)) for j in range(8)]
                    for g in range(b, groups)}
            pivots = jnp.ones((8, 128), jnp.float32)
            for r in range(8):
                pivot = jnp.broadcast_to(cols[b][r][r:r + 1], (8, 128))
                pivots = jnp.where(sub == r, pivot, pivots)
                inverse = 1.0 / pivot
                raw = [jnp.broadcast_to(v[r:r + 1], (8, 128)) for v in x[b]]
                craw = [jnp.broadcast_to(cols[b][j][r:r + 1], (8, 128)) if j > r else None for j in range(8)]
                for g in range(b, groups):
                    coef = cols[g][r] * inverse
                    if g == b:
                        coef = jnp.where(sub > r, coef, 0.0)
                    x[g] = [v - coef * w for v, w in zip(x[g], raw)]
                    cols[g] = [cols[g][j] - coef * craw[j] if j > r else cols[g][j] for j in range(8)]
            x[b] = [v * lax.rsqrt(pivots) for v in x[b]]
        done = jnp.concatenate([jnp.concatenate(v[:tiles], axis=1) for v in x], axis=0)
        lane = lax.broadcasted_iota(jnp.int32, (PANEL, members), 1)
        lower = jnp.where(lane >= start + PANEL, done[:, :members], 0.0)
        work_ref[...] = work_ref[...] - mm(lower, done, ((0,), (0,)))
        work_ref[pl.ds(start, PANEL), :] = done
        return carry

    lax.fori_loop(0, members // PANEL, panel_step, 0)


def ordered(index_ref, mine_ref, other_ref, out_ref, chips, parts):
    half = mine_ref.shape[0]
    rows = half // chips // parts
    for k in range(chips * parts):
        at = (index_ref[2] ^ (k // parts)) * (rows * parts)
        if parts > 1:
            at = at + (index_ref[3] ^ (k % parts)) * rows
        piece = slice(k * rows, (k + 1) * rows)
        out_ref[pl.ds(pl.multiple_of(index_ref[1] * half + at, rows), rows), :] = mine_ref[piece, :]
        out_ref[pl.ds(pl.multiple_of((1 - index_ref[1]) * half + at, rows), rows), :] = other_ref[piece, :]


def solve_kernel(index_ref, sums_ref, sums2_ref, gram_ref, gram2_ref, rot_ref, high_ref, low_ref, coords_ref,
                 work_ref, all_ref, basis_ref, *, count, chips):
    rank, members = coords_ref.shape
    ordered(index_ref, sums_ref, sums2_ref, all_ref, chips, 1)
    ordered(index_ref, gram_ref, gram2_ref, basis_ref, chips, 2)
    row = lax.broadcasted_iota(jnp.int32, (members, members), 0)
    col = lax.broadcasted_iota(jnp.int32, (members, members), 1)
    eye = row == col
    inner = all_ref[:, rank:]
    diag = jnp.where(eye, inner, 0.0)
    across = lax.rsqrt(jnp.sum(diag, axis=0, keepdims=True) / count + EPS)
    along = lax.rsqrt(jnp.sum(diag, axis=1, keepdims=True) / count + EPS)
    coef = all_ref[:, :rank] * (along / count)
    correct = 2.0 * coef - mm(coef, basis_ref[...], ((1,), (0,))) / count
    work_ref[:, :members] = inner * (along / count) * across - mm(correct, coef, ((1,), (1,)))
    work_ref[:, members:] = jnp.where(eye, 1.0, 0.0)
    eliminate(work_ref, members)
    top, bottom = rot_ref[:rank, :], rot_ref[rank:, :]
    upper = jnp.where(row <= col, work_ref[:, :members], 0.0)
    mix = mm(work_ref[:, members:], bottom, ((0,), (0,)))
    high_ref[:rank, :], low_ref[:rank, :] = halves(top - mm(coef, mix, ((0,), (0,))))
    high_ref[rank:, :], low_ref[rank:, :] = halves(mix * along)
    coords = (mm(coef, top, ((1,), (0,))) + mm(upper, bottom, ((0,), (0,)))) * math.sqrt(rank)
    coords_ref[...] = coords.T


def solve(index, sums, gram, rotation, count, chips):
    rank = gram[0].shape[1]
    members = rotation.shape[0] - rank
    return pl.pallas_call(
        functools.partial(solve_kernel, count=float(count), chips=chips),
        in_specs=[SCALARS] + [pl.BlockSpec(memory_space=pltpu.VMEM)] * 5,
        out_shape=[shape(members + rank, rank, dtype=jnp.bfloat16)] * 2 + [shape(rank, members)],
        scratch_shapes=[pltpu.VMEM((members, 2 * members), jnp.float32),
                        pltpu.VMEM((members, rank + members), jnp.float32),
                        pltpu.VMEM((rank, rank), jnp.float32)],
        compiler_params=params(40),
        name="solve",
    )(index, *sums, *gram, rotation)


def rotate_kernel(index_ref, high_ref, low_ref, basis_ref, *rest):
    pieces, (out_ref, snap_ref) = rest[:-2], rest[-2:]
    lines, members, width = pieces[0].shape
    rank = basis_ref.shape[-1]
    for k, piece in enumerate(pieces):
        at = pl.multiple_of((index_ref[0] ^ index_ref[FIRST + k]) * members, members)
        for line in range(lines):
            snap_ref[pl.ds(at, members), line * width:(line + 1) * width] = piece[line]
    rows = basis_ref[...].reshape(lines * width, rank)
    out = mm3(halves(rows), (high_ref[:rank, :], low_ref[:rank, :]), ((1,), (0,)))
    out = out + mm3(halves(snap_ref[...].T), (high_ref[rank:, :], low_ref[rank:, :]), ((1,), (0,)))
    out_ref[...] = out.reshape(out_ref.shape)


def rotate(index, high, low, basis, pieces):
    lines, width, rank = basis.shape
    members = pieces[0].shape[1]
    block = 4
    rows = pl.BlockSpec((block, width, rank), lambda i: (i, 0, 0))
    return pl.pallas_call(
        rotate_kernel,
        grid=(lines // block,),
        in_specs=[SCALARS] + [pl.BlockSpec(high.shape, lambda i: (0, 0))] * 2 + [rows]
        + [pl.BlockSpec((block, members, width), lambda i: (i, 0, 0))] * len(pieces),
        out_specs=rows,
        out_shape=shape(lines, width, rank),
        scratch_shapes=[pltpu.VMEM((members * len(pieces), block * width), jnp.float32)],
        compiler_params=params(32),
        name="rotate",
    )(index, high, low, in_hbm(basis), *pieces)


def per_device(initial_disp, initial_vel, stiffness, basis, rotation):
    ranks, sims = lax.axis_size("ana"), lax.axis_size("sim")
    ana, sim = lax.axis_index("ana"), lax.axis_index("sim")
    lines, width, rank = basis.shape
    count = lines * width * sims * ranks
    chips = sims // 2
    core = sim % 2
    near, far = list(range(1, ranks // 2)), list(range(ranks // 2, ranks))
    orders = (near + far[::-1] + [0], far[::-1] + near + [0])
    masks = jnp.where(core == 0, jnp.array(orders[0]), jnp.array(orders[1]))
    first_index = jnp.stack([ana, core, sim // 2, ana // (ranks // 2)])
    index = jnp.concatenate([first_index, masks]).astype(jnp.int32)

    disp, vel, last, first = to_lines(initial_disp, initial_vel, stiffness)
    up = [(i, i + 1) for i in range(sims - 1)]
    before = lax.ppermute(last, "sim", up)
    after = lax.ppermute(first, "sim", [(j, i) for i, j in up])

    basis_late, _ = lax.optimization_barrier((basis, last[0, 0, 0]))
    send, keep = basis_gram(index, basis_late)
    before, after, send = lax.optimization_barrier((before, after, send))

    pieces = []
    order = index
    for slot in range(ranks):
        piece = evolve(order, disp, vel, stiffness, before, after, slot, lines)
        order, piece = lax.optimization_barrier((order, piece))
        if slot < ranks - 1:
            pairs = [(s * ranks + a, s * ranks + (a ^ orders[s % 2][slot])) for s in range(sims) for a in range(ranks)]
            piece = lax.ppermute(piece, ("sim", "ana"), pairs)
        pieces.append(piece)
    pieces[-1], send = lax.optimization_barrier((pieces[-1], send))
    once = 1 + (ana >> 20)
    gram = lax.fori_loop(
        0, once, lambda _, pair: chip_gather(ana_sum_halved(chip_scatter(index, *pair, 2)), 2), (send, keep))
    pieces, gram = lax.optimization_barrier((pieces, gram))

    send, keep = products(index, basis, pieces)
    sums = chip_gather(ana_sum(chip_scatter(index, send, keep, chips)), chips)
    high, low, coords = solve(index, sums, gram, rotation, count, chips)
    return rotate(index, high, low, basis, pieces), coords


def solution(mesh):
    in_specs = (
        P("ana", "sim", None),
        P("ana", "sim", None),
        P("sim", None),
        P(("sim", "ana"), None, None),
        P(),
    )
    out_specs = (P(("sim", "ana"), None, None), P())
    return jax.shard_map(
        per_device, mesh=mesh, in_specs=in_specs, out_specs=out_specs, check_vma=False
    )
```

```python
import functools
import math

import jax
import jax.numpy as jnp
from jax import lax
from jax.experimental import pallas as pl
from jax.experimental.pallas import tpu as pltpu
from jax.sharding import PartitionSpec as P

STEPS = 4
EPS = 1e-06
MIB = 1024 * 1024
HI = lax.Precision.HIGHEST
FIRST = 3
SCALARS = pl.BlockSpec(memory_space=pltpu.SMEM)


def mm(left, right, dims, precision=HI):
    return lax.dot_general(left, right, (dims, ((), ())), precision=precision, preferred_element_type=jnp.float32)


def shape(*dims, dtype=jnp.float32):
    return jax.ShapeDtypeStruct(dims, dtype)


def params(mib):
    return pltpu.CompilerParams(vmem_limit_bytes=mib * MIB)


def in_hbm(value):
    return pltpu.with_memory_space_constraint(value, pltpu.HBM)


def halves(value):
    high = value.astype(jnp.bfloat16)
    return high, (value - high.astype(jnp.float32)).astype(jnp.bfloat16)


def mm3(left, right, dims):
    (lh, ll), (rh, rl) = left, right
    return mm(lh, rh, dims, None) + (mm(lh, rl, dims, None) + mm(ll, rh, dims, None))


def xor_permute(value, axis, mask):
    size = lax.axis_size(axis)
    return lax.ppermute(value, axis, [(i, i ^ mask) for i in range(size)])


def edges_kernel(stiff_ref, disp_low, vel_low, disp_high, vel_high, last_ref, first_ref):
    w = STEPS
    lines = stiff_ref.shape[0]
    for ref, disp, vel, at, start in ((last_ref, disp_high, vel_high, 8 - w, lines - w), (first_ref, disp_low, vel_low, 0, 0)):
        for i in range(w):
            ref[i] = disp[:, at + i, :]
            ref[w + i] = vel[:, at + i, :]
        ref[2 * w] = jnp.zeros_like(ref[2 * w])
        ref[2 * w, :w, :] = stiff_ref[start:start + w, :]


def edges(disp, vel, stiff):
    members, lines, width = disp.shape
    w = STEPS
    low = pl.BlockSpec((members, 8, width), lambda i: (0, 0, 0))
    high = pl.BlockSpec((members, 8, width), lambda i: (0, lines // 8 - 1, 0))
    edge = pl.BlockSpec((2 * w + 1, members, width), lambda i: (0, 0, 0))
    return pl.pallas_call(
        edges_kernel,
        grid=(1,),
        in_specs=[pl.BlockSpec((lines, width), lambda i: (0, 0)), low, low, high, high],
        out_specs=[edge, edge],
        out_shape=[pltpu.HBM((2 * w + 1, members, width), jnp.float32)] * 2,
        compiler_params=params(6),
        name="edges",
    )(in_hbm(stiff), in_hbm(disp), in_hbm(vel), in_hbm(disp), in_hbm(vel))


def to_lines_kernel(disp_ref, vel_ref, disp_out, vel_out):
    lines, group, _ = disp_out.shape
    for line in range(lines):
        disp_out[line] = disp_ref[pl.ds(line, group, stride=lines), :]
        vel_out[line] = vel_ref[pl.ds(line, group, stride=lines), :]


def to_lines(disp, vel):
    members, lines, width = disp.shape
    group = 16
    flat = pl.BlockSpec((group * lines, width), lambda i: (i, 0))
    out = pl.BlockSpec((lines, group, width), lambda i: (0, i, 0))
    return pl.pallas_call(
        to_lines_kernel,
        grid=(members // group,),
        in_specs=[flat, flat],
        out_specs=[out, out],
        out_shape=[shape(lines, members, width)] * 2,
        compiler_params=params(8),
        name="to_lines",
    )(in_hbm(disp.reshape(members * lines, width)), in_hbm(vel.reshape(members * lines, width)))


def evolve_kernel(index_ref, disp_ref, vel_ref, stiff_ref, before_ref, after_ref, *rest, slots):
    outs, (disp_pad, vel_pad, stiff_pad) = rest[:-3], rest[-3:]
    size = outs[0].shape[0]
    lines, members, width = disp_ref.shape
    w = STEPS
    blocks = lines // size
    lane = lax.broadcasted_iota(jnp.int32, (8, width), 1)
    for slot, out in zip(slots, outs):
        block = index_ref[0] ^ index_ref[FIRST + slot]
        start = block * size
        disp_pad[w:w + size] = disp_ref[pl.ds(start, size)]
        vel_pad[w:w + size] = vel_ref[pl.ds(start, size)]
        stiff_pad[8:8 + size, :] = stiff_ref[pl.ds(pl.multiple_of(start, 8), size), :]

        @pl.when(block == 0)
        def _():
            disp_pad[:w] = before_ref[:w]
            vel_pad[:w] = before_ref[w:2 * w]
            stiff_pad[8 - w:8, :] = before_ref[2 * w, :w, :]

        @pl.when(block > 0)
        def _():
            low = jnp.maximum(start - w, 0)
            disp_pad[:w] = disp_ref[pl.ds(low, w)]
            vel_pad[:w] = vel_ref[pl.ds(low, w)]
            stiff_pad[:8, :] = stiff_ref[pl.ds(pl.multiple_of(jnp.maximum(start - 8, 0), 8), 8), :]

        @pl.when(block == blocks - 1)
        def _():
            disp_pad[w + size:] = after_ref[:w]
            vel_pad[w + size:] = after_ref[w:2 * w]
            stiff_pad[8 + size:8 + size + w, :] = after_ref[2 * w, :w, :]

        @pl.when(block < blocks - 1)
        def _():
            high = jnp.minimum(start + size, lines - 8)
            disp_pad[w + size:] = disp_ref[pl.ds(high, w)]
            vel_pad[w + size:] = vel_ref[pl.ds(high, w)]
            stiff_pad[8 + size:, :] = stiff_ref[pl.ds(pl.multiple_of(high, 8), 8), :]

        def group_step(g, carry):
            at = pl.ds(pl.multiple_of(g * 8, 8), 8)
            disp = {i: disp_pad[i, at, :] for i in range(size + 2 * w)}
            vel = {i: vel_pad[i, at, :] for i in range(1, size + 2 * w - 1)}
            for step in range(1, w + 1):
                new = {}
                for i in range(step, size + 2 * w - step):
                    u = disp[i]
                    right = jnp.where(lane == width - 1, 0.0, pltpu.roll(u, width - 1, 1))
                    left = jnp.where(lane == 0, 0.0, pltpu.roll(u, 1, 1))
                    around = (disp[i + 1] + disp[i - 1]) + (right + left)
                    stiff = jnp.broadcast_to(stiff_pad[8 - w + i:8 - w + i + 1, :], (8, width))
                    vel[i] = vel[i] + stiff * (around + u * (0.5 * pl.reciprocal(1.0 + u * u) - 4.5))
                    new[i] = u + vel[i]
                disp = new
            for i in range(size):
                out[i, at, :] = disp[w + i]
            return carry

        lax.fori_loop(0, members // 8, group_step, 0)


def evolve(index, disp, vel, stiff, before, after, slots, size):
    lines, members, width = disp.shape
    w = STEPS
    return pl.pallas_call(
        functools.partial(evolve_kernel, slots=slots),
        in_specs=[SCALARS] + [pl.BlockSpec(memory_space=pltpu.VMEM)] * 5,
        out_shape=[pltpu.HBM((size, members, width), jnp.float32)] * len(slots),
        out_specs=[pl.BlockSpec((size, members, width), lambda: (0, 0, 0))] * len(slots),
        scratch_shapes=[pltpu.VMEM((size + 2 * w, members, width), jnp.float32)] * 2
        + [pltpu.VMEM((size + 16, width), jnp.float32)],
        compiler_params=params(10),
        name="evolve%d" % slots[0],
    )(index, disp, vel, stiff, before, after)


def basis_gram_kernel(index_ref, basis_ref, send_ref, keep_ref, sum_ref, mixed_ref):
    lines, width, rank = basis_ref.shape
    step = pl.program_id(0)

    @pl.when(step == 0)
    def _():
        sum_ref[...] = jnp.zeros_like(sum_ref)
        mixed_ref[...] = jnp.zeros_like(mixed_ref)

    high, low = halves(basis_ref[...].reshape(lines * width, rank))
    sum_ref[...] += mm(high, high, ((0,), (0,)), None)
    mixed_ref[...] += mm(high, low, ((0,), (0,)), None)

    @pl.when(step == pl.num_programs(0) - 1)
    def _():
        sum_ref[...] += mixed_ref[...] + mixed_ref[...].T
        half = keep_ref.shape[0]
        core = index_ref[1]
        keep_ref[...] = sum_ref[pl.ds(pl.multiple_of(core * half, half), half), :]
        send_ref[...] = sum_ref[pl.ds(pl.multiple_of((1 - core) * half, half), half), :]


def basis_gram(index, basis):
    lines, width, rank = basis.shape
    block = 4
    half = pl.BlockSpec((rank // 2, rank), lambda i: (0, 0))
    return pl.pallas_call(
        basis_gram_kernel,
        grid=(lines // block,),
        in_specs=[SCALARS, pl.BlockSpec((block, width, rank), lambda i: (i, 0, 0))],
        out_specs=[half, half],
        out_shape=[shape(rank // 2, rank)] * 2,
        scratch_shapes=[pltpu.VMEM((rank, rank), jnp.float32)] * 2,
        compiler_params=params(14),
        name="basis_gram",
    )(index, in_hbm(basis))


def products_kernel(index_ref, basis_ref, *rest):
    pieces, (send_ref, keep_ref, snap_ref, sum_ref) = rest[:-4], rest[-4:]
    lines, members, width = pieces[0].shape
    rank = basis_ref.shape[-1]
    step = pl.program_id(0)
    for k, piece in enumerate(pieces):
        at = pl.multiple_of((index_ref[0] ^ index_ref[FIRST + k]) * members, members)
        for line in range(lines):
            snap_ref[pl.ds(at, members), line * width:(line + 1) * width] = piece[line]

    @pl.when(step == 0)
    def _():
        sum_ref[...] = jnp.zeros_like(sum_ref)

    snap = snap_ref[...]
    rows = basis_ref[...].reshape(lines * width, rank)
    sum_ref[:, :rank] += mm3(halves(snap), halves(rows), ((1,), (0,)))
    sum_ref[:, rank:] += mm(snap, snap, ((1,), (1,)))

    @pl.when(step == pl.num_programs(0) - 1)
    def _():
        half = keep_ref.shape[0]
        core = index_ref[1]
        keep_ref[...] = sum_ref[pl.ds(pl.multiple_of(core * half, half), half), :]
        send_ref[...] = sum_ref[pl.ds(pl.multiple_of((1 - core) * half, half), half), :]


def products(index, basis, pieces):
    lines, width, rank = basis.shape
    members = pieces[0].shape[1]
    total = members * len(pieces)
    block = 4
    half = pl.BlockSpec((total // 2, rank + total), lambda i: (0, 0))
    return pl.pallas_call(
        products_kernel,
        grid=(lines // block,),
        in_specs=[SCALARS, pl.BlockSpec((block, width, rank), lambda i: (i, 0, 0))]
        + [pl.BlockSpec((block, members, width), lambda i: (i, 0, 0))] * len(pieces),
        out_specs=[half, half],
        out_shape=[shape(total // 2, rank + total)] * 2,
        scratch_shapes=[pltpu.VMEM((total, block * width), jnp.float32), pltpu.VMEM((total, rank + total), jnp.float32)],
        compiler_params=params(14),
        name="products",
    )(index, in_hbm(basis), *pieces)


def split_kernel(index_ref, keep_ref, got_ref, *outs):
    rows = outs[0].shape[0]
    for k, out in enumerate(outs):
        at = pl.ds(pl.multiple_of((index_ref[2] ^ k) * rows, rows), rows)
        out[...] = keep_ref[at, :] + got_ref[at, :]


def split(index, keep, got, chips):
    rows, cols = keep.shape
    return pl.pallas_call(
        split_kernel,
        in_specs=[SCALARS] + [pl.BlockSpec(memory_space=pltpu.VMEM)] * 2,
        out_shape=[shape(rows // chips, cols)] * chips,
        compiler_params=params(4),
        name="split",
    )(index, keep, got)


def tree_sum(values):
    while len(values) > 1:
        values = [a + b for a, b in zip(values[::2], values[1::2])]
    return values[0]


def exchange_chips(pieces, limit):
    found = []
    for k in range(1, len(pieces)):
        piece = pieces[k]
        if k > limit:
            piece, found[k - limit - 1] = lax.optimization_barrier((piece, found[k - limit - 1]))
        found.append(xor_permute(piece, "sim", 2 * k))
    return found


def chip_scatter(index, send, keep, limit):
    chips = lax.axis_size("sim") // 2
    got = xor_permute(send, "sim", 1)
    pieces = split(index, keep, got, chips)
    return tree_sum([pieces[0]] + exchange_chips(pieces, limit))


def ana_sum(value):
    return tree_sum([value] + [xor_permute(value, "ana", k) for k in range(1, lax.axis_size("ana"))])


def chip_gather(value, limit):
    chips = lax.axis_size("sim") // 2
    return jnp.concatenate([value] + exchange_chips([value] * chips, limit), axis=0)


def with_other_core(value):
    return value, xor_permute(value, "sim", 1)


PANEL = 32

def eliminate(work_ref, members):
    tiles = work_ref.shape[1] // 128
    groups = PANEL // 8
    sub = lax.broadcasted_iota(jnp.int32, (8, 128), 0)

    def panel_step(k, carry):
        start = pl.multiple_of(k * PANEL, PANEL)
        at = pl.multiple_of((k * PANEL) // 128 * 128, 128)
        diag = work_ref[pl.ds(start, PANEL), pl.ds(at, 128)]
        diag = pltpu.roll(diag, (128 - (k * PANEL) % 128) % 128, 1)
        rows = work_ref[pl.ds(start, PANEL), :]
        x = [[rows[8 * g:8 * g + 8, 128 * t:128 * t + 128] for t in range(tiles)] + [diag[8 * g:8 * g + 8]]
             for g in range(groups)]
        for b in range(groups):
            cols = {g: [jnp.broadcast_to(x[g][tiles][:, 8 * b + j:8 * b + j + 1], (8, 128)) for j in range(8)]
                    for g in range(b, groups)}
            pivots = jnp.ones((8, 128), jnp.float32)
            for r in range(8):
                pivot = jnp.broadcast_to(cols[b][r][r:r + 1], (8, 128))
                pivots = jnp.where(sub == r, pivot, pivots)
                inverse = 1.0 / pivot
                raw = [jnp.broadcast_to(v[r:r + 1], (8, 128)) for v in x[b]]
                craw = [jnp.broadcast_to(cols[b][j][r:r + 1], (8, 128)) if j > r else None for j in range(8)]
                for g in range(b, groups):
                    coef = cols[g][r] * inverse
                    if g == b:
                        coef = jnp.where(sub > r, coef, 0.0)
                    x[g] = [v - coef * w for v, w in zip(x[g], raw)]
                    cols[g] = [cols[g][j] - coef * craw[j] if j > r else cols[g][j] for j in range(8)]
            x[b] = [v * lax.rsqrt(pivots) for v in x[b]]
        done = jnp.concatenate([jnp.concatenate(v[:tiles], axis=1) for v in x], axis=0)
        lane = lax.broadcasted_iota(jnp.int32, (PANEL, members), 1)
        lower = jnp.where(lane >= start + PANEL, done[:, :members], 0.0)
        work_ref[...] = work_ref[...] - mm(lower, done, ((0,), (0,)))
        work_ref[pl.ds(start, PANEL), :] = done
        return carry

    lax.fori_loop(0, members // PANEL, panel_step, 0)


def ordered(index_ref, mine_ref, other_ref, out_ref, chips):
    half = mine_ref.shape[0]
    rows = half // chips
    for k in range(chips):
        at = (index_ref[2] ^ k) * rows
        piece = slice(k * rows, (k + 1) * rows)
        out_ref[pl.ds(pl.multiple_of(index_ref[1] * half + at, rows), rows), :] = mine_ref[piece, :]
        out_ref[pl.ds(pl.multiple_of((1 - index_ref[1]) * half + at, rows), rows), :] = other_ref[piece, :]


def solve_kernel(index_ref, sums_ref, sums2_ref, gram_ref, gram2_ref, rot_ref, high_ref, low_ref, coords_ref,
                 work_ref, all_ref, basis_ref, *, count, chips):
    rank, members = coords_ref.shape
    ordered(index_ref, sums_ref, sums2_ref, all_ref, chips)
    ordered(index_ref, gram_ref, gram2_ref, basis_ref, chips)
    row = lax.broadcasted_iota(jnp.int32, (members, members), 0)
    col = lax.broadcasted_iota(jnp.int32, (members, members), 1)
    eye = row == col
    inner = all_ref[:, rank:]
    diag = jnp.where(eye, inner, 0.0)
    across = lax.rsqrt(jnp.sum(diag, axis=0, keepdims=True) / count + EPS)
    along = lax.rsqrt(jnp.sum(diag, axis=1, keepdims=True) / count + EPS)
    coef = all_ref[:, :rank] * (along / count)
    correct = 2.0 * coef - mm(coef, basis_ref[...], ((1,), (0,))) / count
    work_ref[:, :members] = inner * (along / count) * across - mm(correct, coef, ((1,), (1,)))
    work_ref[:, members:] = jnp.where(eye, 1.0, 0.0)
    eliminate(work_ref, members)
    top, bottom = rot_ref[:rank, :], rot_ref[rank:, :]
    upper = jnp.where(row <= col, work_ref[:, :members], 0.0)
    mix = mm(work_ref[:, members:], bottom, ((0,), (0,)))
    high_ref[:rank, :], low_ref[:rank, :] = halves(top - mm(coef, mix, ((0,), (0,))))
    high_ref[rank:, :], low_ref[rank:, :] = halves(mix * along)
    coords = (mm(coef, top, ((1,), (0,))) + mm(upper, bottom, ((0,), (0,)))) * math.sqrt(rank)
    coords_ref[...] = coords.T


def solve(index, sums, gram, rotation, count, chips):
    rank = gram[0].shape[1]
    members = rotation.shape[0] - rank
    return pl.pallas_call(
        functools.partial(solve_kernel, count=float(count), chips=chips),
        in_specs=[SCALARS] + [pl.BlockSpec(memory_space=pltpu.VMEM)] * 5,
        out_shape=[shape(members + rank, rank, dtype=jnp.bfloat16)] * 2 + [shape(rank, members)],
        scratch_shapes=[pltpu.VMEM((members, 2 * members), jnp.float32),
                        pltpu.VMEM((members, rank + members), jnp.float32),
                        pltpu.VMEM((rank, rank), jnp.float32)],
        compiler_params=params(20),
        name="solve",
    )(index, *sums, *gram, rotation)


def rotate_kernel(index_ref, high_ref, low_ref, basis_ref, *rest):
    pieces, (out_ref, snap_ref) = rest[:-2], rest[-2:]
    lines, members, width = pieces[0].shape
    rank = basis_ref.shape[-1]
    for k, piece in enumerate(pieces):
        at = pl.multiple_of((index_ref[0] ^ index_ref[FIRST + k]) * members, members)
        for line in range(lines):
            snap_ref[pl.ds(at, members), line * width:(line + 1) * width] = piece[line]
    rows = basis_ref[...].reshape(lines * width, rank)
    out = mm3(halves(rows), (high_ref[:rank, :], low_ref[:rank, :]), ((1,), (0,)))
    out = out + mm3(halves(snap_ref[...].T), (high_ref[rank:, :], low_ref[rank:, :]), ((1,), (0,)))
    out_ref[...] = out.reshape(out_ref.shape)


def rotate(index, high, low, basis, pieces):
    lines, width, rank = basis.shape
    members = pieces[0].shape[1]
    block = 4
    rows = pl.BlockSpec((block, width, rank), lambda i: (i, 0, 0))
    return pl.pallas_call(
        rotate_kernel,
        grid=(lines // block,),
        in_specs=[SCALARS] + [pl.BlockSpec(high.shape, lambda i: (0, 0))] * 2 + [rows]
        + [pl.BlockSpec((block, members, width), lambda i: (i, 0, 0))] * len(pieces),
        out_specs=rows,
        out_shape=shape(lines, width, rank),
        scratch_shapes=[pltpu.VMEM((members * len(pieces), block * width), jnp.float32)],
        compiler_params=params(20),
        name="rotate",
    )(index, high, low, in_hbm(basis), *pieces)


def per_device(initial_disp, initial_vel, stiffness, basis, rotation):
    ranks, sims = lax.axis_size("ana"), lax.axis_size("sim")
    ana, sim = lax.axis_index("ana"), lax.axis_index("sim")
    lines, width, rank = basis.shape
    count = lines * width * sims * ranks
    chips = sims // 2
    core = sim % 2
    near, far = list(range(1, ranks // 2)), list(range(ranks // 2, ranks))
    orders = (near + far[::-1] + [0], far[::-1] + near + [0])
    masks = jnp.where(core == 0, jnp.array(orders[0]), jnp.array(orders[1]))
    first_index = jnp.stack([ana, core, sim // 2])
    index = jnp.concatenate([first_index, masks]).astype(jnp.int32)

    last, first = edges(initial_disp, initial_vel, stiffness)
    up = [(i, i + 1) for i in range(sims - 1)]
    before = lax.ppermute(last, "sim", up)
    after = lax.ppermute(first, "sim", [(j, i) for i, j in up])
    late_disp, late_vel, _ = lax.optimization_barrier((initial_disp, initial_vel, last[0, 0, 0]))
    disp, vel = to_lines(late_disp, late_vel)
    before, after, disp = lax.optimization_barrier((before, after, disp))

    pieces = list(evolve(index, disp, vel, stiffness, before, after, tuple(range(ranks - 1)), lines))
    order, pieces = lax.optimization_barrier((index, pieces))
    for slot in range(ranks - 1):
        pairs = [(s * ranks + a, s * ranks + (a ^ orders[s % 2][slot])) for s in range(sims) for a in range(ranks)]
        pieces[slot] = lax.ppermute(pieces[slot], ("sim", "ana"), pairs)

    once = 1 + (ana >> 20)

    def meanwhile(_, carry):
        at, _, _ = carry
        own, = evolve(at, disp, vel, stiffness, before, after, (ranks - 1,), lines)
        send, keep = basis_gram(at, basis)
        return at + (at >> 20), own, chip_scatter(at, send, keep, 2)

    order, own, gram = lax.fori_loop(0, once, meanwhile, (
        order, jnp.zeros((lines, disp.shape[1], width), jnp.float32), jnp.zeros((rank // sims, rank), jnp.float32)))
    pieces = pieces + [own]
    gram_parts = [xor_permute(gram, "ana", k) for k in range(1, ranks)]

    def first_stages(_, carry):
        at, _ = carry
        send, keep = products(at, basis, pieces)
        return at + (at >> 20), chip_scatter(at, send, keep, 2)

    total = initial_disp.shape[0] * ranks
    order, sums = lax.fori_loop(0, once, first_stages, (order, jnp.zeros((total // sims, rank + total), jnp.float32)))
    sums, gram, gram_parts = lax.optimization_barrier((sums, gram, gram_parts))
    gram = chip_gather(tree_sum([gram] + gram_parts), chips)
    sums = ana_sum(sums)
    sums = with_other_core(chip_gather(sums, chips))
    gram = with_other_core(gram)
    high, low, coords = solve(index, sums, gram, rotation, count, chips)
    return rotate(index, high, low, basis, pieces), coords


def solution(mesh):
    in_specs = (
        P("ana", "sim", None),
        P("ana", "sim", None),
        P("sim", None),
        P(("sim", "ana"), None, None),
        P(),
    )
    out_specs = (P(("sim", "ana"), None, None), P())
    return jax.shard_map(
        per_device, mesh=mesh, in_specs=in_specs, out_specs=out_specs, check_vma=False
    )
```

```python
import functools
import math

import jax
import jax.numpy as jnp
from jax import lax
from jax.experimental import pallas as pl
from jax.experimental.pallas import tpu as pltpu
from jax.sharding import PartitionSpec as P

STEPS = 4
EPS = 1e-06
MIB = 1024 * 1024
HI = lax.Precision.HIGHEST
FIRST = 3
SCALARS = pl.BlockSpec(memory_space=pltpu.SMEM)


def mm(left, right, dims, precision=HI):
    return lax.dot_general(left, right, (dims, ((), ())), precision=precision, preferred_element_type=jnp.float32)


def shape(*dims, dtype=jnp.float32):
    return jax.ShapeDtypeStruct(dims, dtype)


def params(mib):
    return pltpu.CompilerParams(vmem_limit_bytes=mib * MIB)


def in_hbm(value):
    return pltpu.with_memory_space_constraint(value, pltpu.HBM)


def halves(value):
    high = value.astype(jnp.bfloat16)
    return high, (value - high.astype(jnp.float32)).astype(jnp.bfloat16)


def mm3(left, right, dims):
    (lh, ll), (rh, rl) = left, right
    return mm(lh, rh, dims, None) + (mm(lh, rl, dims, None) + mm(ll, rh, dims, None))


def xor_permute(value, axis, mask):
    size = lax.axis_size(axis)
    return lax.ppermute(value, axis, [(i, i ^ mask) for i in range(size)])


def edges_kernel(stiff_ref, disp_low, vel_low, disp_high, vel_high, last_ref, first_ref):
    w = STEPS
    lines = stiff_ref.shape[0]
    for ref, disp, vel, at, start in ((last_ref, disp_high, vel_high, 8 - w, lines - w), (first_ref, disp_low, vel_low, 0, 0)):
        for i in range(w):
            ref[i] = disp[:, at + i, :]
            ref[w + i] = vel[:, at + i, :]
        ref[2 * w] = jnp.zeros_like(ref[2 * w])
        ref[2 * w, :w, :] = stiff_ref[start:start + w, :]


def edges(disp, vel, stiff):
    members, lines, width = disp.shape
    w = STEPS
    low = pl.BlockSpec((members, 8, width), lambda i: (0, 0, 0))
    high = pl.BlockSpec((members, 8, width), lambda i: (0, lines // 8 - 1, 0))
    edge = pl.BlockSpec((2 * w + 1, members, width), lambda i: (0, 0, 0))
    return pl.pallas_call(
        edges_kernel,
        grid=(1,),
        in_specs=[pl.BlockSpec((lines, width), lambda i: (0, 0)), low, low, high, high],
        out_specs=[edge, edge],
        out_shape=[pltpu.HBM((2 * w + 1, members, width), jnp.float32)] * 2,
        compiler_params=params(6),
        name="edges",
    )(in_hbm(stiff), in_hbm(disp), in_hbm(vel), in_hbm(disp), in_hbm(vel))


def to_lines_kernel(disp_ref, vel_ref, disp_out, vel_out):
    lines, group, _ = disp_out.shape
    for line in range(lines):
        disp_out[line] = disp_ref[pl.ds(line, group, stride=lines), :]
        vel_out[line] = vel_ref[pl.ds(line, group, stride=lines), :]


def to_lines(disp, vel):
    members, lines, width = disp.shape
    group = 16
    flat = pl.BlockSpec((group * lines, width), lambda i: (i, 0))
    out = pl.BlockSpec((lines, group, width), lambda i: (0, i, 0))
    return pl.pallas_call(
        to_lines_kernel,
        grid=(members // group,),
        in_specs=[flat, flat],
        out_specs=[out, out],
        out_shape=[shape(lines, members, width)] * 2,
        compiler_params=params(8),
        name="to_lines",
    )(in_hbm(disp.reshape(members * lines, width)), in_hbm(vel.reshape(members * lines, width)))


def evolve_kernel(index_ref, disp_ref, vel_ref, stiff_ref, before_ref, after_ref, *rest, slots):
    outs, (even_ref, odd_ref, speed_ref, pad_ref, all_ref, sem) = rest[:slots], rest[slots:]
    lines, members, width = disp_ref.shape
    w = STEPS
    full = lines + 2 * w
    size = lines // slots
    lane = lax.broadcasted_iota(jnp.int32, (8, width), 1)
    pad_ref[w:2 * w, :] = before_ref[2 * w, :w, :]
    pad_ref[8:8 + lines, :] = stiff_ref[...]
    pad_ref[8 + lines:8 + lines + w, :] = after_ref[2 * w, :w, :]

    def group_step(g, carry):
        at = pl.ds(pl.multiple_of(g * 8, 8), 8)
        for i in range(w):
            even_ref[i], speed_ref[i] = before_ref[i, at, :], before_ref[w + i, at, :]
            even_ref[w + lines + i], speed_ref[w + lines + i] = after_ref[i, at, :], after_ref[w + i, at, :]
        for i in range(lines):
            even_ref[w + i], speed_ref[w + i] = disp_ref[i, at, :], vel_ref[i, at, :]
        now, then = even_ref, odd_ref
        for step in range(1, w + 1):
            for i in range(step, full - step):
                u = now[i]
                right = jnp.where(lane == width - 1, 0.0, pltpu.roll(u, width - 1, 1))
                left = jnp.where(lane == 0, 0.0, pltpu.roll(u, 1, 1))
                around = (now[i + 1] + now[i - 1]) + (right + left)
                stiff = jnp.broadcast_to(pad_ref[8 - w + i:8 - w + i + 1, :], (8, width))
                speed = speed_ref[i] + stiff * (around + u * (0.5 / (1.0 + u * u) - 4.5))
                if step < w:
                    then[i], speed_ref[i] = u + speed, speed
                else:
                    all_ref[i - w, at, :] = u + speed
            now, then = then, now
        return carry

    lax.fori_loop(0, members // 8, group_step, 0)
    copies = []
    for slot, out in enumerate(outs):
        start = (index_ref[0] ^ index_ref[FIRST + slot]) * size
        copies.append(pltpu.make_async_copy(all_ref.at[pl.ds(start, size)], out, sem.at[slot]))
        copies[-1].start()
    for copy in copies:
        copy.wait()


def evolve(index, disp, vel, stiff, before, after, slots):
    lines, members, width = disp.shape
    line = pltpu.VMEM((lines + 2 * STEPS, 8, width), jnp.float32)
    return pl.pallas_call(
        functools.partial(evolve_kernel, slots=slots),
        in_specs=[SCALARS] + [pl.BlockSpec(memory_space=pltpu.VMEM)] * 5,
        out_shape=[pltpu.HBM((lines // slots, members, width), jnp.float32)] * slots,
        out_specs=[pl.BlockSpec(memory_space=pltpu.HBM)] * slots,
        scratch_shapes=[line, line, line, pltpu.VMEM((lines + 16, width), jnp.float32),
                        pltpu.VMEM((lines, members, width), jnp.float32), pltpu.SemaphoreType.DMA((slots,))],
        compiler_params=params(8),
        name="evolve",
    )(index, disp, vel, stiff, before, after)


def basis_gram_kernel(index_ref, basis_ref, send_ref, keep_ref, sum_ref, mixed_ref):
    lines, width, rank = basis_ref.shape
    step = pl.program_id(0)

    @pl.when(step == 0)
    def _():
        sum_ref[...] = jnp.zeros_like(sum_ref)
        mixed_ref[...] = jnp.zeros_like(mixed_ref)

    high, low = halves(basis_ref[...].reshape(lines * width, rank))
    sum_ref[...] += mm(high, high, ((0,), (0,)), None)
    mixed_ref[...] += mm(high, low, ((0,), (0,)), None)

    @pl.when(step == pl.num_programs(0) - 1)
    def _():
        sum_ref[...] += mixed_ref[...] + mixed_ref[...].T
        half = keep_ref.shape[0]
        core = index_ref[1]
        keep_ref[...] = sum_ref[pl.ds(pl.multiple_of(core * half, half), half), :]
        send_ref[...] = sum_ref[pl.ds(pl.multiple_of((1 - core) * half, half), half), :]


def basis_gram(index, basis):
    lines, width, rank = basis.shape
    block = 4
    half = pl.BlockSpec((rank // 2, rank), lambda i: (0, 0))
    return pl.pallas_call(
        basis_gram_kernel,
        grid=(lines // block,),
        in_specs=[SCALARS, pl.BlockSpec((block, width, rank), lambda i: (i, 0, 0))],
        out_specs=[half, half],
        out_shape=[shape(rank // 2, rank)] * 2,
        scratch_shapes=[pltpu.VMEM((rank, rank), jnp.float32)] * 2,
        compiler_params=params(14),
        name="basis_gram",
    )(index, in_hbm(basis))


def products_kernel(index_ref, basis_ref, *rest):
    pieces, (send_ref, keep_ref, snap_ref, sum_ref) = rest[:-4], rest[-4:]
    lines, members, width = pieces[0].shape
    rank = basis_ref.shape[-1]
    step = pl.program_id(0)
    for k, piece in enumerate(pieces):
        at = pl.multiple_of((index_ref[0] ^ index_ref[FIRST + k]) * members, members)
        for line in range(lines):
            snap_ref[pl.ds(at, members), line * width:(line + 1) * width] = piece[line]

    @pl.when(step == 0)
    def _():
        sum_ref[...] = jnp.zeros_like(sum_ref)

    snap = snap_ref[...]
    rows = basis_ref[...].reshape(lines * width, rank)
    sum_ref[:, :rank] += mm3(halves(snap), halves(rows), ((1,), (0,)))
    sum_ref[:, rank:] += mm(snap, snap, ((1,), (1,)))

    @pl.when(step == pl.num_programs(0) - 1)
    def _():
        half = keep_ref.shape[0]
        core = index_ref[1]
        keep_ref[...] = sum_ref[pl.ds(pl.multiple_of(core * half, half), half), :]
        send_ref[...] = sum_ref[pl.ds(pl.multiple_of((1 - core) * half, half), half), :]


def products(index, basis, pieces):
    lines, width, rank = basis.shape
    members = pieces[0].shape[1]
    total = members * len(pieces)
    block = 4
    half = pl.BlockSpec((total // 2, rank + total), lambda i: (0, 0))
    return pl.pallas_call(
        products_kernel,
        grid=(lines // block,),
        in_specs=[SCALARS, pl.BlockSpec((block, width, rank), lambda i: (i, 0, 0))]
        + [pl.BlockSpec((block, members, width), lambda i: (i, 0, 0))] * len(pieces),
        out_specs=[half, half],
        out_shape=[shape(total // 2, rank + total)] * 2,
        scratch_shapes=[pltpu.VMEM((total, block * width), jnp.float32), pltpu.VMEM((total, rank + total), jnp.float32)],
        compiler_params=params(14),
        name="products",
    )(index, in_hbm(basis), *pieces)


def split_kernel(index_ref, keep_ref, got_ref, *outs):
    rows = outs[0].shape[0]
    for k, out in enumerate(outs):
        at = pl.ds(pl.multiple_of((index_ref[2] ^ k) * rows, rows), rows)
        out[...] = keep_ref[at, :] + got_ref[at, :]


def split(index, keep, got, chips):
    rows, cols = keep.shape
    return pl.pallas_call(
        split_kernel,
        in_specs=[SCALARS] + [pl.BlockSpec(memory_space=pltpu.VMEM)] * 2,
        out_shape=[shape(rows // chips, cols)] * chips,
        compiler_params=params(4),
        name="split",
    )(index, keep, got)


def tree_sum(values):
    while len(values) > 1:
        values = [a + b for a, b in zip(values[::2], values[1::2])]
    return values[0]


def exchange_chips(pieces, limit):
    found = []
    for k in range(1, len(pieces)):
        piece = pieces[k]
        if k > limit:
            piece, found[k - limit - 1] = lax.optimization_barrier((piece, found[k - limit - 1]))
        found.append(xor_permute(piece, "sim", 2 * k))
    return found


def chip_scatter(index, send, keep, limit):
    chips = lax.axis_size("sim") // 2
    got = xor_permute(send, "sim", 1)
    pieces = split(index, keep, got, chips)
    return tree_sum([pieces[0]] + exchange_chips(pieces, limit))


def ana_sum(value):
    return tree_sum([value] + [xor_permute(value, "ana", k) for k in range(1, lax.axis_size("ana"))])


def chip_gather(value, limit):
    chips = lax.axis_size("sim") // 2
    return jnp.concatenate([value] + exchange_chips([value] * chips, limit), axis=0)


def with_other_core(value):
    return value, xor_permute(value, "sim", 1)


PANEL = 32

def eliminate(work_ref, members):
    tiles = work_ref.shape[1] // 128
    groups = PANEL // 8
    sub = lax.broadcasted_iota(jnp.int32, (8, 128), 0)

    def panel_step(k, carry):
        start = pl.multiple_of(k * PANEL, PANEL)
        at = pl.multiple_of((k * PANEL) // 128 * 128, 128)
        diag = work_ref[pl.ds(start, PANEL), pl.ds(at, 128)]
        diag = pltpu.roll(diag, (128 - (k * PANEL) % 128) % 128, 1)
        rows = work_ref[pl.ds(start, PANEL), :]
        x = [[rows[8 * g:8 * g + 8, 128 * t:128 * t + 128] for t in range(tiles)] + [diag[8 * g:8 * g + 8]]
             for g in range(groups)]
        for b in range(groups):
            cols = {g: [jnp.broadcast_to(x[g][tiles][:, 8 * b + j:8 * b + j + 1], (8, 128)) for j in range(8)]
                    for g in range(b, groups)}
            pivots = jnp.ones((8, 128), jnp.float32)
            for r in range(8):
                pivot = jnp.broadcast_to(cols[b][r][r:r + 1], (8, 128))
                pivots = jnp.where(sub == r, pivot, pivots)
                inverse = 1.0 / pivot
                raw = [jnp.broadcast_to(v[r:r + 1], (8, 128)) for v in x[b]]
                craw = [jnp.broadcast_to(cols[b][j][r:r + 1], (8, 128)) if j > r else None for j in range(8)]
                for g in range(b, groups):
                    coef = cols[g][r] * inverse
                    if g == b:
                        coef = jnp.where(sub > r, coef, 0.0)
                    x[g] = [v - coef * w for v, w in zip(x[g], raw)]
                    cols[g] = [cols[g][j] - coef * craw[j] if j > r else cols[g][j] for j in range(8)]
            x[b] = [v * lax.rsqrt(pivots) for v in x[b]]
        done = jnp.concatenate([jnp.concatenate(v[:tiles], axis=1) for v in x], axis=0)
        lane = lax.broadcasted_iota(jnp.int32, (PANEL, members), 1)
        lower = jnp.where(lane >= start + PANEL, done[:, :members], 0.0)
        work_ref[...] = work_ref[...] - mm(lower, done, ((0,), (0,)))
        work_ref[pl.ds(start, PANEL), :] = done
        return carry

    lax.fori_loop(0, members // PANEL, panel_step, 0)


def ordered(index_ref, mine_ref, other_ref, out_ref, chips):
    half = mine_ref.shape[0]
    rows = half // chips
    for k in range(chips):
        at = (index_ref[2] ^ k) * rows
        piece = slice(k * rows, (k + 1) * rows)
        out_ref[pl.ds(pl.multiple_of(index_ref[1] * half + at, rows), rows), :] = mine_ref[piece, :]
        out_ref[pl.ds(pl.multiple_of((1 - index_ref[1]) * half + at, rows), rows), :] = other_ref[piece, :]


def solve_kernel(index_ref, sums_ref, sums2_ref, gram_ref, gram2_ref, rot_ref, high_ref, low_ref, coords_ref,
                 work_ref, all_ref, basis_ref, *, count, chips):
    rank, members = coords_ref.shape
    ordered(index_ref, sums_ref, sums2_ref, all_ref, chips)
    ordered(index_ref, gram_ref, gram2_ref, basis_ref, chips)
    row = lax.broadcasted_iota(jnp.int32, (members, members), 0)
    col = lax.broadcasted_iota(jnp.int32, (members, members), 1)
    eye = row == col
    inner = all_ref[:, rank:]
    diag = jnp.where(eye, inner, 0.0)
    across = lax.rsqrt(jnp.sum(diag, axis=0, keepdims=True) / count + EPS)
    along = lax.rsqrt(jnp.sum(diag, axis=1, keepdims=True) / count + EPS)
    coef = all_ref[:, :rank] * (along / count)
    correct = 2.0 * coef - mm(coef, basis_ref[...], ((1,), (0,))) / count
    work_ref[:, :members] = inner * (along / count) * across - mm(correct, coef, ((1,), (1,)))
    work_ref[:, members:] = jnp.where(eye, 1.0, 0.0)
    eliminate(work_ref, members)
    top, bottom = rot_ref[:rank, :], rot_ref[rank:, :]
    upper = jnp.where(row <= col, work_ref[:, :members], 0.0)
    mix = mm(work_ref[:, members:], bottom, ((0,), (0,)))
    high_ref[:rank, :], low_ref[:rank, :] = halves(top - mm(coef, mix, ((0,), (0,))))
    high_ref[rank:, :], low_ref[rank:, :] = halves(mix * along)
    coords = (mm(coef, top, ((1,), (0,))) + mm(upper, bottom, ((0,), (0,)))) * math.sqrt(rank)
    coords_ref[...] = coords.T


def solve(index, sums, gram, rotation, count, chips):
    rank = gram[0].shape[1]
    members = rotation.shape[0] - rank
    return pl.pallas_call(
        functools.partial(solve_kernel, count=float(count), chips=chips),
        in_specs=[SCALARS] + [pl.BlockSpec(memory_space=pltpu.VMEM)] * 5,
        out_shape=[shape(members + rank, rank, dtype=jnp.bfloat16)] * 2 + [shape(rank, members)],
        scratch_shapes=[pltpu.VMEM((members, 2 * members), jnp.float32),
                        pltpu.VMEM((members, rank + members), jnp.float32),
                        pltpu.VMEM((rank, rank), jnp.float32)],
        compiler_params=params(20),
        name="solve",
    )(index, *sums, *gram, rotation)


def rotate_kernel(index_ref, high_ref, low_ref, basis_ref, *rest):
    pieces, (out_ref, snap_ref) = rest[:-2], rest[-2:]
    lines, members, width = pieces[0].shape
    rank = basis_ref.shape[-1]
    for k, piece in enumerate(pieces):
        at = pl.multiple_of((index_ref[0] ^ index_ref[FIRST + k]) * members, members)
        for line in range(lines):
            snap_ref[pl.ds(at, members), line * width:(line + 1) * width] = piece[line]
    rows = basis_ref[...].reshape(lines * width, rank)
    out = mm3(halves(rows), (high_ref[:rank, :], low_ref[:rank, :]), ((1,), (0,)))
    out = out + mm3(halves(snap_ref[...].T), (high_ref[rank:, :], low_ref[rank:, :]), ((1,), (0,)))
    out_ref[...] = out.reshape(out_ref.shape)


def rotate(index, high, low, basis, pieces):
    lines, width, rank = basis.shape
    members = pieces[0].shape[1]
    block = 4
    rows = pl.BlockSpec((block, width, rank), lambda i: (i, 0, 0))
    return pl.pallas_call(
        rotate_kernel,
        grid=(lines // block,),
        in_specs=[SCALARS] + [pl.BlockSpec(high.shape, lambda i: (0, 0))] * 2 + [rows]
        + [pl.BlockSpec((block, members, width), lambda i: (i, 0, 0))] * len(pieces),
        out_specs=rows,
        out_shape=shape(lines, width, rank),
        scratch_shapes=[pltpu.VMEM((members * len(pieces), block * width), jnp.float32)],
        compiler_params=params(20),
        name="rotate",
    )(index, high, low, in_hbm(basis), *pieces)


def per_device(initial_disp, initial_vel, stiffness, basis, rotation):
    ranks, sims = lax.axis_size("ana"), lax.axis_size("sim")
    ana, sim = lax.axis_index("ana"), lax.axis_index("sim")
    lines, width, rank = basis.shape
    count = lines * width * sims * ranks
    chips = sims // 2
    core = sim % 2
    near, far = list(range(1, ranks // 2)), list(range(ranks // 2, ranks))
    orders = (near + far[::-1] + [0], far[::-1] + near + [0])
    masks = jnp.where(core == 0, jnp.array(orders[0]), jnp.array(orders[1]))
    first_index = jnp.stack([ana, core, sim // 2])
    index = jnp.concatenate([first_index, masks]).astype(jnp.int32)

    last, first = edges(initial_disp, initial_vel, stiffness)
    up = [(i, i + 1) for i in range(sims - 1)]
    before = lax.ppermute(last, "sim", up)
    after = lax.ppermute(first, "sim", [(j, i) for i, j in up])
    late_disp, late_vel, _ = lax.optimization_barrier((initial_disp, initial_vel, last[0, 0, 0]))
    disp, vel = to_lines(late_disp, late_vel)
    before, after, disp = lax.optimization_barrier((before, after, disp))

    pieces = list(evolve(index, disp, vel, stiffness, before, after, ranks))
    order, pieces = lax.optimization_barrier((index, pieces))
    for slot in range(ranks - 1):
        pairs = [(s * ranks + a, s * ranks + (a ^ orders[s % 2][slot])) for s in range(sims) for a in range(ranks)]
        pieces[slot] = lax.ppermute(pieces[slot], ("sim", "ana"), pairs)

    def meanwhile(_, carry):
        at, _ = carry
        send, keep = basis_gram(at, basis)
        return at + (at >> 20), chip_scatter(at, send, keep, 2)

    order, gram = lax.fori_loop(0, 1 + (ana >> 20), meanwhile, (order, jnp.zeros((rank // sims, rank), jnp.float32)))
    gram_parts = [xor_permute(gram, "ana", k) for k in range(1, ranks)]

    send, keep = products(order, basis, pieces)
    sums = chip_scatter(order, send, keep, chips)
    sums, gram, gram_parts = lax.optimization_barrier((sums, gram, gram_parts))
    gram = chip_gather(tree_sum([gram] + gram_parts), chips)
    sums = ana_sum(sums)
    sums = with_other_core(chip_gather(sums, chips))
    gram = with_other_core(gram)
    high, low, coords = solve(index, sums, gram, rotation, count, chips)
    return rotate(index, high, low, basis, pieces), coords


def solution(mesh):
    in_specs = (
        P("ana", "sim", None),
        P("ana", "sim", None),
        P("sim", None),
        P(("sim", "ana"), None, None),
        P(),
    )
    out_specs = (P(("sim", "ana"), None, None), P())
    return jax.shard_map(
        per_device, mesh=mesh, in_specs=in_specs, out_specs=out_specs, check_vma=False
    )
```

```python
import functools
import math

import jax
import jax.numpy as jnp
from jax import lax
from jax.experimental import pallas as pl
from jax.experimental.pallas import tpu as pltpu
from jax.sharding import PartitionSpec as P

STEPS = 4
EPS = 1e-06
MIB = 1024 * 1024
HI = lax.Precision.HIGHEST
FIRST = 3
SCALARS = pl.BlockSpec(memory_space=pltpu.SMEM)


def mm(left, right, dims, precision=HI):
    return lax.dot_general(left, right, (dims, ((), ())), precision=precision, preferred_element_type=jnp.float32)


def shape(*dims, dtype=jnp.float32):
    return jax.ShapeDtypeStruct(dims, dtype)


def params(mib):
    return pltpu.CompilerParams(vmem_limit_bytes=mib * MIB)


def in_hbm(value):
    return pltpu.with_memory_space_constraint(value, pltpu.HBM)


def halves(value):
    high = value.astype(jnp.bfloat16)
    return high, (value - high.astype(jnp.float32)).astype(jnp.bfloat16)


def thirds(value):
    high, _ = halves(value)
    rest = value - high.astype(jnp.float32)
    return (high,) + halves(rest)


def mm3(left, right, dims):
    (lh, ll), (rh, rl) = left, right
    return mm(lh, rh, dims, None) + (mm(lh, rl, dims, None) + mm(ll, rh, dims, None))


def xor_permute(value, axis, mask):
    size = lax.axis_size(axis)
    return lax.ppermute(value, axis, [(i, i ^ mask) for i in range(size)])


def edges_kernel(stiff_ref, disp_low, vel_low, disp_high, vel_high, last_ref, first_ref):
    w = STEPS
    lines = stiff_ref.shape[0]
    for ref, disp, vel, at, start in ((last_ref, disp_high, vel_high, 8 - w, lines - w), (first_ref, disp_low, vel_low, 0, 0)):
        for i in range(w):
            ref[i] = disp[:, at + i, :]
            ref[w + i] = vel[:, at + i, :]
        ref[2 * w] = jnp.zeros_like(ref[2 * w])
        ref[2 * w, :w, :] = stiff_ref[start:start + w, :]


def edges(disp, vel, stiff):
    members, lines, width = disp.shape
    w = STEPS
    low = pl.BlockSpec((members, 8, width), lambda i: (0, 0, 0))
    high = pl.BlockSpec((members, 8, width), lambda i: (0, lines // 8 - 1, 0))
    edge = pl.BlockSpec((2 * w + 1, members, width), lambda i: (0, 0, 0))
    return pl.pallas_call(
        edges_kernel,
        grid=(1,),
        in_specs=[pl.BlockSpec((lines, width), lambda i: (0, 0)), low, low, high, high],
        out_specs=[edge, edge],
        out_shape=[pltpu.HBM((2 * w + 1, members, width), jnp.float32)] * 2,
        compiler_params=params(6),
        name="edges",
    )(in_hbm(stiff), in_hbm(disp), in_hbm(vel), in_hbm(disp), in_hbm(vel))


def to_lines_kernel(disp_ref, vel_ref, disp_out, vel_out):
    lines, group, _ = disp_out.shape
    for line in range(lines):
        disp_out[line] = disp_ref[pl.ds(line, group, stride=lines), :]
        vel_out[line] = vel_ref[pl.ds(line, group, stride=lines), :]


def to_lines(disp, vel):
    members, lines, width = disp.shape
    group = 16
    flat = pl.BlockSpec((group * lines, width), lambda i: (i, 0))
    out = pl.BlockSpec((lines, group, width), lambda i: (0, i, 0))
    return pl.pallas_call(
        to_lines_kernel,
        grid=(members // group,),
        in_specs=[flat, flat],
        out_specs=[out, out],
        out_shape=[shape(lines, members, width)] * 2,
        compiler_params=params(8),
        name="to_lines",
    )(in_hbm(disp.reshape(members * lines, width)), in_hbm(vel.reshape(members * lines, width)))


def evolve_kernel(index_ref, disp_ref, vel_ref, stiff_ref, before_ref, after_ref, *rest, slots):
    outs, (even_ref, odd_ref, speed_ref, pad_ref, all_ref, sem) = rest[:slots], rest[slots:]
    lines, members, width = disp_ref.shape
    w = STEPS
    full = lines + 2 * w
    size = lines // slots
    lane = lax.broadcasted_iota(jnp.int32, (8, width), 1)
    pad_ref[w:2 * w, :] = before_ref[2 * w, :w, :]
    pad_ref[8:8 + lines, :] = stiff_ref[...]
    pad_ref[8 + lines:8 + lines + w, :] = after_ref[2 * w, :w, :]

    def group_step(g, carry):
        at = pl.ds(pl.multiple_of(g * 8, 8), 8)
        for i in range(w):
            even_ref[i], speed_ref[i] = before_ref[i, at, :], before_ref[w + i, at, :]
            even_ref[w + lines + i], speed_ref[w + lines + i] = after_ref[i, at, :], after_ref[w + i, at, :]
        for i in range(lines):
            even_ref[w + i], speed_ref[w + i] = disp_ref[i, at, :], vel_ref[i, at, :]
        now, then = even_ref, odd_ref
        for step in range(1, w + 1):
            for i in range(step, full - step):
                u = now[i]
                right = jnp.where(lane == width - 1, 0.0, pltpu.roll(u, width - 1, 1))
                left = jnp.where(lane == 0, 0.0, pltpu.roll(u, 1, 1))
                around = (now[i + 1] + now[i - 1]) + (right + left)
                stiff = jnp.broadcast_to(pad_ref[8 - w + i:8 - w + i + 1, :], (8, width))
                speed = speed_ref[i] + stiff * (around + u * (0.5 / (1.0 + u * u) - 4.5))
                if step < w:
                    then[i], speed_ref[i] = u + speed, speed
                else:
                    all_ref[i - w, at, :] = u + speed
            now, then = then, now
        for slot, out in enumerate(outs):
            pltpu.make_async_copy(all_ref.at[block(slot), at], out.at[:, at], sem.at[slot]).start()
        return carry

    def block(slot):
        return pl.ds((index_ref[0] ^ index_ref[FIRST + slot]) * size, size)

    lax.fori_loop(0, members // 8, group_step, 0)
    for slot, out in enumerate(outs):
        pltpu.make_async_copy(all_ref.at[block(slot)], out, sem.at[slot]).wait()


def evolve(index, disp, vel, stiff, before, after, slots):
    lines, members, width = disp.shape
    line = pltpu.VMEM((lines + 2 * STEPS, 8, width), jnp.float32)
    return pl.pallas_call(
        functools.partial(evolve_kernel, slots=slots),
        in_specs=[SCALARS] + [pl.BlockSpec(memory_space=pltpu.VMEM)] * 5,
        out_shape=[pltpu.HBM((lines // slots, members, width), jnp.float32)] * slots,
        out_specs=[pl.BlockSpec(memory_space=pltpu.HBM)] * slots,
        scratch_shapes=[line, line, line, pltpu.VMEM((lines + 16, width), jnp.float32),
                        pltpu.VMEM((lines, members, width), jnp.float32), pltpu.SemaphoreType.DMA((slots,))],
        compiler_params=params(8),
        name="evolve",
    )(index, disp, vel, stiff, before, after)


def basis_gram_kernel(index_ref, basis_ref, send_ref, keep_ref, sum_ref, mixed_ref):
    lines, width, rank = basis_ref.shape
    step = pl.program_id(0)

    @pl.when(step == 0)
    def _():
        sum_ref[...] = jnp.zeros_like(sum_ref)
        mixed_ref[...] = jnp.zeros_like(mixed_ref)

    high, low = halves(basis_ref[...].reshape(lines * width, rank))
    sum_ref[...] += mm(high, high, ((0,), (0,)), None)
    mixed_ref[...] += mm(high, low, ((0,), (0,)), None)

    @pl.when(step == pl.num_programs(0) - 1)
    def _():
        sum_ref[...] += mixed_ref[...] + mixed_ref[...].T
        half = keep_ref.shape[0]
        core = index_ref[1]
        keep_ref[...] = sum_ref[pl.ds(pl.multiple_of(core * half, half), half), :]
        send_ref[...] = sum_ref[pl.ds(pl.multiple_of((1 - core) * half, half), half), :]


def basis_gram(index, basis):
    lines, width, rank = basis.shape
    block = 4
    half = pl.BlockSpec((rank // 2, rank), lambda i: (0, 0))
    return pl.pallas_call(
        basis_gram_kernel,
        grid=(lines // block,),
        in_specs=[SCALARS, pl.BlockSpec((block, width, rank), lambda i: (i, 0, 0))],
        out_specs=[half, half],
        out_shape=[shape(rank // 2, rank)] * 2,
        scratch_shapes=[pltpu.VMEM((rank, rank), jnp.float32)] * 2,
        compiler_params=params(14),
        name="basis_gram",
    )(index, in_hbm(basis))


def products_kernel(index_ref, basis_ref, *rest):
    pieces, (send_ref, keep_ref, snap_ref, sum_ref, mixed_ref) = rest[:-5], rest[-5:]
    lines, members, width = pieces[0].shape
    rank = basis_ref.shape[-1]
    step = pl.program_id(0)
    for k, piece in enumerate(pieces):
        at = pl.multiple_of((index_ref[0] ^ index_ref[FIRST + k]) * members, members)
        for line in range(lines):
            snap_ref[pl.ds(at, members), line * width:(line + 1) * width] = piece[line]

    @pl.when(step == 0)
    def _():
        sum_ref[...] = jnp.zeros_like(sum_ref)
        mixed_ref[...] = jnp.zeros_like(mixed_ref)

    snap = halves(snap_ref[...])
    rows = basis_ref[...].reshape(lines * width, rank)
    sum_ref[:, :rank] += mm3(snap, halves(rows), ((1,), (0,)))
    sum_ref[:, rank:] += mm(snap[0], snap[0], ((1,), (1,)), None)
    mixed_ref[...] += mm(snap[0], snap[1], ((1,), (1,)), None)

    @pl.when(step == pl.num_programs(0) - 1)
    def _():
        sum_ref[:, rank:] += mixed_ref[...] + mixed_ref[...].T
        half = keep_ref.shape[0]
        core = index_ref[1]
        keep_ref[...] = sum_ref[pl.ds(pl.multiple_of(core * half, half), half), :]
        send_ref[...] = sum_ref[pl.ds(pl.multiple_of((1 - core) * half, half), half), :]


def products(index, basis, pieces):
    lines, width, rank = basis.shape
    members = pieces[0].shape[1]
    total = members * len(pieces)
    block = 4
    half = pl.BlockSpec((total // 2, rank + total), lambda i: (0, 0))
    return pl.pallas_call(
        products_kernel,
        grid=(lines // block,),
        in_specs=[SCALARS, pl.BlockSpec((block, width, rank), lambda i: (i, 0, 0))]
        + [pl.BlockSpec((block, members, width), lambda i: (i, 0, 0))] * len(pieces),
        out_specs=[half, half],
        out_shape=[shape(total // 2, rank + total)] * 2,
        scratch_shapes=[pltpu.VMEM((total, block * width), jnp.float32), pltpu.VMEM((total, rank + total), jnp.float32),
                        pltpu.VMEM((total, total), jnp.float32)],
        compiler_params=params(14),
        name="products",
    )(index, in_hbm(basis), *pieces)


def split_kernel(index_ref, keep_ref, got_ref, *outs):
    rows = outs[0].shape[0]
    for k, out in enumerate(outs):
        at = pl.ds(pl.multiple_of((index_ref[2] ^ k) * rows, rows), rows)
        out[...] = keep_ref[at, :] + got_ref[at, :]


def split(index, keep, got, chips):
    rows, cols = keep.shape
    return pl.pallas_call(
        split_kernel,
        in_specs=[SCALARS] + [pl.BlockSpec(memory_space=pltpu.VMEM)] * 2,
        out_shape=[shape(rows // chips, cols)] * chips,
        compiler_params=params(4),
        name="split",
    )(index, keep, got)


def tree_sum(values):
    while len(values) > 1:
        values = [a + b for a, b in zip(values[::2], values[1::2])]
    return values[0]


def ana_sum_by_pairs(value, bits):
    for bit in bits:
        value = value + xor_permute(value, "ana", bit)
    return value


def exchange_chips(pieces, limit):
    found = []
    for k in range(1, len(pieces)):
        piece = pieces[k]
        if k > limit:
            piece, found[k - limit - 1] = lax.optimization_barrier((piece, found[k - limit - 1]))
        found.append(xor_permute(piece, "sim", 2 * k))
    return found


def chip_scatter(index, send, keep, limit):
    chips = lax.axis_size("sim") // 2
    got = xor_permute(send, "sim", 1)
    pieces = split(index, keep, got, chips)
    return tree_sum([pieces[0]] + exchange_chips(pieces, limit))


def ana_sum(value):
    return tree_sum([value] + [xor_permute(value, "ana", k) for k in range(1, lax.axis_size("ana"))])


def chip_gather(value, limit):
    chips = lax.axis_size("sim") // 2
    return jnp.concatenate([value] + exchange_chips([value] * chips, limit), axis=0)


def with_other_core(value):
    return value, xor_permute(value, "sim", 1)


PANEL = 32

def eliminate(work_ref, members):
    tiles = work_ref.shape[1] // 128
    groups = PANEL // 8
    sub = lax.broadcasted_iota(jnp.int32, (8, 128), 0)

    def panel_step(k, carry):
        start = pl.multiple_of(k * PANEL, PANEL)
        at = pl.multiple_of((k * PANEL) // 128 * 128, 128)
        diag = work_ref[pl.ds(start, PANEL), pl.ds(at, 128)]
        diag = pltpu.roll(diag, (128 - (k * PANEL) % 128) % 128, 1)
        rows = work_ref[pl.ds(start, PANEL), :]
        x = [[rows[8 * g:8 * g + 8, 128 * t:128 * t + 128] for t in range(tiles)] + [diag[8 * g:8 * g + 8]]
             for g in range(groups)]
        for b in range(groups):
            cols = {g: [jnp.broadcast_to(x[g][tiles][:, 8 * b + j:8 * b + j + 1], (8, 128)) for j in range(8)]
                    for g in range(b, groups)}
            pivots = jnp.ones((8, 128), jnp.float32)
            for r in range(8):
                pivot = jnp.broadcast_to(cols[b][r][r:r + 1], (8, 128))
                pivots = jnp.where(sub == r, pivot, pivots)
                inverse = 1.0 / pivot
                raw = [jnp.broadcast_to(v[r:r + 1], (8, 128)) for v in x[b]]
                craw = [jnp.broadcast_to(cols[b][j][r:r + 1], (8, 128)) if j > r else None for j in range(8)]
                for g in range(b, groups):
                    coef = cols[g][r] * inverse
                    if g == b:
                        coef = jnp.where(sub > r, coef, 0.0)
                    x[g] = [v - coef * w for v, w in zip(x[g], raw)]
                    cols[g] = [cols[g][j] - coef * craw[j] if j > r else cols[g][j] for j in range(8)]
            x[b] = [v * lax.rsqrt(pivots) for v in x[b]]
        done = jnp.concatenate([jnp.concatenate(v[:tiles], axis=1) for v in x], axis=0)
        lane = lax.broadcasted_iota(jnp.int32, (PANEL, members), 1)
        lower = jnp.where(lane >= start + PANEL, done[:, :members], 0.0)
        lh, lm, ll = thirds(lower)
        dh, dm, dl = thirds(done)
        left = jnp.concatenate([lh, lh, lm, lh, ll, lm], axis=0)
        right = jnp.concatenate([dh, dm, dh, dl, dh, dm], axis=0)
        work_ref[...] = work_ref[...] - mm(left, right, ((0,), (0,)), None)
        work_ref[pl.ds(start, PANEL), :] = done
        return carry

    lax.fori_loop(0, members // PANEL, panel_step, 0)


def ordered(index_ref, mine_ref, other_ref, out_ref, chips):
    half = mine_ref.shape[0]
    rows = half // chips
    for k in range(chips):
        at = (index_ref[2] ^ k) * rows
        piece = slice(k * rows, (k + 1) * rows)
        out_ref[pl.ds(pl.multiple_of(index_ref[1] * half + at, rows), rows), :] = mine_ref[piece, :]
        out_ref[pl.ds(pl.multiple_of((1 - index_ref[1]) * half + at, rows), rows), :] = other_ref[piece, :]


def solve_kernel(index_ref, sums_ref, sums2_ref, gram_ref, gram2_ref, rot_ref, high_ref, low_ref, coords_ref,
                 work_ref, all_ref, basis_ref, *, count, chips):
    rank, members = coords_ref.shape
    ordered(index_ref, sums_ref, sums2_ref, all_ref, chips)
    ordered(index_ref, gram_ref, gram2_ref, basis_ref, chips)
    row = lax.broadcasted_iota(jnp.int32, (members, members), 0)
    col = lax.broadcasted_iota(jnp.int32, (members, members), 1)
    eye = row == col
    inner = all_ref[:, rank:]
    diag = jnp.where(eye, inner, 0.0)
    across = lax.rsqrt(jnp.sum(diag, axis=0, keepdims=True) / count + EPS)
    along = lax.rsqrt(jnp.sum(diag, axis=1, keepdims=True) / count + EPS)
    coef = all_ref[:, :rank] * (along / count)
    correct = 2.0 * coef - mm(coef, basis_ref[...], ((1,), (0,))) / count
    work_ref[:, :members] = inner * (along / count) * across - mm(correct, coef, ((1,), (1,)))
    work_ref[:, members:] = jnp.where(eye, 1.0, 0.0)
    eliminate(work_ref, members)
    top, bottom = rot_ref[:rank, :], rot_ref[rank:, :]
    upper = jnp.where(row <= col, work_ref[:, :members], 0.0)
    tops, bottoms, coefs = halves(top), halves(bottom), halves(coef)
    mix = mm3(halves(work_ref[:, members:]), bottoms, ((0,), (0,)))
    high_ref[:rank, :], low_ref[:rank, :] = halves(top - mm3(coefs, halves(mix), ((0,), (0,))))
    high_ref[rank:, :], low_ref[rank:, :] = halves(mix * along)
    coords = (mm3(coefs, tops, ((1,), (0,))) + mm3(halves(upper), bottoms, ((0,), (0,)))) * math.sqrt(rank)
    coords_ref[...] = coords.T


def solve(index, sums, gram, rotation, count, chips):
    rank = gram[0].shape[1]
    members = rotation.shape[0] - rank
    return pl.pallas_call(
        functools.partial(solve_kernel, count=float(count), chips=chips),
        in_specs=[SCALARS] + [pl.BlockSpec(memory_space=pltpu.VMEM)] * 5,
        out_shape=[shape(members + rank, rank, dtype=jnp.bfloat16)] * 2 + [shape(rank, members)],
        scratch_shapes=[pltpu.VMEM((members, 2 * members), jnp.float32),
                        pltpu.VMEM((members, rank + members), jnp.float32),
                        pltpu.VMEM((rank, rank), jnp.float32)],
        compiler_params=params(20),
        name="solve",
    )(index, *sums, *gram, rotation)


def rotate_kernel(index_ref, high_ref, low_ref, basis_ref, *rest):
    pieces, (out_ref, snap_ref) = rest[:-2], rest[-2:]
    lines, members, width = pieces[0].shape
    rank = basis_ref.shape[-1]
    for k, piece in enumerate(pieces):
        at = pl.multiple_of((index_ref[0] ^ index_ref[FIRST + k]) * members, members)
        for line in range(lines):
            snap_ref[pl.ds(at, members), line * width:(line + 1) * width] = piece[line]
    rows = basis_ref[...].reshape(lines * width, rank)
    out = mm3(halves(rows), (high_ref[:rank, :], low_ref[:rank, :]), ((1,), (0,)))
    out = out + mm3(halves(snap_ref[...].T), (high_ref[rank:, :], low_ref[rank:, :]), ((1,), (0,)))
    out_ref[...] = out.reshape(out_ref.shape)


def rotate(index, high, low, basis, pieces):
    lines, width, rank = basis.shape
    members = pieces[0].shape[1]
    block = 4
    rows = pl.BlockSpec((block, width, rank), lambda i: (i, 0, 0))
    return pl.pallas_call(
        rotate_kernel,
        grid=(lines // block,),
        in_specs=[SCALARS] + [pl.BlockSpec(high.shape, lambda i: (0, 0))] * 2 + [rows]
        + [pl.BlockSpec((block, members, width), lambda i: (i, 0, 0))] * len(pieces),
        out_specs=rows,
        out_shape=shape(lines, width, rank),
        scratch_shapes=[pltpu.VMEM((members * len(pieces), block * width), jnp.float32)],
        compiler_params=params(20),
        name="rotate",
    )(index, high, low, in_hbm(basis), *pieces)


def per_device(initial_disp, initial_vel, stiffness, basis, rotation):
    ranks, sims = lax.axis_size("ana"), lax.axis_size("sim")
    ana, sim = lax.axis_index("ana"), lax.axis_index("sim")
    lines, width, rank = basis.shape
    count = lines * width * sims * ranks
    chips = sims // 2
    core = sim % 2
    near, far = list(range(1, ranks // 2)), list(range(ranks // 2, ranks))
    orders = (near + far[::-1] + [0], far[::-1] + near + [0])
    masks = jnp.where(core == 0, jnp.array(orders[0]), jnp.array(orders[1]))
    first_index = jnp.stack([ana, core, sim // 2])
    index = jnp.concatenate([first_index, masks]).astype(jnp.int32)

    last, first = edges(initial_disp, initial_vel, stiffness)
    up = [(i, i + 1) for i in range(sims - 1)]
    before = lax.ppermute(last, "sim", up)
    after = lax.ppermute(first, "sim", [(j, i) for i, j in up])
    late_disp, late_vel, _ = lax.optimization_barrier((initial_disp, initial_vel, last[0, 0, 0]))
    disp, vel = to_lines(late_disp, late_vel)
    before, after, disp = lax.optimization_barrier((before, after, disp))

    pieces = list(evolve(index, disp, vel, stiffness, before, after, ranks))
    order, pieces = lax.optimization_barrier((index, pieces))
    for slot in range(ranks - 1):
        pairs = [(s * ranks + a, s * ranks + (a ^ orders[s % 2][slot])) for s in range(sims) for a in range(ranks)]
        pieces[slot] = lax.ppermute(pieces[slot], ("sim", "ana"), pairs)

    def meanwhile(_, carry):
        at, _ = carry
        send, keep = basis_gram(at, basis)
        return at + (at >> 20), ana_sum_by_pairs(chip_scatter(at, send, keep, 2), bits[:-1])

    bits = [2 ** i for i in range(ranks.bit_length() - 1)]
    order, gram = lax.fori_loop(0, 1 + (ana >> 20), meanwhile, (order, jnp.zeros((rank // sims, rank), jnp.float32)))
    gram = ana_sum_by_pairs(gram, bits[-1:])

    send, keep = products(order, basis, pieces)
    sums = chip_scatter(order, send, keep, chips)
    sums, gram = lax.optimization_barrier((sums, gram))
    gram = chip_gather(gram, chips)
    sums = ana_sum(sums)
    sums = with_other_core(chip_gather(sums, chips))
    gram = with_other_core(gram)
    high, low, coords = solve(index, sums, gram, rotation, count, chips)
    return rotate(index, high, low, basis, pieces), coords


def solution(mesh):
    in_specs = (
        P("ana", "sim", None),
        P("ana", "sim", None),
        P("sim", None),
        P(("sim", "ana"), None, None),
        P(),
    )
    out_specs = (P(("sim", "ana"), None, None), P())
    return jax.shard_map(
        per_device, mesh=mesh, in_specs=in_specs, out_specs=out_specs, check_vma=False
    )
```

```python
import functools
import math

import jax
import jax.numpy as jnp
from jax import lax
from jax.experimental import pallas as pl
from jax.experimental.pallas import tpu as pltpu
from jax.sharding import PartitionSpec as P

STEPS = 4
EPS = 1e-06
MIB = 1024 * 1024
HI = lax.Precision.HIGHEST
FIRST = 3
SCALARS = pl.BlockSpec(memory_space=pltpu.SMEM)


def mm(left, right, dims, precision=HI):
    return lax.dot_general(left, right, (dims, ((), ())), precision=precision, preferred_element_type=jnp.float32)


def shape(*dims, dtype=jnp.float32):
    return jax.ShapeDtypeStruct(dims, dtype)


def params(mib):
    return pltpu.CompilerParams(vmem_limit_bytes=mib * MIB)


def in_hbm(value):
    return pltpu.with_memory_space_constraint(value, pltpu.HBM)


def halves(value):
    high = value.astype(jnp.bfloat16)
    return high, (value - high.astype(jnp.float32)).astype(jnp.bfloat16)


def thirds(value):
    high, _ = halves(value)
    rest = value - high.astype(jnp.float32)
    return (high,) + halves(rest)


def mm3(left, right, dims):
    (lh, ll), (rh, rl) = left, right
    return mm(lh, rh, dims, None) + (mm(lh, rl, dims, None) + mm(ll, rh, dims, None))


def xor_permute(value, axis, mask):
    size = lax.axis_size(axis)
    return lax.ppermute(value, axis, [(i, i ^ mask) for i in range(size)])


def edges_kernel(stiff_ref, disp_low, vel_low, disp_high, vel_high, last_ref, first_ref):
    w = STEPS
    lines = stiff_ref.shape[0]
    for ref, disp, vel, at, start in ((last_ref, disp_high, vel_high, 8 - w, lines - w), (first_ref, disp_low, vel_low, 0, 0)):
        for i in range(w):
            ref[i] = disp[:, at + i, :]
            ref[w + i] = vel[:, at + i, :]
        ref[2 * w] = jnp.zeros_like(ref[2 * w])
        ref[2 * w, :w, :] = stiff_ref[start:start + w, :]


def edges(disp, vel, stiff):
    members, lines, width = disp.shape
    w = STEPS
    low = pl.BlockSpec((members, 8, width), lambda i: (0, 0, 0))
    high = pl.BlockSpec((members, 8, width), lambda i: (0, lines // 8 - 1, 0))
    edge = pl.BlockSpec((2 * w + 1, members, width), lambda i: (0, 0, 0))
    return pl.pallas_call(
        edges_kernel,
        grid=(1,),
        in_specs=[pl.BlockSpec((lines, width), lambda i: (0, 0)), low, low, high, high],
        out_specs=[edge, edge],
        out_shape=[pltpu.HBM((2 * w + 1, members, width), jnp.float32)] * 2,
        compiler_params=params(6),
        name="edges",
    )(in_hbm(stiff), in_hbm(disp), in_hbm(vel), in_hbm(disp), in_hbm(vel))


def to_lines_kernel(disp_ref, vel_ref, disp_out, vel_out):
    lines, group, _ = disp_out.shape
    for line in range(lines):
        disp_out[line] = disp_ref[pl.ds(line, group, stride=lines), :]
        vel_out[line] = vel_ref[pl.ds(line, group, stride=lines), :]


def to_lines(disp, vel):
    members, lines, width = disp.shape
    group = 16
    flat = pl.BlockSpec((group * lines, width), lambda i: (i, 0))
    out = pl.BlockSpec((lines, group, width), lambda i: (0, i, 0))
    return pl.pallas_call(
        to_lines_kernel,
        grid=(members // group,),
        in_specs=[flat, flat],
        out_specs=[out, out],
        out_shape=[shape(lines, members, width)] * 2,
        compiler_params=params(8),
        name="to_lines",
    )(in_hbm(disp.reshape(members * lines, width)), in_hbm(vel.reshape(members * lines, width)))


def evolve_kernel(index_ref, disp_ref, vel_ref, stiff_ref, before_ref, after_ref, *rest, slots):
    outs, (even_ref, odd_ref, speed_ref, pad_ref, all_ref, sem) = rest[:slots], rest[slots:]
    lines, members, width = disp_ref.shape
    w = STEPS
    full = lines + 2 * w
    size = lines // slots
    lane = lax.broadcasted_iota(jnp.int32, (8, width), 1)
    pad_ref[w:2 * w, :] = before_ref[2 * w, :w, :]
    pad_ref[8:8 + lines, :] = stiff_ref[...]
    pad_ref[8 + lines:8 + lines + w, :] = after_ref[2 * w, :w, :]

    def group_step(g, carry):
        at = pl.ds(pl.multiple_of(g * 8, 8), 8)
        for i in range(w):
            even_ref[i], speed_ref[i] = before_ref[i, at, :], before_ref[w + i, at, :]
            even_ref[w + lines + i], speed_ref[w + lines + i] = after_ref[i, at, :], after_ref[w + i, at, :]
        for i in range(lines):
            even_ref[w + i], speed_ref[w + i] = disp_ref[i, at, :], vel_ref[i, at, :]
        now, then = even_ref, odd_ref
        for step in range(1, w + 1):
            for i in range(step, full - step):
                u = now[i]
                right = jnp.where(lane == width - 1, 0.0, pltpu.roll(u, width - 1, 1))
                left = jnp.where(lane == 0, 0.0, pltpu.roll(u, 1, 1))
                around = (now[i + 1] + now[i - 1]) + (right + left)
                stiff = jnp.broadcast_to(pad_ref[8 - w + i:8 - w + i + 1, :], (8, width))
                speed = speed_ref[i] + stiff * (around + u * (0.5 / (1.0 + u * u) - 4.5))
                if step < w:
                    then[i], speed_ref[i] = u + speed, speed
                else:
                    all_ref[i - w, at, :] = u + speed
            now, then = then, now
        for slot, out in enumerate(outs):
            pltpu.make_async_copy(all_ref.at[block(slot), at], out.at[:, at], sem.at[slot]).start()
        return carry

    def block(slot):
        return pl.ds((index_ref[0] ^ index_ref[FIRST + slot]) * size, size)

    lax.fori_loop(0, members // 8, group_step, 0)
    for slot, out in enumerate(outs):
        pltpu.make_async_copy(all_ref.at[block(slot)], out, sem.at[slot]).wait()


def evolve(index, disp, vel, stiff, before, after, slots):
    lines, members, width = disp.shape
    line = pltpu.VMEM((lines + 2 * STEPS, 8, width), jnp.float32)
    return pl.pallas_call(
        functools.partial(evolve_kernel, slots=slots),
        in_specs=[SCALARS] + [pl.BlockSpec(memory_space=pltpu.VMEM)] * 5,
        out_shape=[pltpu.HBM((lines // slots, members, width), jnp.float32)] * slots,
        out_specs=[pl.BlockSpec(memory_space=pltpu.HBM)] * slots,
        scratch_shapes=[line, line, line, pltpu.VMEM((lines + 16, width), jnp.float32),
                        pltpu.VMEM((lines, members, width), jnp.float32), pltpu.SemaphoreType.DMA((slots,))],
        compiler_params=params(8),
        name="evolve",
    )(index, disp, vel, stiff, before, after)


def basis_kernel(index_ref, rot_ref, basis_ref, send_ref, keep_ref, high_ref, low_ref, turned_ref, sum_ref, mixed_ref):
    lines, width, rank = basis_ref.shape
    step = pl.program_id(0)

    @pl.when(step == 0)
    def _():
        sum_ref[...] = jnp.zeros_like(sum_ref)
        mixed_ref[...] = jnp.zeros_like(mixed_ref)

    high, low = halves(basis_ref[...].reshape(lines * width, rank))
    high_ref[...] = high
    low_ref[...] = low
    sum_ref[...] += mm(high, high, ((0,), (0,)), None)
    mixed_ref[...] += mm(high, low, ((0,), (0,)), None)
    turned_ref[...] = mm3((high, low), halves(rot_ref[...]), ((1,), (0,)))

    @pl.when(step == pl.num_programs(0) - 1)
    def _():
        sum_ref[...] += mixed_ref[...] + mixed_ref[...].T
        half = keep_ref.shape[0]
        core = index_ref[1]
        keep_ref[...] = sum_ref[pl.ds(pl.multiple_of(core * half, half), half), :]
        send_ref[...] = sum_ref[pl.ds(pl.multiple_of((1 - core) * half, half), half), :]


def basis_parts(index, basis, rotation):
    lines, width, rank = basis.shape
    block = 4
    half = pl.BlockSpec((rank // 2, rank), lambda i: (0, 0))
    rows = pl.BlockSpec((block * width, rank), lambda i: (i, 0))
    return pl.pallas_call(
        basis_kernel,
        grid=(lines // block,),
        in_specs=[SCALARS, pl.BlockSpec((rank, rank), lambda i: (0, 0)), pl.BlockSpec((block, width, rank), lambda i: (i, 0, 0))],
        out_specs=[half, half, rows, rows, rows],
        out_shape=[shape(rank // 2, rank)] * 2 + [pltpu.HBM((lines * width, rank), jnp.bfloat16)] * 2
        + [pltpu.HBM((lines * width, rank), jnp.float32)],
        scratch_shapes=[pltpu.VMEM((rank, rank), jnp.float32)] * 2,
        compiler_params=params(24),
        name="basis_parts",
    )(index, in_hbm(rotation), in_hbm(basis))


def products_kernel(index_ref, high_ref, low_ref, *rest):
    pieces, (send_ref, keep_ref, snap_ref, sum_ref, mixed_ref) = rest[:-5], rest[-5:]
    lines, members, width = pieces[0].shape
    rank = high_ref.shape[-1]
    step = pl.program_id(0)
    for k, piece in enumerate(pieces):
        at = pl.multiple_of((index_ref[0] ^ index_ref[FIRST + k]) * members, members)
        for line in range(lines):
            snap_ref[pl.ds(at, members), line * width:(line + 1) * width] = piece[line]

    @pl.when(step == 0)
    def _():
        sum_ref[...] = jnp.zeros_like(sum_ref)
        mixed_ref[...] = jnp.zeros_like(mixed_ref)

    snap = halves(snap_ref[...])
    sum_ref[:, :rank] += mm3(snap, (high_ref[...], low_ref[...]), ((1,), (0,)))
    sum_ref[:, rank:] += mm(snap[0], snap[0], ((1,), (1,)), None)
    mixed_ref[...] += mm(snap[0], snap[1], ((1,), (1,)), None)

    @pl.when(step == pl.num_programs(0) - 1)
    def _():
        sum_ref[:, rank:] += mixed_ref[...] + mixed_ref[...].T
        half = keep_ref.shape[0]
        core = index_ref[1]
        keep_ref[...] = sum_ref[pl.ds(pl.multiple_of(core * half, half), half), :]
        send_ref[...] = sum_ref[pl.ds(pl.multiple_of((1 - core) * half, half), half), :]


def products(index, high, low, pieces):
    rank = high.shape[1]
    lines, members, width = pieces[0].shape
    total = members * len(pieces)
    block = 4
    half = pl.BlockSpec((total // 2, rank + total), lambda i: (0, 0))
    return pl.pallas_call(
        products_kernel,
        grid=(lines // block,),
        in_specs=[SCALARS] + [pl.BlockSpec((block * width, rank), lambda i: (i, 0))] * 2
        + [pl.BlockSpec((block, members, width), lambda i: (i, 0, 0))] * len(pieces),
        out_specs=[half, half],
        out_shape=[shape(total // 2, rank + total)] * 2,
        scratch_shapes=[pltpu.VMEM((total, block * width), jnp.float32), pltpu.VMEM((total, rank + total), jnp.float32),
                        pltpu.VMEM((total, total), jnp.float32)],
        compiler_params=params(14),
        name="products",
    )(index, in_hbm(high), in_hbm(low), *pieces)


def split_kernel(index_ref, keep_ref, got_ref, *outs):
    rows = outs[0].shape[0]
    for k, out in enumerate(outs):
        at = pl.ds(pl.multiple_of((index_ref[2] ^ k) * rows, rows), rows)
        out[...] = keep_ref[at, :] + got_ref[at, :]


def split(index, keep, got, chips):
    rows, cols = keep.shape
    return pl.pallas_call(
        split_kernel,
        in_specs=[SCALARS] + [pl.BlockSpec(memory_space=pltpu.VMEM)] * 2,
        out_shape=[shape(rows // chips, cols)] * chips,
        compiler_params=params(4),
        name="split",
    )(index, keep, got)


def tree_sum(values):
    while len(values) > 1:
        values = [a + b for a, b in zip(values[::2], values[1::2])]
    return values[0]


def ana_sum_by_pairs(value, bits):
    for bit in bits:
        value = value + xor_permute(value, "ana", bit)
    return value


def exchange_chips(pieces, limit):
    found = []
    for k in range(1, len(pieces)):
        piece = pieces[k]
        if k > limit:
            piece, found[k - limit - 1] = lax.optimization_barrier((piece, found[k - limit - 1]))
        found.append(xor_permute(piece, "sim", 2 * k))
    return found


def chip_scatter(index, send, keep, limit):
    chips = lax.axis_size("sim") // 2
    got = xor_permute(send, "sim", 1)
    pieces = split(index, keep, got, chips)
    return tree_sum([pieces[0]] + exchange_chips(pieces, limit))


def ana_sum(value):
    return tree_sum([value] + [xor_permute(value, "ana", k) for k in range(1, lax.axis_size("ana"))])


def chip_gather(value, limit):
    chips = lax.axis_size("sim") // 2
    return jnp.concatenate([value] + exchange_chips([value] * chips, limit), axis=0)


def with_other_core(value):
    return value, xor_permute(value, "sim", 1)


PANEL = 32

def eliminate(work_ref, members, aside):
    tiles = work_ref.shape[1] // 128
    groups = PANEL // 8
    sub = lax.broadcasted_iota(jnp.int32, (8, 128), 0)

    def panel_step(k, carry):
        aside(k)
        start = pl.multiple_of(k * PANEL, PANEL)
        at = pl.multiple_of((k * PANEL) // 128 * 128, 128)
        diag = work_ref[pl.ds(start, PANEL), pl.ds(at, 128)]
        diag = pltpu.roll(diag, (128 - (k * PANEL) % 128) % 128, 1)
        rows = work_ref[pl.ds(start, PANEL), :]
        x = [[rows[8 * g:8 * g + 8, 128 * t:128 * t + 128] for t in range(tiles)] + [diag[8 * g:8 * g + 8]]
             for g in range(groups)]
        for b in range(groups):
            cols = {g: [jnp.broadcast_to(x[g][tiles][:, 8 * b + j:8 * b + j + 1], (8, 128)) for j in range(8)]
                    for g in range(b, groups)}
            pivots = jnp.ones((8, 128), jnp.float32)
            for r in range(8):
                pivot = jnp.broadcast_to(cols[b][r][r:r + 1], (8, 128))
                pivots = jnp.where(sub == r, pivot, pivots)
                inverse = 1.0 / pivot
                raw = [jnp.broadcast_to(v[r:r + 1], (8, 128)) for v in x[b]]
                craw = [jnp.broadcast_to(cols[b][j][r:r + 1], (8, 128)) if j > r else None for j in range(8)]
                for g in range(b, groups):
                    coef = cols[g][r] * inverse
                    if g == b:
                        coef = jnp.where(sub > r, coef, 0.0)
                    x[g] = [v - coef * w for v, w in zip(x[g], raw)]
                    cols[g] = [cols[g][j] - coef * craw[j] if j > r else cols[g][j] for j in range(8)]
            x[b] = [v * lax.rsqrt(pivots) for v in x[b]]
        done = jnp.concatenate([jnp.concatenate(v[:tiles], axis=1) for v in x], axis=0)
        lane = lax.broadcasted_iota(jnp.int32, (PANEL, members), 1)
        lower = jnp.where(lane >= start + PANEL, done[:, :members], 0.0)
        lh, lm, ll = thirds(lower)
        dh, dm, dl = thirds(done)
        left = jnp.concatenate([lh, lh, lm, lh, ll, lm], axis=0)
        right = jnp.concatenate([dh, dm, dh, dl, dh, dm], axis=0)
        work_ref[...] = work_ref[...] - mm(left, right, ((0,), (0,)), None)
        work_ref[pl.ds(start, PANEL), :] = done
        return carry

    lax.fori_loop(0, members // PANEL, panel_step, 0)


def ordered(index_ref, mine_ref, other_ref, out_ref, chips):
    half = mine_ref.shape[0]
    rows = half // chips
    for k in range(chips):
        at = (index_ref[2] ^ k) * rows
        piece = slice(k * rows, (k + 1) * rows)
        out_ref[pl.ds(pl.multiple_of(index_ref[1] * half + at, rows), rows), :] = mine_ref[piece, :]
        out_ref[pl.ds(pl.multiple_of((1 - index_ref[1]) * half + at, rows), rows), :] = other_ref[piece, :]


def solve_kernel(index_ref, sums_ref, sums2_ref, gram_ref, gram2_ref, rot_ref, high_hbm, low_hbm, *rest, count, chips, ranks):
    pieces, rest = rest[:ranks], rest[ranks:]
    mix_high, mix_low, rem_high, rem_low, coords_ref = rest[:5]
    work_ref, all_ref, basis_ref, high_ref, low_ref, snap_ref, sem = rest[5:]
    rank, members = coords_ref.shape
    each = members // ranks
    copies = [pltpu.make_async_copy(high_hbm, high_ref, sem.at[0]), pltpu.make_async_copy(low_hbm, low_ref, sem.at[1])]
    for k, piece in enumerate(pieces):
        at = pl.multiple_of((index_ref[0] ^ index_ref[FIRST + k]) * each, each)
        copies.append(pltpu.make_async_copy(piece, snap_ref.at[:, pl.ds(at, each), :], sem.at[2 + k]))
    for copy in copies:
        copy.start()
    ordered(index_ref, sums_ref, sums2_ref, all_ref, chips)
    ordered(index_ref, gram_ref, gram2_ref, basis_ref, chips)
    row = lax.broadcasted_iota(jnp.int32, (members, members), 0)
    col = lax.broadcasted_iota(jnp.int32, (members, members), 1)
    eye = row == col
    inner = all_ref[:, rank:]
    diag = jnp.where(eye, inner, 0.0)
    across = lax.rsqrt(jnp.sum(diag, axis=0, keepdims=True) / count + EPS)
    along = lax.rsqrt(jnp.sum(diag, axis=1, keepdims=True) / count + EPS)
    coef = all_ref[:, :rank] * (along / count)
    correct = 2.0 * coef - mm(coef, basis_ref[...], ((1,), (0,))) / count
    work_ref[:, :members] = inner * (along / count) * across - mm(correct, coef, ((1,), (1,)))
    work_ref[:, members:] = jnp.where(eye, 1.0, 0.0)
    all_ref[:, :rank] = coef
    for copy in copies:
        copy.wait()
    lines, _, width = snap_ref.shape
    block = lines // (members // PANEL)

    def remainder(k):
        at = pl.ds(pl.multiple_of(k * (block * width), block * width), block * width)
        taken = mm3((high_ref[at, :], low_ref[at, :]), halves(all_ref[:, :rank]), ((1,), (1,)))
        panel = jnp.concatenate([snap_ref[k * block + i].T for i in range(block)], axis=0) * across
        rem_high[at, :], rem_low[at, :] = halves(panel - taken)

    eliminate(work_ref, members, remainder)
    coefs, tops, bottoms = halves(all_ref[:, :rank]), halves(rot_ref[:rank, :]), halves(rot_ref[rank:, :])
    upper = jnp.where(row <= col, work_ref[:, :members], 0.0)
    mix_high[...], mix_low[...] = halves(mm3(halves(work_ref[:, members:]), bottoms, ((0,), (0,))))
    coords = (mm3(coefs, tops, ((1,), (0,))) + mm3(halves(upper), bottoms, ((0,), (0,)))) * math.sqrt(rank)
    coords_ref[...] = coords.T


def solve(index, sums, gram, rotation, high, low, pieces, count, chips):
    rows, rank = high.shape
    members = rotation.shape[0] - rank
    ranks = len(pieces)
    lines, each, width = pieces[0].shape
    half = jnp.bfloat16
    return pl.pallas_call(
        functools.partial(solve_kernel, count=float(count), chips=chips, ranks=ranks),
        in_specs=[SCALARS] + [pl.BlockSpec(memory_space=pltpu.VMEM)] * 5 + [pl.BlockSpec(memory_space=pl.ANY)] * (2 + ranks),
        out_shape=[shape(members, rank, dtype=half)] * 2 + [shape(rows, members, dtype=half)] * 2 + [shape(rank, members)],
        scratch_shapes=[pltpu.VMEM((members, 2 * members), jnp.float32),
                        pltpu.VMEM((members, rank + members), jnp.float32),
                        pltpu.VMEM((rank, rank), jnp.float32),
                        pltpu.VMEM((rows, rank), half), pltpu.VMEM((rows, rank), half),
                        pltpu.VMEM((lines, members, width), jnp.float32), pltpu.SemaphoreType.DMA((2 + ranks,))],
        compiler_params=params(28),
        name="solve",
    )(index, *sums, *gram, rotation, high, low, *pieces)


def rotate_kernel(mix_high, mix_low, rem_high, rem_low, turned_ref, out_ref):
    out = turned_ref[...] + mm3((rem_high[...], rem_low[...]), (mix_high[...], mix_low[...]), ((1,), (0,)))
    out_ref[...] = out.reshape(out_ref.shape)


def rotate(mix, rest, turned, dims):
    lines, width, rank = dims
    members = mix[0].shape[0]
    block = 4
    return pl.pallas_call(
        rotate_kernel,
        grid=(lines // block,),
        in_specs=[pl.BlockSpec((members, rank), lambda i: (0, 0))] * 2 + [pl.BlockSpec((block * width, members), lambda i: (i, 0))] * 2
        + [pl.BlockSpec((block * width, rank), lambda i: (i, 0))],
        out_specs=pl.BlockSpec((block, width, rank), lambda i: (i, 0, 0)),
        out_shape=shape(lines, width, rank),
        compiler_params=params(14),
        name="rotate",
    )(*mix, *rest, in_hbm(turned))


def per_device(initial_disp, initial_vel, stiffness, basis, rotation):
    ranks, sims = lax.axis_size("ana"), lax.axis_size("sim")
    ana, sim = lax.axis_index("ana"), lax.axis_index("sim")
    lines, width, rank = basis.shape
    count = lines * width * sims * ranks
    chips = sims // 2
    core = sim % 2
    near, far = list(range(1, ranks // 2)), list(range(ranks // 2, ranks))
    orders = (near + far[::-1] + [0], far[::-1] + near + [0])
    masks = jnp.where(core == 0, jnp.array(orders[0]), jnp.array(orders[1]))
    first_index = jnp.stack([ana, core, sim // 2])
    index = jnp.concatenate([first_index, masks]).astype(jnp.int32)

    last, first = edges(initial_disp, initial_vel, stiffness)
    up = [(i, i + 1) for i in range(sims - 1)]
    before = lax.ppermute(last, "sim", up)
    after = lax.ppermute(first, "sim", [(j, i) for i, j in up])
    late_disp, late_vel, _ = lax.optimization_barrier((initial_disp, initial_vel, last[0, 0, 0]))
    disp, vel = to_lines(late_disp, late_vel)
    before, after, disp = lax.optimization_barrier((before, after, disp))

    pieces = list(evolve(index, disp, vel, stiffness, before, after, ranks))
    order, pieces = lax.optimization_barrier((index, pieces))
    for slot in range(ranks - 1):
        pairs = [(s * ranks + a, s * ranks + (a ^ orders[s % 2][slot])) for s in range(sims) for a in range(ranks)]
        pieces[slot] = lax.ppermute(pieces[slot], ("sim", "ana"), pairs)

    def meanwhile(_, carry):
        at, *_ = carry
        send, keep, high, low, turned = basis_parts(at, basis, rotation)
        return at + (at >> 20), ana_sum_by_pairs(chip_scatter(at, send, keep, 2), bits[:-1]), high, low, turned

    bits = [2 ** i for i in range(ranks.bit_length() - 1)]
    empty = [jnp.zeros((lines * width, rank), t) for t in (jnp.bfloat16, jnp.bfloat16, jnp.float32)]
    order, gram, high, low, turned = lax.fori_loop(
        0, 1 + (ana >> 20), meanwhile, (order, jnp.zeros((rank // sims, rank), jnp.float32), *empty))
    gram = ana_sum_by_pairs(gram, bits[-1:])

    send, keep = products(order, high, low, pieces)
    sums = chip_scatter(order, send, keep, chips)
    sums, gram = lax.optimization_barrier((sums, gram))
    gram = chip_gather(gram, chips)
    sums = ana_sum(sums)
    sums = with_other_core(chip_gather(sums, chips))
    gram = with_other_core(gram)
    *found, coords = solve(index, sums, gram, rotation, high, low, pieces, count, chips)
    return rotate(found[:2], found[2:], turned, basis.shape), coords


def solution(mesh):
    in_specs = (
        P("ana", "sim", None),
        P("ana", "sim", None),
        P("sim", None),
        P(("sim", "ana"), None, None),
        P(),
    )
    out_specs = (P(("sim", "ana"), None, None), P())
    return jax.shard_map(
        per_device, mesh=mesh, in_specs=in_specs, out_specs=out_specs, check_vma=False
    )
```

```python
import functools
import math

import jax
import jax.numpy as jnp
from jax import lax
from jax.experimental import pallas as pl
from jax.experimental.pallas import tpu as pltpu
from jax.sharding import PartitionSpec as P

STEPS = 4
EPS = 1e-06
MIB = 1024 * 1024
HI = lax.Precision.HIGHEST
FIRST = 3
SCALARS = pl.BlockSpec(memory_space=pltpu.SMEM)


def mm(left, right, dims, precision=HI):
    return lax.dot_general(left, right, (dims, ((), ())), precision=precision, preferred_element_type=jnp.float32)


def shape(*dims, dtype=jnp.float32):
    return jax.ShapeDtypeStruct(dims, dtype)


def params(mib):
    return pltpu.CompilerParams(vmem_limit_bytes=mib * MIB)


def in_hbm(value):
    return pltpu.with_memory_space_constraint(value, pltpu.HBM)


def halves(value):
    high = value.astype(jnp.bfloat16)
    return high, (value - high.astype(jnp.float32)).astype(jnp.bfloat16)


def thirds(value):
    high, _ = halves(value)
    rest = value - high.astype(jnp.float32)
    return (high,) + halves(rest)


def mm3(left, right, dims):
    (lh, ll), (rh, rl) = left, right
    (over,), (under,) = dims
    return mm(jnp.concatenate([ll, lh, lh], axis=over), jnp.concatenate([rh, rl, rh], axis=under), dims, None)


def xor_permute(value, axis, mask):
    size = lax.axis_size(axis)
    return lax.ppermute(value, axis, [(i, i ^ mask) for i in range(size)])


def edges_kernel(stiff_ref, disp_low, vel_low, disp_high, vel_high, last_ref, first_ref):
    w = STEPS
    lines = stiff_ref.shape[0]
    for ref, disp, vel, at, start in ((last_ref, disp_high, vel_high, 8 - w, lines - w), (first_ref, disp_low, vel_low, 0, 0)):
        for i in range(w):
            ref[i] = disp[:, at + i, :]
            ref[w + i] = vel[:, at + i, :]
        ref[2 * w] = jnp.zeros_like(ref[2 * w])
        ref[2 * w, :w, :] = stiff_ref[start:start + w, :]


def edges(disp, vel, stiff):
    members, lines, width = disp.shape
    w = STEPS
    low = pl.BlockSpec((members, 8, width), lambda i: (0, 0, 0))
    high = pl.BlockSpec((members, 8, width), lambda i: (0, lines // 8 - 1, 0))
    edge = pl.BlockSpec((2 * w + 1, members, width), lambda i: (0, 0, 0))
    return pl.pallas_call(
        edges_kernel,
        grid=(1,),
        in_specs=[pl.BlockSpec((lines, width), lambda i: (0, 0)), low, low, high, high],
        out_specs=[edge, edge],
        out_shape=[pltpu.HBM((2 * w + 1, members, width), jnp.float32)] * 2,
        compiler_params=params(6),
        name="edges",
    )(in_hbm(stiff), in_hbm(disp), in_hbm(vel), in_hbm(disp), in_hbm(vel))


def to_lines_kernel(disp_ref, vel_ref, disp_out, vel_out):
    lines, group, _ = disp_out.shape
    for line in range(lines):
        disp_out[line] = disp_ref[pl.ds(line, group, stride=lines), :]
        vel_out[line] = vel_ref[pl.ds(line, group, stride=lines), :]


def to_lines(disp, vel):
    members, lines, width = disp.shape
    group = 16
    flat = pl.BlockSpec((group * lines, width), lambda i: (i, 0))
    out = pl.BlockSpec((lines, group, width), lambda i: (0, i, 0))
    return pl.pallas_call(
        to_lines_kernel,
        grid=(members // group,),
        in_specs=[flat, flat],
        out_specs=[out, out],
        out_shape=[shape(lines, members, width)] * 2,
        compiler_params=params(8),
        name="to_lines",
    )(in_hbm(disp.reshape(members * lines, width)), in_hbm(vel.reshape(members * lines, width)))


def evolve_kernel(index_ref, disp_ref, vel_ref, stiff_ref, before_ref, after_ref, *rest, slots):
    outs, (even_ref, odd_ref, speed_ref, pad_ref, all_ref, sem) = rest[:slots], rest[slots:]
    lines, members, width = disp_ref.shape
    w = STEPS
    full = lines + 2 * w
    size = lines // slots
    lane = lax.broadcasted_iota(jnp.int32, (8, width), 1)
    pad_ref[w:2 * w, :] = before_ref[2 * w, :w, :]
    pad_ref[8:8 + lines, :] = stiff_ref[...]
    pad_ref[8 + lines:8 + lines + w, :] = after_ref[2 * w, :w, :]

    def group_step(g, carry):
        at = pl.ds(pl.multiple_of(g * 8, 8), 8)
        for i in range(w):
            even_ref[i], speed_ref[i] = before_ref[i, at, :], before_ref[w + i, at, :]
            even_ref[w + lines + i], speed_ref[w + lines + i] = after_ref[i, at, :], after_ref[w + i, at, :]
        for i in range(lines):
            even_ref[w + i], speed_ref[w + i] = disp_ref[i, at, :], vel_ref[i, at, :]
        now, then = even_ref, odd_ref
        for step in range(1, w + 1):
            for i in range(step, full - step):
                u = now[i]
                right = jnp.where(lane == width - 1, 0.0, pltpu.roll(u, width - 1, 1))
                left = jnp.where(lane == 0, 0.0, pltpu.roll(u, 1, 1))
                around = (now[i + 1] + now[i - 1]) + (right + left)
                stiff = jnp.broadcast_to(pad_ref[8 - w + i:8 - w + i + 1, :], (8, width))
                speed = speed_ref[i] + stiff * (around + u * (0.5 / (1.0 + u * u) - 4.5))
                if step < w:
                    then[i], speed_ref[i] = u + speed, speed
                else:
                    all_ref[i - w, at, :] = u + speed
            now, then = then, now
        for slot, out in enumerate(outs):
            pltpu.make_async_copy(all_ref.at[block(slot), at], out.at[:, at], sem.at[slot]).start()
        return carry

    def block(slot):
        return pl.ds((index_ref[0] ^ index_ref[FIRST + slot]) * size, size)

    lax.fori_loop(0, members // 8, group_step, 0)
    for slot, out in enumerate(outs):
        pltpu.make_async_copy(all_ref.at[block(slot)], out, sem.at[slot]).wait()


def evolve(index, disp, vel, stiff, before, after, slots):
    lines, members, width = disp.shape
    line = pltpu.VMEM((lines + 2 * STEPS, 8, width), jnp.float32)
    return pl.pallas_call(
        functools.partial(evolve_kernel, slots=slots),
        in_specs=[SCALARS] + [pl.BlockSpec(memory_space=pltpu.VMEM)] * 5,
        out_shape=[pltpu.HBM((lines // slots, members, width), jnp.float32)] * slots,
        out_specs=[pl.BlockSpec(memory_space=pltpu.HBM)] * slots,
        scratch_shapes=[line, line, line, pltpu.VMEM((lines + 16, width), jnp.float32),
                        pltpu.VMEM((lines, members, width), jnp.float32), pltpu.SemaphoreType.DMA((slots,))],
        compiler_params=params(8),
        name="evolve",
    )(index, disp, vel, stiff, before, after)


def room(*arrays):
    return pl.pallas_call(
        lambda *refs: None,
        out_specs=[pl.BlockSpec(memory_space=pl.ANY)] * len(arrays),
        out_shape=[pltpu.HBM(a.shape, a.dtype) for a in arrays],
        name="room",
    )()


def basis_kernel(index_ref, rot_ref, basis_ref, send_ref, keep_ref, high_ref, low_ref, turned_ref, sum_ref, mixed_ref):
    lines, width, rank = basis_ref.shape
    step = pl.program_id(0)

    @pl.when(step == 0)
    def _():
        sum_ref[...] = jnp.zeros_like(sum_ref)
        mixed_ref[...] = jnp.zeros_like(mixed_ref)

    high, low = halves(basis_ref[...].reshape(lines * width, rank))
    high_ref[...] = high
    low_ref[...] = low
    sum_ref[...] += mm(high, high, ((0,), (0,)), None)
    mixed_ref[...] += mm(high, low, ((0,), (0,)), None)
    turned_ref[...] = mm3((high, low), halves(rot_ref[...]), ((1,), (0,)))

    @pl.when(step == pl.num_programs(0) - 1)
    def _():
        sum_ref[...] += mixed_ref[...] + mixed_ref[...].T
        half = keep_ref.shape[0]
        core = index_ref[1]
        keep_ref[...] = sum_ref[pl.ds(pl.multiple_of(core * half, half), half), :]
        send_ref[...] = sum_ref[pl.ds(pl.multiple_of((1 - core) * half, half), half), :]


def basis_parts(index, basis, rotation):
    lines, width, rank = basis.shape
    block = 4
    half = pl.BlockSpec((rank // 2, rank), lambda i: (0, 0))
    rows = pl.BlockSpec((block * width, rank), lambda i: (i, 0))
    return pl.pallas_call(
        basis_kernel,
        grid=(lines // block,),
        in_specs=[SCALARS, pl.BlockSpec((rank, rank), lambda i: (0, 0)), pl.BlockSpec((block, width, rank), lambda i: (i, 0, 0))],
        out_specs=[half, half, rows, rows, rows],
        out_shape=[shape(rank // 2, rank)] * 2 + [pltpu.HBM((lines * width, rank), jnp.bfloat16)] * 2
        + [pltpu.HBM((lines * width, rank), jnp.float32)],
        scratch_shapes=[pltpu.VMEM((rank, rank), jnp.float32)] * 2,
        compiler_params=params(24),
        name="basis_parts",
    )(index, in_hbm(rotation), in_hbm(basis))


def products_kernel(index_ref, high_ref, low_ref, *rest):
    pieces, (send_ref, keep_ref, snap_ref, sum_ref, mixed_ref) = rest[:-5], rest[-5:]
    lines, members, width = pieces[0].shape
    rank = high_ref.shape[-1]
    step = pl.program_id(0)
    for k, piece in enumerate(pieces):
        at = pl.multiple_of((index_ref[0] ^ index_ref[FIRST + k]) * members, members)
        for line in range(lines):
            snap_ref[pl.ds(at, members), line * width:(line + 1) * width] = piece[line]

    @pl.when(step == 0)
    def _():
        sum_ref[...] = jnp.zeros_like(sum_ref)
        mixed_ref[...] = jnp.zeros_like(mixed_ref)

    snap = halves(snap_ref[...])
    sum_ref[:, :rank] += mm3(snap, (high_ref[...], low_ref[...]), ((1,), (0,)))
    sum_ref[:, rank:] += mm(snap[0], snap[0], ((1,), (1,)), None)
    mixed_ref[...] += mm(snap[0], snap[1], ((1,), (1,)), None)

    @pl.when(step == pl.num_programs(0) - 1)
    def _():
        sum_ref[:, rank:] += mixed_ref[...] + mixed_ref[...].T
        half = keep_ref.shape[0]
        core = index_ref[1]
        keep_ref[...] = sum_ref[pl.ds(pl.multiple_of(core * half, half), half), :]
        send_ref[...] = sum_ref[pl.ds(pl.multiple_of((1 - core) * half, half), half), :]


def products(index, high, low, pieces):
    rank = high.shape[1]
    lines, members, width = pieces[0].shape
    total = members * len(pieces)
    block = 4
    half = pl.BlockSpec((total // 2, rank + total), lambda i: (0, 0))
    return pl.pallas_call(
        products_kernel,
        grid=(lines // block,),
        in_specs=[SCALARS] + [pl.BlockSpec((block * width, rank), lambda i: (i, 0))] * 2
        + [pl.BlockSpec((block, members, width), lambda i: (i, 0, 0))] * len(pieces),
        out_specs=[half, half],
        out_shape=[shape(total // 2, rank + total)] * 2,
        scratch_shapes=[pltpu.VMEM((total, block * width), jnp.float32), pltpu.VMEM((total, rank + total), jnp.float32),
                        pltpu.VMEM((total, total), jnp.float32)],
        compiler_params=params(14),
        name="products",
    )(index, in_hbm(high), in_hbm(low), *pieces)


def split_kernel(index_ref, keep_ref, got_ref, *outs):
    rows = outs[0].shape[0]
    for k, out in enumerate(outs):
        at = pl.ds(pl.multiple_of((index_ref[2] ^ k) * rows, rows), rows)
        out[...] = keep_ref[at, :] + got_ref[at, :]


def split(index, keep, got, chips):
    rows, cols = keep.shape
    return pl.pallas_call(
        split_kernel,
        in_specs=[SCALARS] + [pl.BlockSpec(memory_space=pltpu.VMEM)] * 2,
        out_shape=[shape(rows // chips, cols)] * chips,
        compiler_params=params(4),
        name="split",
    )(index, keep, got)


def tree_sum(values):
    while len(values) > 1:
        values = [a + b for a, b in zip(values[::2], values[1::2])]
    return values[0]


def ana_sum_by_pairs(value, bits):
    for bit in bits:
        value = value + xor_permute(value, "ana", bit)
    return value


def exchange_chips(pieces, limit):
    found = []
    for k in range(1, len(pieces)):
        piece = pieces[k]
        if k > limit:
            piece, found[k - limit - 1] = lax.optimization_barrier((piece, found[k - limit - 1]))
        found.append(xor_permute(piece, "sim", 2 * k))
    return found


def chip_scatter(index, send, keep, limit):
    chips = lax.axis_size("sim") // 2
    got = xor_permute(send, "sim", 1)
    pieces = split(index, keep, got, chips)
    return tree_sum([pieces[0]] + exchange_chips(pieces, limit))


def ana_sum(value):
    return tree_sum([value] + [xor_permute(value, "ana", k) for k in range(1, lax.axis_size("ana"))])


def chip_gather(value, limit):
    chips = lax.axis_size("sim") // 2
    return jnp.concatenate([value] + exchange_chips([value] * chips, limit), axis=0)


def with_other_core(value):
    return value, xor_permute(value, "sim", 1)


PANEL = 32

def eliminate(work_ref, members, aside):
    tiles = work_ref.shape[1] // 128
    groups = PANEL // 8
    sub = lax.broadcasted_iota(jnp.int32, (8, 128), 0)

    def panel_step(k, carry):
        aside(k)
        start = pl.multiple_of(k * PANEL, PANEL)
        at = pl.multiple_of((k * PANEL) // 128 * 128, 128)
        diag = work_ref[pl.ds(start, PANEL), pl.ds(at, 128)]
        diag = pltpu.roll(diag, (128 - (k * PANEL) % 128) % 128, 1)
        rows = work_ref[pl.ds(start, PANEL), :]
        x = [[rows[8 * g:8 * g + 8, 128 * t:128 * t + 128] for t in range(tiles)] + [diag[8 * g:8 * g + 8]]
             for g in range(groups)]
        for b in range(groups):
            cols = {g: [jnp.broadcast_to(x[g][tiles][:, 8 * b + j:8 * b + j + 1], (8, 128)) for j in range(8)]
                    for g in range(b, groups)}
            pivots = jnp.ones((8, 128), jnp.float32)
            for r in range(8):
                pivot = jnp.broadcast_to(cols[b][r][r:r + 1], (8, 128))
                pivots = jnp.where(sub == r, pivot, pivots)
                inverse = 1.0 / pivot
                raw = [jnp.broadcast_to(v[r:r + 1], (8, 128)) for v in x[b]]
                craw = [jnp.broadcast_to(cols[b][j][r:r + 1], (8, 128)) if j > r else None for j in range(8)]
                for g in range(b, groups):
                    coef = cols[g][r] * inverse
                    if g == b:
                        coef = jnp.where(sub > r, coef, 0.0)
                    x[g] = [v - coef * w for v, w in zip(x[g], raw)]
                    cols[g] = [cols[g][j] - coef * craw[j] if j > r else cols[g][j] for j in range(8)]
            x[b] = [v * lax.rsqrt(pivots) for v in x[b]]
        done = jnp.concatenate([jnp.concatenate(v[:tiles], axis=1) for v in x], axis=0)
        lane = lax.broadcasted_iota(jnp.int32, (PANEL, members), 1)
        lower = jnp.where(lane >= start + PANEL, done[:, :members], 0.0)
        lh, lm, ll = thirds(lower)
        dh, dm, dl = thirds(done)
        left = jnp.concatenate([lh, lh, lm, lh, ll, lm], axis=0)
        right = jnp.concatenate([dh, dm, dh, dl, dh, dm], axis=0)
        work_ref[...] = work_ref[...] - mm(left, right, ((0,), (0,)), None)
        work_ref[pl.ds(start, PANEL), :] = done
        return carry

    lax.fori_loop(0, members // PANEL, panel_step, 0)


def ordered(index_ref, mine_ref, other_ref, out_ref, chips):
    half = mine_ref.shape[0]
    rows = half // chips
    for k in range(chips):
        at = (index_ref[2] ^ k) * rows
        piece = slice(k * rows, (k + 1) * rows)
        out_ref[pl.ds(pl.multiple_of(index_ref[1] * half + at, rows), rows), :] = mine_ref[piece, :]
        out_ref[pl.ds(pl.multiple_of((1 - index_ref[1]) * half + at, rows), rows), :] = other_ref[piece, :]


def solve_kernel(index_ref, sums_ref, sums2_ref, gram_ref, gram2_ref, rot_ref, high_hbm, low_hbm, *rest, count, chips, ranks):
    pieces, rest = rest[:ranks], rest[ranks:]
    mix_high, mix_low, rem_high, rem_low, coords_ref = rest[:5]
    work_ref, all_ref, basis_ref, high_ref, low_ref, snap_ref, sem = rest[5:]
    rank, members = coords_ref.shape
    each = members // ranks
    copies = [pltpu.make_async_copy(high_hbm, high_ref, sem.at[0]), pltpu.make_async_copy(low_hbm, low_ref, sem.at[1])]
    for k, piece in enumerate(pieces):
        at = pl.multiple_of((index_ref[0] ^ index_ref[FIRST + k]) * each, each)
        copies.append(pltpu.make_async_copy(piece, snap_ref.at[:, pl.ds(at, each), :], sem.at[2 + k]))
    for copy in copies:
        copy.start()
    ordered(index_ref, sums_ref, sums2_ref, all_ref, chips)
    ordered(index_ref, gram_ref, gram2_ref, basis_ref, chips)
    row = lax.broadcasted_iota(jnp.int32, (members, members), 0)
    col = lax.broadcasted_iota(jnp.int32, (members, members), 1)
    eye = row == col
    inner = all_ref[:, rank:]
    diag = jnp.where(eye, inner, 0.0)
    across = lax.rsqrt(jnp.sum(diag, axis=0, keepdims=True) / count + EPS)
    along = lax.rsqrt(jnp.sum(diag, axis=1, keepdims=True) / count + EPS)
    coef = all_ref[:, :rank] * (along / count)
    correct = 2.0 * coef - mm(coef, basis_ref[...], ((1,), (0,))) / count
    work_ref[:, :members] = inner * (along / count) * across - mm(correct, coef, ((1,), (1,)))
    work_ref[:, members:] = jnp.where(eye, 1.0, 0.0)
    all_ref[:, :rank] = coef
    for copy in copies:
        copy.wait()
    lines, _, width = snap_ref.shape
    block = lines // (members // PANEL)

    def remainder(k):
        at = pl.ds(pl.multiple_of(k * (block * width), block * width), block * width)
        taken = mm3((high_ref[at, :], low_ref[at, :]), halves(all_ref[:, :rank]), ((1,), (1,)))
        panel = jnp.concatenate([snap_ref[k * block + i].T for i in range(block)], axis=0) * across
        rem_high[at, :], rem_low[at, :] = halves(panel - taken)

    eliminate(work_ref, members, remainder)
    coefs, tops, bottoms = halves(all_ref[:, :rank]), halves(rot_ref[:rank, :]), halves(rot_ref[rank:, :])
    upper = jnp.where(row <= col, work_ref[:, :members], 0.0)
    mix_high[...], mix_low[...] = halves(mm3(halves(work_ref[:, members:]), bottoms, ((0,), (0,))))
    coords = (mm3(coefs, tops, ((1,), (0,))) + mm3(halves(upper), bottoms, ((0,), (0,)))) * math.sqrt(rank)
    coords_ref[...] = coords.T


def solve(index, sums, gram, rotation, high, low, pieces, count, chips):
    rows, rank = high.shape
    members = rotation.shape[0] - rank
    ranks = len(pieces)
    lines, each, width = pieces[0].shape
    half = jnp.bfloat16
    return pl.pallas_call(
        functools.partial(solve_kernel, count=float(count), chips=chips, ranks=ranks),
        in_specs=[SCALARS] + [pl.BlockSpec(memory_space=pltpu.VMEM)] * 5 + [pl.BlockSpec(memory_space=pl.ANY)] * (2 + ranks),
        out_shape=[shape(members, rank, dtype=half)] * 2 + [shape(rows, members, dtype=half)] * 2 + [shape(rank, members)],
        scratch_shapes=[pltpu.VMEM((members, 2 * members), jnp.float32),
                        pltpu.VMEM((members, rank + members), jnp.float32),
                        pltpu.VMEM((rank, rank), jnp.float32),
                        pltpu.VMEM((rows, rank), half), pltpu.VMEM((rows, rank), half),
                        pltpu.VMEM((lines, members, width), jnp.float32), pltpu.SemaphoreType.DMA((2 + ranks,))],
        compiler_params=params(28),
        name="solve",
    )(index, *sums, *gram, rotation, high, low, *pieces)


def rotate_kernel(mix_high, mix_low, rem_high, rem_low, turned_ref, out_ref):
    out = turned_ref[...] + mm3((rem_high[...], rem_low[...]), (mix_high[...], mix_low[...]), ((1,), (0,)))
    out_ref[...] = out.reshape(out_ref.shape)


def rotate(mix, rest, turned, dims):
    lines, width, rank = dims
    members = mix[0].shape[0]
    block = 4
    return pl.pallas_call(
        rotate_kernel,
        grid=(lines // block,),
        in_specs=[pl.BlockSpec((members, rank), lambda i: (0, 0))] * 2 + [pl.BlockSpec((block * width, members), lambda i: (i, 0))] * 2
        + [pl.BlockSpec((block * width, rank), lambda i: (i, 0))],
        out_specs=pl.BlockSpec((block, width, rank), lambda i: (i, 0, 0)),
        out_shape=shape(lines, width, rank),
        compiler_params=params(14),
        name="rotate",
    )(*mix, *rest, in_hbm(turned))


def per_device(initial_disp, initial_vel, stiffness, basis, rotation):
    ranks, sims = lax.axis_size("ana"), lax.axis_size("sim")
    ana, sim = lax.axis_index("ana"), lax.axis_index("sim")
    lines, width, rank = basis.shape
    count = lines * width * sims * ranks
    chips = sims // 2
    core = sim % 2
    near, far = list(range(1, ranks // 2)), list(range(ranks // 2, ranks))
    orders = (near + far[::-1] + [0], far[::-1] + near + [0])
    masks = jnp.where(core == 0, jnp.array(orders[0]), jnp.array(orders[1]))
    first_index = jnp.stack([ana, core, sim // 2])
    index = jnp.concatenate([first_index, masks]).astype(jnp.int32)

    last, first = edges(initial_disp, initial_vel, stiffness)
    up = [(i, i + 1) for i in range(sims - 1)]
    before = lax.ppermute(last, "sim", up)
    after = lax.ppermute(first, "sim", [(j, i) for i, j in up])
    late_disp, late_vel, _ = lax.optimization_barrier((initial_disp, initial_vel, last[0, 0, 0]))
    disp, vel = to_lines(late_disp, late_vel)
    before, after, disp = lax.optimization_barrier((before, after, disp))

    pieces = list(evolve(index, disp, vel, stiffness, before, after, ranks))
    order, pieces = lax.optimization_barrier((index, pieces))
    for slot in range(ranks - 1):
        pairs = [(s * ranks + a, s * ranks + (a ^ orders[s % 2][slot])) for s in range(sims) for a in range(ranks)]
        pieces[slot] = lax.ppermute(pieces[slot], ("sim", "ana"), pairs)

    def meanwhile(_, carry):
        at, *_ = carry
        send, keep, high, low, turned = basis_parts(at, basis, rotation)
        return at + (at >> 20), ana_sum_by_pairs(chip_scatter(at, send, keep, 2), bits[:-1]), high, low, turned

    bits = [2 ** i for i in range(ranks.bit_length() - 1)]
    empty = room(*[shape(lines * width, rank, dtype=t) for t in (jnp.bfloat16, jnp.bfloat16, jnp.float32)])
    order, gram, high, low, turned = lax.fori_loop(
        0, 1 + (ana >> 20), meanwhile, (order, jnp.zeros((rank // sims, rank), jnp.float32), *empty))
    gram = ana_sum_by_pairs(gram, bits[-1:])

    send, keep = products(order, high, low, pieces)
    sums = chip_scatter(order, send, keep, chips)
    sums, gram = lax.optimization_barrier((sums, gram))
    gram = chip_gather(gram, chips)
    sums = ana_sum(sums)
    sums = with_other_core(chip_gather(sums, chips))
    gram = with_other_core(gram)
    *found, coords = solve(index, sums, gram, rotation, high, low, pieces, count, chips)
    return rotate(found[:2], found[2:], turned, basis.shape), coords


def solution(mesh):
    in_specs = (
        P("ana", "sim", None),
        P("ana", "sim", None),
        P("sim", None),
        P(("sim", "ana"), None, None),
        P(),
    )
    out_specs = (P(("sim", "ana"), None, None), P())
    return jax.shard_map(
        per_device, mesh=mesh, in_specs=in_specs, out_specs=out_specs, check_vma=False
    )
```

```python
import functools
import math

import jax
import jax.numpy as jnp
from jax import lax
from jax.experimental import pallas as pl
from jax.experimental.pallas import tpu as pltpu
from jax.sharding import PartitionSpec as P

STEPS = 4
EPS = 1e-06
MIB = 1024 * 1024
HI = lax.Precision.HIGHEST
FIRST = 3
SCALARS = pl.BlockSpec(memory_space=pltpu.SMEM)


def mm(left, right, dims, precision=HI):
    return lax.dot_general(left, right, (dims, ((), ())), precision=precision, preferred_element_type=jnp.float32)


def shape(*dims, dtype=jnp.float32):
    return jax.ShapeDtypeStruct(dims, dtype)


def params(mib):
    return pltpu.CompilerParams(vmem_limit_bytes=mib * MIB)


def in_hbm(value):
    return pltpu.with_memory_space_constraint(value, pltpu.HBM)


def halves(value):
    high = value.astype(jnp.bfloat16)
    return high, (value - high.astype(jnp.float32)).astype(jnp.bfloat16)


def thirds(value):
    high, _ = halves(value)
    rest = value - high.astype(jnp.float32)
    return (high,) + halves(rest)


def mm3(left, right, dims):
    (lh, ll), (rh, rl) = left, right
    (over,), (under,) = dims
    return mm(jnp.concatenate([ll, lh, lh], axis=over), jnp.concatenate([rh, rl, rh], axis=under), dims, None)


def xor_permute(value, axis, mask):
    size = lax.axis_size(axis)
    return lax.ppermute(value, axis, [(i, i ^ mask) for i in range(size)])


def edges_kernel(stiff_ref, disp_low, vel_low, disp_high, vel_high, last_ref, first_ref):
    w = STEPS
    lines = stiff_ref.shape[0]
    for ref, disp, vel, at, start in ((last_ref, disp_high, vel_high, 8 - w, lines - w), (first_ref, disp_low, vel_low, 0, 0)):
        for i in range(w):
            ref[i] = disp[:, at + i, :]
            ref[w + i] = vel[:, at + i, :]
        ref[2 * w] = jnp.zeros_like(ref[2 * w])
        ref[2 * w, :w, :] = stiff_ref[start:start + w, :]


def edges(disp, vel, stiff):
    members, lines, width = disp.shape
    w = STEPS
    low = pl.BlockSpec((members, 8, width), lambda i: (0, 0, 0))
    high = pl.BlockSpec((members, 8, width), lambda i: (0, lines // 8 - 1, 0))
    edge = pl.BlockSpec((2 * w + 1, members, width), lambda i: (0, 0, 0))
    return pl.pallas_call(
        edges_kernel,
        grid=(1,),
        in_specs=[pl.BlockSpec((lines, width), lambda i: (0, 0)), low, low, high, high],
        out_specs=[edge, edge],
        out_shape=[pltpu.HBM((2 * w + 1, members, width), jnp.float32)] * 2,
        compiler_params=params(6),
        name="edges",
    )(in_hbm(stiff), in_hbm(disp), in_hbm(vel), in_hbm(disp), in_hbm(vel))


def to_lines_kernel(disp_ref, vel_ref, disp_out, vel_out):
    lines, group, _ = disp_out.shape
    for line in range(lines):
        disp_out[line] = disp_ref[pl.ds(line, group, stride=lines), :]
        vel_out[line] = vel_ref[pl.ds(line, group, stride=lines), :]


def to_lines(disp, vel):
    members, lines, width = disp.shape
    group = 16
    flat = pl.BlockSpec((group * lines, width), lambda i: (i, 0))
    out = pl.BlockSpec((lines, group, width), lambda i: (0, i, 0))
    return pl.pallas_call(
        to_lines_kernel,
        grid=(members // group,),
        in_specs=[flat, flat],
        out_specs=[out, out],
        out_shape=[shape(lines, members, width)] * 2,
        compiler_params=params(8),
        name="to_lines",
    )(in_hbm(disp.reshape(members * lines, width)), in_hbm(vel.reshape(members * lines, width)))


def evolve_kernel(index_ref, disp_ref, vel_ref, stiff_ref, before_ref, after_ref, *rest, slots):
    outs, (even_ref, odd_ref, speed_ref, pad_ref, all_ref, sem) = rest[:slots], rest[slots:]
    lines, members, width = disp_ref.shape
    w = STEPS
    full = lines + 2 * w
    size = lines // slots
    lane = lax.broadcasted_iota(jnp.int32, (8, width), 1)
    pad_ref[w:2 * w, :] = before_ref[2 * w, :w, :]
    pad_ref[8:8 + lines, :] = stiff_ref[...]
    pad_ref[8 + lines:8 + lines + w, :] = after_ref[2 * w, :w, :]

    def group_step(g, carry):
        at = pl.ds(pl.multiple_of(g * 8, 8), 8)
        for i in range(w):
            even_ref[i], speed_ref[i] = before_ref[i, at, :], before_ref[w + i, at, :]
            even_ref[w + lines + i], speed_ref[w + lines + i] = after_ref[i, at, :], after_ref[w + i, at, :]
        for i in range(lines):
            even_ref[w + i], speed_ref[w + i] = disp_ref[i, at, :], vel_ref[i, at, :]
        now, then = even_ref, odd_ref
        for step in range(1, w + 1):
            for i in range(step, full - step):
                u = now[i]
                right = jnp.where(lane == width - 1, 0.0, pltpu.roll(u, width - 1, 1))
                left = jnp.where(lane == 0, 0.0, pltpu.roll(u, 1, 1))
                around = (now[i + 1] + now[i - 1]) + (right + left)
                stiff = jnp.broadcast_to(pad_ref[8 - w + i:8 - w + i + 1, :], (8, width))
                speed = speed_ref[i] + stiff * (around + u * (0.5 / (1.0 + u * u) - 4.5))
                if step < w:
                    then[i], speed_ref[i] = u + speed, speed
                else:
                    all_ref[i - w, at, :] = u + speed
            now, then = then, now
        for slot, out in enumerate(outs):
            pltpu.make_async_copy(all_ref.at[block(slot), at], out.at[:, at], sem.at[slot]).start()
        return carry

    def block(slot):
        return pl.ds((index_ref[0] ^ index_ref[FIRST + slot]) * size, size)

    lax.fori_loop(0, members // 8, group_step, 0)
    for slot, out in enumerate(outs):
        pltpu.make_async_copy(all_ref.at[block(slot)], out, sem.at[slot]).wait()


def evolve(index, disp, vel, stiff, before, after, slots):
    lines, members, width = disp.shape
    line = pltpu.VMEM((lines + 2 * STEPS, 8, width), jnp.float32)
    return pl.pallas_call(
        functools.partial(evolve_kernel, slots=slots),
        in_specs=[SCALARS] + [pl.BlockSpec(memory_space=pltpu.VMEM)] * 5,
        out_shape=[pltpu.HBM((lines // slots, members, width), jnp.float32)] * slots,
        out_specs=[pl.BlockSpec(memory_space=pltpu.HBM)] * slots,
        scratch_shapes=[line, line, line, pltpu.VMEM((lines + 16, width), jnp.float32),
                        pltpu.VMEM((lines, members, width), jnp.float32), pltpu.SemaphoreType.DMA((slots,))],
        compiler_params=params(8),
        name="evolve",
    )(index, disp, vel, stiff, before, after)


def room(*arrays):
    return pl.pallas_call(
        lambda *refs: None,
        out_specs=[pl.BlockSpec(memory_space=pl.ANY)] * len(arrays),
        out_shape=[pltpu.HBM(a.shape, a.dtype) for a in arrays],
        name="room",
    )()


def basis_kernel(index_ref, rot_ref, basis_ref, send_ref, keep_ref, high_ref, low_ref, turned_ref, sum_ref, mixed_ref):
    lines, width, rank = basis_ref.shape
    step = pl.program_id(0)

    @pl.when(step == 0)
    def _():
        sum_ref[...] = jnp.zeros_like(sum_ref)
        mixed_ref[...] = jnp.zeros_like(mixed_ref)

    high, low = halves(basis_ref[...].reshape(lines * width, rank))
    high_ref[...] = high
    low_ref[...] = low
    sum_ref[...] += mm(high, high, ((0,), (0,)), None)
    mixed_ref[...] += mm(high, low, ((0,), (0,)), None)
    turned_ref[...] = mm3((high, low), halves(rot_ref[...]), ((1,), (0,)))

    @pl.when(step == pl.num_programs(0) - 1)
    def _():
        sum_ref[...] += mixed_ref[...] + mixed_ref[...].T
        half = keep_ref.shape[0]
        core = index_ref[1]
        keep_ref[...] = sum_ref[pl.ds(pl.multiple_of(core * half, half), half), :]
        send_ref[...] = sum_ref[pl.ds(pl.multiple_of((1 - core) * half, half), half), :]


def basis_parts(index, basis, rotation):
    lines, width, rank = basis.shape
    block = 4
    half = pl.BlockSpec((rank // 2, rank), lambda i: (0, 0))
    rows = pl.BlockSpec((block * width, rank), lambda i: (i, 0))
    return pl.pallas_call(
        basis_kernel,
        grid=(lines // block,),
        in_specs=[SCALARS, pl.BlockSpec((rank, rank), lambda i: (0, 0)), pl.BlockSpec((block, width, rank), lambda i: (i, 0, 0))],
        out_specs=[half, half, rows, rows, rows],
        out_shape=[shape(rank // 2, rank)] * 2 + [pltpu.HBM((lines * width, rank), jnp.bfloat16)] * 2
        + [pltpu.HBM((lines * width, rank), jnp.float32)],
        scratch_shapes=[pltpu.VMEM((rank, rank), jnp.float32)] * 2,
        compiler_params=params(24),
        name="basis_parts",
    )(index, in_hbm(rotation), in_hbm(basis))


def products_kernel(index_ref, high_ref, low_ref, *rest):
    pieces, (send_ref, keep_ref, snap_ref, sum_ref, mixed_ref) = rest[:-5], rest[-5:]
    lines, members, width = pieces[0].shape
    rank = high_ref.shape[-1]
    step = pl.program_id(0)
    for k, piece in enumerate(pieces):
        at = pl.multiple_of((index_ref[0] ^ index_ref[FIRST + k]) * members, members)
        for line in range(lines):
            snap_ref[pl.ds(at, members), line * width:(line + 1) * width] = piece[line]

    @pl.when(step == 0)
    def _():
        sum_ref[...] = jnp.zeros_like(sum_ref)
        mixed_ref[...] = jnp.zeros_like(mixed_ref)

    snap = halves(snap_ref[...])
    sum_ref[:, :rank] += mm3(snap, (high_ref[...], low_ref[...]), ((1,), (0,)))
    sum_ref[:, rank:] += mm(snap[0], snap[0], ((1,), (1,)), None)
    mixed_ref[...] += mm(snap[0], snap[1], ((1,), (1,)), None)

    @pl.when(step == pl.num_programs(0) - 1)
    def _():
        sum_ref[:, rank:] += mixed_ref[...] + mixed_ref[...].T
        half = keep_ref.shape[0]
        core = index_ref[1]
        keep_ref[...] = sum_ref[pl.ds(pl.multiple_of(core * half, half), half), :]
        send_ref[...] = sum_ref[pl.ds(pl.multiple_of((1 - core) * half, half), half), :]


def products(index, high, low, pieces):
    rank = high.shape[1]
    lines, members, width = pieces[0].shape
    total = members * len(pieces)
    block = 4
    half = pl.BlockSpec((total // 2, rank + total), lambda i: (0, 0))
    return pl.pallas_call(
        products_kernel,
        grid=(lines // block,),
        in_specs=[SCALARS] + [pl.BlockSpec((block * width, rank), lambda i: (i, 0))] * 2
        + [pl.BlockSpec((block, members, width), lambda i: (i, 0, 0))] * len(pieces),
        out_specs=[half, half],
        out_shape=[shape(total // 2, rank + total)] * 2,
        scratch_shapes=[pltpu.VMEM((total, block * width), jnp.float32), pltpu.VMEM((total, rank + total), jnp.float32),
                        pltpu.VMEM((total, total), jnp.float32)],
        compiler_params=params(14),
        name="products",
    )(index, in_hbm(high), in_hbm(low), *pieces)


def split_kernel(index_ref, keep_ref, got_ref, *outs):
    rows = outs[0].shape[0]
    for k, out in enumerate(outs):
        at = pl.ds(pl.multiple_of((index_ref[2] ^ k) * rows, rows), rows)
        out[...] = keep_ref[at, :] + got_ref[at, :]


def split(index, keep, got, chips):
    rows, cols = keep.shape
    return pl.pallas_call(
        split_kernel,
        in_specs=[SCALARS] + [pl.BlockSpec(memory_space=pltpu.VMEM)] * 2,
        out_shape=[shape(rows // chips, cols)] * chips,
        compiler_params=params(4),
        name="split",
    )(index, keep, got)


def tree_sum(values):
    while len(values) > 1:
        values = [a + b for a, b in zip(values[::2], values[1::2])]
    return values[0]


def ana_sum_by_pairs(value, bits):
    for bit in bits:
        value = value + xor_permute(value, "ana", bit)
    return value


def exchange_chips(pieces, limit):
    found = []
    for k in range(1, len(pieces)):
        piece = pieces[k]
        if k > limit:
            piece, found[k - limit - 1] = lax.optimization_barrier((piece, found[k - limit - 1]))
        found.append(xor_permute(piece, "sim", 2 * k))
    return found


def chip_scatter(index, send, keep, limit):
    chips = lax.axis_size("sim") // 2
    got = xor_permute(send, "sim", 1)
    pieces = split(index, keep, got, chips)
    return tree_sum([pieces[0]] + exchange_chips(pieces, limit))


def ana_sum(value):
    return tree_sum([value] + [xor_permute(value, "ana", k) for k in range(1, lax.axis_size("ana"))])


def chip_gather(value, limit):
    chips = lax.axis_size("sim") // 2
    return jnp.concatenate([value] + exchange_chips([value] * chips, limit), axis=0)


def with_other_core(value):
    return value, xor_permute(value, "sim", 1)


PANEL = 32

def eliminate(work_ref, members, aside):
    tiles = work_ref.shape[1] // 128
    groups = PANEL // 8
    sub = lax.broadcasted_iota(jnp.int32, (8, 128), 0)

    def panel_step(k, carry):
        aside(k)
        start = pl.multiple_of(k * PANEL, PANEL)
        at = pl.multiple_of((k * PANEL) // 128 * 128, 128)
        diag = work_ref[pl.ds(start, PANEL), pl.ds(at, 128)]
        diag = pltpu.roll(diag, (128 - (k * PANEL) % 128) % 128, 1)
        rows = work_ref[pl.ds(start, PANEL), :]
        x = [[rows[8 * g:8 * g + 8, 128 * t:128 * t + 128] for t in range(tiles)] + [diag[8 * g:8 * g + 8]]
             for g in range(groups)]
        for b in range(groups):
            cols = {g: [jnp.broadcast_to(x[g][tiles][:, 8 * b + j:8 * b + j + 1], (8, 128)) for j in range(8)]
                    for g in range(b, groups)}
            pivots = jnp.ones((8, 128), jnp.float32)
            for r in range(8):
                pivot = jnp.broadcast_to(cols[b][r][r:r + 1], (8, 128))
                pivots = jnp.where(sub == r, pivot, pivots)
                inverse = 1.0 / pivot
                raw = [jnp.broadcast_to(v[r:r + 1], (8, 128)) for v in x[b]]
                craw = [jnp.broadcast_to(cols[b][j][r:r + 1], (8, 128)) if j > r else None for j in range(8)]
                for g in range(b, groups):
                    coef = cols[g][r] * inverse
                    if g == b:
                        coef = jnp.where(sub > r, coef, 0.0)
                    x[g] = [v - coef * w for v, w in zip(x[g], raw)]
                    cols[g] = [cols[g][j] - coef * craw[j] if j > r else cols[g][j] for j in range(8)]
            x[b] = [v * lax.rsqrt(pivots) for v in x[b]]
        done = jnp.concatenate([jnp.concatenate(v[:tiles], axis=1) for v in x], axis=0)
        lane = lax.broadcasted_iota(jnp.int32, (PANEL, members), 1)
        lower = jnp.where(lane >= start + PANEL, done[:, :members], 0.0)
        lh, lm, ll = thirds(lower)
        dh, dm, dl = thirds(done)
        left = jnp.concatenate([lh, lh, lm, lh, ll, lm], axis=0)
        right = jnp.concatenate([dh, dm, dh, dl, dh, dm], axis=0)
        work_ref[...] = work_ref[...] - mm(left, right, ((0,), (0,)), None)
        work_ref[pl.ds(start, PANEL), :] = done
        return carry

    lax.fori_loop(0, members // PANEL, panel_step, 0)


def ordered(index_ref, mine_ref, other_ref, out_ref, chips):
    half = mine_ref.shape[0]
    rows = half // chips
    for k in range(chips):
        at = (index_ref[2] ^ k) * rows
        piece = slice(k * rows, (k + 1) * rows)
        out_ref[pl.ds(pl.multiple_of(index_ref[1] * half + at, rows), rows), :] = mine_ref[piece, :]
        out_ref[pl.ds(pl.multiple_of((1 - index_ref[1]) * half + at, rows), rows), :] = other_ref[piece, :]


def solve_kernel(index_ref, sums_ref, sums2_ref, gram_ref, gram2_ref, rot_ref, high_hbm, low_hbm, turned_hbm, *rest, count, chips, ranks):
    pieces, rest = rest[:ranks], rest[ranks:]
    out_hbm, coords_ref, work_ref, all_ref, basis_ref, high_ref, low_ref, snap_ref, rem_high, rem_low, out_ref, sem, out_sem = rest
    rank, members = coords_ref.shape
    each = members // ranks
    copies = [pltpu.make_async_copy(high_hbm, high_ref, sem.at[0]), pltpu.make_async_copy(low_hbm, low_ref, sem.at[1])]
    for k, piece in enumerate(pieces):
        at = pl.multiple_of((index_ref[0] ^ index_ref[FIRST + k]) * each, each)
        copies.append(pltpu.make_async_copy(piece, snap_ref.at[:, pl.ds(at, each), :], sem.at[2 + k]))
    turned = pltpu.make_async_copy(turned_hbm, out_ref, out_sem)
    for copy in copies + [turned]:
        copy.start()
    ordered(index_ref, sums_ref, sums2_ref, all_ref, chips)
    ordered(index_ref, gram_ref, gram2_ref, basis_ref, chips)
    row = lax.broadcasted_iota(jnp.int32, (members, members), 0)
    col = lax.broadcasted_iota(jnp.int32, (members, members), 1)
    eye = row == col
    inner = all_ref[:, rank:]
    diag = jnp.where(eye, inner, 0.0)
    across = lax.rsqrt(jnp.sum(diag, axis=0, keepdims=True) / count + EPS)
    along = lax.rsqrt(jnp.sum(diag, axis=1, keepdims=True) / count + EPS)
    coef = all_ref[:, :rank] * (along / count)
    correct = 2.0 * coef - mm(coef, basis_ref[...], ((1,), (0,))) / count
    work_ref[:, :members] = inner * (along / count) * across - mm(correct, coef, ((1,), (1,)))
    work_ref[:, members:] = jnp.where(eye, 1.0, 0.0)
    all_ref[:, :rank] = coef
    for copy in copies:
        copy.wait()
    lines, _, width = snap_ref.shape
    block = lines // (members // PANEL)

    def remainder(k):
        at = pl.ds(pl.multiple_of(k * (block * width), block * width), block * width)
        taken = mm3((high_ref[at, :], low_ref[at, :]), halves(all_ref[:, :rank]), ((1,), (1,)))
        panel = jnp.concatenate([snap_ref[k * block + i].T for i in range(block)], axis=0) * across
        rem_high[at, :], rem_low[at, :] = halves(panel - taken)

    eliminate(work_ref, members, remainder)
    coefs, tops, bottoms = halves(all_ref[:, :rank]), halves(rot_ref[:rank, :]), halves(rot_ref[rank:, :])
    mix_high, mix_low = halves(mm3(halves(work_ref[:, members:]), bottoms, ((0,), (0,))))
    turned.wait()
    step = 2 * block
    for first in range(0, lines, step):
        at = slice(first * width, (first + step) * width)
        done = mm3((rem_high[at, :], rem_low[at, :]), (mix_high, mix_low), ((1,), (0,)))
        out_ref[first:first + step] += done.reshape(step, width, rank)
        pltpu.make_async_copy(out_ref.at[pl.ds(first, step)], out_hbm.at[pl.ds(first, step)], out_sem).start()
    upper = jnp.where(row <= col, work_ref[:, :members], 0.0)
    coords = (mm3(coefs, tops, ((1,), (0,))) + mm3(halves(upper), bottoms, ((0,), (0,)))) * math.sqrt(rank)
    coords_ref[...] = coords.T
    pltpu.make_async_copy(out_ref, out_hbm, out_sem).wait()


def solve(index, sums, gram, rotation, high, low, turned, pieces, count, chips):
    rows, rank = high.shape
    members = rotation.shape[0] - rank
    ranks = len(pieces)
    lines, each, width = pieces[0].shape
    half = jnp.bfloat16
    return pl.pallas_call(
        functools.partial(solve_kernel, count=float(count), chips=chips, ranks=ranks),
        in_specs=[SCALARS] + [pl.BlockSpec(memory_space=pltpu.VMEM)] * 5 + [pl.BlockSpec(memory_space=pl.ANY)] * (3 + ranks),
        out_specs=[pl.BlockSpec(memory_space=pltpu.HBM), pl.BlockSpec(memory_space=pltpu.VMEM)],
        out_shape=[pltpu.HBM((lines, width, rank), jnp.float32), shape(rank, members)],
        scratch_shapes=[pltpu.VMEM((members, 2 * members), jnp.float32),
                        pltpu.VMEM((members, rank + members), jnp.float32),
                        pltpu.VMEM((rank, rank), jnp.float32),
                        pltpu.VMEM((rows, rank), half), pltpu.VMEM((rows, rank), half),
                        pltpu.VMEM((lines, members, width), jnp.float32),
                        pltpu.VMEM((rows, members), half), pltpu.VMEM((rows, members), half),
                        pltpu.VMEM((lines, width, rank), jnp.float32),
                        pltpu.SemaphoreType.DMA((2 + ranks,)), pltpu.SemaphoreType.DMA],
        compiler_params=params(36),
        name="solve",
    )(index, *sums, *gram, rotation, high, low, in_hbm(turned.reshape(lines, width, rank)), *pieces)


def per_device(initial_disp, initial_vel, stiffness, basis, rotation):
    ranks, sims = lax.axis_size("ana"), lax.axis_size("sim")
    ana, sim = lax.axis_index("ana"), lax.axis_index("sim")
    lines, width, rank = basis.shape
    count = lines * width * sims * ranks
    chips = sims // 2
    core = sim % 2
    near, far = list(range(1, ranks // 2)), list(range(ranks // 2, ranks))
    orders = (near + far[::-1] + [0], far[::-1] + near + [0])
    masks = jnp.where(core == 0, jnp.array(orders[0]), jnp.array(orders[1]))
    first_index = jnp.stack([ana, core, sim // 2])
    index = jnp.concatenate([first_index, masks]).astype(jnp.int32)

    last, first = edges(initial_disp, initial_vel, stiffness)
    up = [(i, i + 1) for i in range(sims - 1)]
    before = lax.ppermute(last, "sim", up)
    after = lax.ppermute(first, "sim", [(j, i) for i, j in up])
    late_disp, late_vel, _ = lax.optimization_barrier((initial_disp, initial_vel, last[0, 0, 0]))
    disp, vel = to_lines(late_disp, late_vel)
    before, after, disp = lax.optimization_barrier((before, after, disp))

    pieces = list(evolve(index, disp, vel, stiffness, before, after, ranks))
    order, pieces = lax.optimization_barrier((index, pieces))
    for slot in range(ranks - 1):
        pairs = [(s * ranks + a, s * ranks + (a ^ orders[s % 2][slot])) for s in range(sims) for a in range(ranks)]
        pieces[slot] = lax.ppermute(pieces[slot], ("sim", "ana"), pairs)

    def meanwhile(_, carry):
        at, *_ = carry
        send, keep, high, low, turned = basis_parts(at, basis, rotation)
        return at + (at >> 20), ana_sum_by_pairs(chip_scatter(at, send, keep, 2), bits[:-1]), high, low, turned

    bits = [2 ** i for i in range(ranks.bit_length() - 1)]
    empty = room(*[shape(lines * width, rank, dtype=t) for t in (jnp.bfloat16, jnp.bfloat16, jnp.float32)])
    order, gram, high, low, turned = lax.fori_loop(
        0, 1 + (ana >> 20), meanwhile, (order, jnp.zeros((rank // sims, rank), jnp.float32), *empty))
    gram = ana_sum_by_pairs(gram, bits[-1:])

    send, keep = products(order, high, low, pieces)
    sums = chip_scatter(order, send, keep, chips)
    sums, gram = lax.optimization_barrier((sums, gram))
    gram = chip_gather(gram, chips)
    sums = ana_sum(sums)
    sums = with_other_core(chip_gather(sums, chips))
    gram = with_other_core(gram)
    return tuple(solve(index, sums, gram, rotation, high, low, turned, pieces, count, chips))


def solution(mesh):
    in_specs = (
        P("ana", "sim", None),
        P("ana", "sim", None),
        P("sim", None),
        P(("sim", "ana"), None, None),
        P(),
    )
    out_specs = (P(("sim", "ana"), None, None), P())
    return jax.shard_map(
        per_device, mesh=mesh, in_specs=in_specs, out_specs=out_specs, check_vma=False
    )
```

```python
import functools
import math

import jax
import jax.numpy as jnp
from jax import lax
from jax.experimental import pallas as pl
from jax.experimental.pallas import tpu as pltpu
from jax.sharding import PartitionSpec as P

STEPS = 4
EPS = 1e-06
MIB = 1024 * 1024
HI = lax.Precision.HIGHEST
FIRST = 3
SCALARS = pl.BlockSpec(memory_space=pltpu.SMEM)


def mm(left, right, dims, precision=HI):
    return lax.dot_general(left, right, (dims, ((), ())), precision=precision, preferred_element_type=jnp.float32)


def shape(*dims, dtype=jnp.float32):
    return jax.ShapeDtypeStruct(dims, dtype)


def params(mib):
    return pltpu.CompilerParams(vmem_limit_bytes=mib * MIB)


def in_hbm(value):
    return pltpu.with_memory_space_constraint(value, pltpu.HBM)


def halves(value):
    high = value.astype(jnp.bfloat16)
    return high, (value - high.astype(jnp.float32)).astype(jnp.bfloat16)


def thirds(value):
    high, _ = halves(value)
    rest = value - high.astype(jnp.float32)
    return (high,) + halves(rest)


def mm3(left, right, dims):
    (lh, ll), (rh, rl) = left, right
    (over,), (under,) = dims
    return mm(jnp.concatenate([ll, lh, lh], axis=over), jnp.concatenate([rh, rl, rh], axis=under), dims, None)


def xor_permute(value, axis, mask):
    size = lax.axis_size(axis)
    return lax.ppermute(value, axis, [(i, i ^ mask) for i in range(size)])


def edges_kernel(stiff_ref, disp_low, vel_low, disp_high, vel_high, last_ref, first_ref):
    w = STEPS
    lines = stiff_ref.shape[0]
    for ref, disp, vel, at, start in ((last_ref, disp_high, vel_high, 8 - w, lines - w), (first_ref, disp_low, vel_low, 0, 0)):
        for i in range(w):
            ref[i] = disp[:, at + i, :]
            ref[w + i] = vel[:, at + i, :]
        ref[2 * w] = jnp.zeros_like(ref[2 * w])
        ref[2 * w, :w, :] = stiff_ref[start:start + w, :]


def edges(disp, vel, stiff):
    members, lines, width = disp.shape
    w = STEPS
    low = pl.BlockSpec((members, 8, width), lambda i: (0, 0, 0))
    high = pl.BlockSpec((members, 8, width), lambda i: (0, lines // 8 - 1, 0))
    edge = pl.BlockSpec((2 * w + 1, members, width), lambda i: (0, 0, 0))
    return pl.pallas_call(
        edges_kernel,
        grid=(1,),
        in_specs=[pl.BlockSpec((lines, width), lambda i: (0, 0)), low, low, high, high],
        out_specs=[edge, edge],
        out_shape=[pltpu.HBM((2 * w + 1, members, width), jnp.float32)] * 2,
        compiler_params=params(6),
        name="edges",
    )(in_hbm(stiff), in_hbm(disp), in_hbm(vel), in_hbm(disp), in_hbm(vel))


def to_lines_kernel(disp_ref, vel_ref, disp_out, vel_out):
    lines, group, _ = disp_out.shape
    for line in range(lines):
        disp_out[line] = disp_ref[pl.ds(line, group, stride=lines), :]
        vel_out[line] = vel_ref[pl.ds(line, group, stride=lines), :]


def to_lines(disp, vel):
    members, lines, width = disp.shape
    group = 16
    flat = pl.BlockSpec((group * lines, width), lambda i: (i, 0))
    out = pl.BlockSpec((lines, group, width), lambda i: (0, i, 0))
    return pl.pallas_call(
        to_lines_kernel,
        grid=(members // group,),
        in_specs=[flat, flat],
        out_specs=[out, out],
        out_shape=[shape(lines, members, width)] * 2,
        compiler_params=params(8),
        name="to_lines",
    )(in_hbm(disp.reshape(members * lines, width)), in_hbm(vel.reshape(members * lines, width)))


def evolve_kernel(index_ref, disp_ref, vel_ref, stiff_ref, before_ref, after_ref, *rest, slots):
    outs, (even_ref, odd_ref, speed_ref, pad_ref, all_ref, sem) = rest[:slots], rest[slots:]
    lines, members, width = disp_ref.shape
    w = STEPS
    full = lines + 2 * w
    size = lines // slots
    lane = lax.broadcasted_iota(jnp.int32, (8, width), 1)
    pad_ref[w:2 * w, :] = before_ref[2 * w, :w, :]
    pad_ref[8:8 + lines, :] = stiff_ref[...]
    pad_ref[8 + lines:8 + lines + w, :] = after_ref[2 * w, :w, :]

    def group_step(g, carry):
        at = pl.ds(pl.multiple_of(g * 8, 8), 8)
        for i in range(w):
            even_ref[i], speed_ref[i] = before_ref[i, at, :], before_ref[w + i, at, :]
            even_ref[w + lines + i], speed_ref[w + lines + i] = after_ref[i, at, :], after_ref[w + i, at, :]
        for i in range(lines):
            even_ref[w + i], speed_ref[w + i] = disp_ref[i, at, :], vel_ref[i, at, :]
        now, then = even_ref, odd_ref
        for step in range(1, w + 1):
            for i in range(step, full - step):
                u = now[i]
                right = jnp.where(lane == width - 1, 0.0, pltpu.roll(u, width - 1, 1))
                left = jnp.where(lane == 0, 0.0, pltpu.roll(u, 1, 1))
                around = (now[i + 1] + now[i - 1]) + (right + left)
                stiff = jnp.broadcast_to(pad_ref[8 - w + i:8 - w + i + 1, :], (8, width))
                speed = speed_ref[i] + stiff * (around + u * (0.5 / (1.0 + u * u) - 4.5))
                if step < w:
                    then[i], speed_ref[i] = u + speed, speed
                else:
                    all_ref[i - w, at, :] = u + speed
            now, then = then, now
        for slot, out in enumerate(outs):
            pltpu.make_async_copy(all_ref.at[block(slot), at], out.at[:, at], sem.at[slot]).start()
        return carry

    def block(slot):
        return pl.ds((index_ref[0] ^ index_ref[FIRST + slot]) * size, size)

    lax.fori_loop(0, members // 8, group_step, 0)
    for slot, out in enumerate(outs):
        pltpu.make_async_copy(all_ref.at[block(slot)], out, sem.at[slot]).wait()


def evolve(index, disp, vel, stiff, before, after, slots):
    lines, members, width = disp.shape
    line = pltpu.VMEM((lines + 2 * STEPS, 8, width), jnp.float32)
    return pl.pallas_call(
        functools.partial(evolve_kernel, slots=slots),
        in_specs=[SCALARS] + [pl.BlockSpec(memory_space=pltpu.VMEM)] * 5,
        out_shape=[pltpu.HBM((lines // slots, members, width), jnp.float32)] * slots,
        out_specs=[pl.BlockSpec(memory_space=pltpu.HBM)] * slots,
        scratch_shapes=[line, line, line, pltpu.VMEM((lines + 16, width), jnp.float32),
                        pltpu.VMEM((lines, members, width), jnp.float32), pltpu.SemaphoreType.DMA((slots,))],
        compiler_params=params(8),
        name="evolve",
    )(index, disp, vel, stiff, before, after)


def room(*arrays):
    return pl.pallas_call(
        lambda *refs: None,
        out_specs=[pl.BlockSpec(memory_space=pl.ANY)] * len(arrays),
        out_shape=[pltpu.HBM(a.shape, a.dtype) for a in arrays],
        name="room",
    )()


def basis_kernel(index_ref, rot_ref, basis_ref, send_ref, keep_ref, high_ref, low_ref, turned_ref, sum_ref, mixed_ref):
    lines, width, rank = basis_ref.shape
    step = pl.program_id(0)

    @pl.when(step == 0)
    def _():
        sum_ref[...] = jnp.zeros_like(sum_ref)
        mixed_ref[...] = jnp.zeros_like(mixed_ref)

    high, low = halves(basis_ref[...].reshape(lines * width, rank))
    high_ref[...] = high
    low_ref[...] = low
    sum_ref[...] += mm(high, high, ((0,), (0,)), None)
    mixed_ref[...] += mm(high, low, ((0,), (0,)), None)
    turned_ref[...] = mm3((high, low), halves(rot_ref[...]), ((1,), (0,)))

    @pl.when(step == pl.num_programs(0) - 1)
    def _():
        sum_ref[...] += mixed_ref[...] + mixed_ref[...].T
        half = keep_ref.shape[0]
        core = index_ref[1]
        keep_ref[...] = sum_ref[pl.ds(pl.multiple_of(core * half, half), half), :]
        send_ref[...] = sum_ref[pl.ds(pl.multiple_of((1 - core) * half, half), half), :]


def basis_parts(index, basis, rotation):
    lines, width, rank = basis.shape
    block = 4
    half = pl.BlockSpec((rank // 2, rank), lambda i: (0, 0))
    rows = pl.BlockSpec((block * width, rank), lambda i: (i, 0))
    return pl.pallas_call(
        basis_kernel,
        grid=(lines // block,),
        in_specs=[SCALARS, pl.BlockSpec((rank, rank), lambda i: (0, 0)), pl.BlockSpec((block, width, rank), lambda i: (i, 0, 0))],
        out_specs=[half, half, rows, rows, rows],
        out_shape=[shape(rank // 2, rank)] * 2 + [pltpu.HBM((lines * width, rank), jnp.bfloat16)] * 2
        + [pltpu.HBM((lines * width, rank), jnp.float32)],
        scratch_shapes=[pltpu.VMEM((rank, rank), jnp.float32)] * 2,
        compiler_params=params(24),
        name="basis_parts",
    )(index, in_hbm(rotation), in_hbm(basis))


CHUNKS = 4


def products_of(high_ref, low_ref, snap_high, snap_low, start, out_ref, waits):
    rows, rank = out_ref.shape[0], high_ref.shape[1]
    at = pl.ds(pl.multiple_of(start, rows), rows)
    high, low = snap_high[at, :], snap_low[at, :]
    across = ((1,), (1,))
    mixed = mm(high, snap_low[...], across, None) + mm(low, snap_high[...], across, None)
    out_ref[:, rank:] = mm(high, snap_high[...], across, None) + mixed
    along = ((1,), (0,))
    size = high_ref.shape[0] // CHUNKS
    for c in range(CHUNKS):
        cells = slice(c * size, (c + 1) * size)
        for wait in waits:
            wait(c)
        mixed = mm(high[:, cells], low_ref[cells, :], along, None) + mm(low[:, cells], high_ref[cells, :], along, None)
        part = mm(high[:, cells], high_ref[cells, :], along, None) + mixed
        out_ref[:, :rank] = part if c == 0 else out_ref[:, :rank] + part


def send_products_kernel(index_ref, high_hbm, low_hbm, *rest):
    pieces, (send_ref, snap_high, snap_low, high_ref, low_ref, sem) = rest[:-6], rest[-6:]
    lines, members, width = pieces[0].shape
    size = high_ref.shape[0] // CHUNKS

    def fetch(which, c):
        source, target = ((high_hbm, high_ref), (low_hbm, low_ref))[which]
        cells = pl.ds(c * size, size)
        return pltpu.make_async_copy(source.at[cells], target.at[cells], sem.at[which, c])

    for c in range(CHUNKS):
        fetch(0, c).start()
        fetch(1, c).start()
    for k, piece in enumerate(pieces):
        at = pl.ds(pl.multiple_of((index_ref[0] ^ index_ref[FIRST + k]) * members, members), members)
        for line in range(lines):
            cols = slice(line * width, (line + 1) * width)
            snap_high[at, cols], snap_low[at, cols] = halves(piece[line])
    start = (1 - index_ref[1]) * send_ref.shape[0]
    waits = [lambda c: fetch(0, c).wait(), lambda c: fetch(1, c).wait()]
    products_of(high_ref, low_ref, snap_high, snap_low, start, send_ref, waits)


def keep_products_kernel(index_ref, high_ref, low_ref, snap_high, snap_low, keep_ref):
    products_of(high_ref, low_ref, snap_high, snap_low, index_ref[1] * keep_ref.shape[0], keep_ref, [])


def products(index, high, low, pieces):
    rows, rank = high.shape
    total = pieces[0].shape[1] * len(pieces)
    vmem = pl.BlockSpec(memory_space=pltpu.VMEM)
    half = shape(total // 2, rank + total)
    send, *snap = pl.pallas_call(
        send_products_kernel,
        in_specs=[SCALARS] + [pl.BlockSpec(memory_space=pl.ANY)] * 2 + [vmem] * len(pieces),
        out_shape=[half] + [shape(total, rows, dtype=jnp.bfloat16)] * 2,
        scratch_shapes=[pltpu.VMEM(high.shape, jnp.bfloat16)] * 2 + [pltpu.SemaphoreType.DMA((2, CHUNKS))],
        compiler_params=params(16),
        name="send_products",
    )(index, in_hbm(high), in_hbm(low), *pieces)
    keep = pl.pallas_call(
        keep_products_kernel,
        in_specs=[SCALARS] + [vmem] * 4,
        out_shape=half,
        compiler_params=params(12),
        name="keep_products",
    )(index, high, low, *snap)
    return send, keep


def split_kernel(index_ref, keep_ref, got_ref, *outs):
    rows = outs[0].shape[0]
    for k, out in enumerate(outs):
        at = pl.ds(pl.multiple_of((index_ref[2] ^ k) * rows, rows), rows)
        out[...] = keep_ref[at, :] + got_ref[at, :]


def split(index, keep, got, chips):
    rows, cols = keep.shape
    return pl.pallas_call(
        split_kernel,
        in_specs=[SCALARS] + [pl.BlockSpec(memory_space=pltpu.VMEM)] * 2,
        out_shape=[shape(rows // chips, cols)] * chips,
        compiler_params=params(4),
        name="split",
    )(index, keep, got)


def tree_sum(values):
    while len(values) > 1:
        values = [a + b for a, b in zip(values[::2], values[1::2])]
    return values[0]


def ana_sum_by_pairs(value, bits):
    for bit in bits:
        value = value + xor_permute(value, "ana", bit)
    return value


def exchange_chips(pieces, limit):
    found = []
    for k in range(1, len(pieces)):
        piece = pieces[k]
        if k > limit:
            piece, found[k - limit - 1] = lax.optimization_barrier((piece, found[k - limit - 1]))
        found.append(xor_permute(piece, "sim", 2 * k))
    return found


def chip_scatter(index, send, keep, limit):
    chips = lax.axis_size("sim") // 2
    got = xor_permute(send, "sim", 1)
    pieces = split(index, keep, got, chips)
    return tree_sum([pieces[0]] + exchange_chips(pieces, limit))


def ana_sum(value):
    return tree_sum([value] + [xor_permute(value, "ana", k) for k in range(1, lax.axis_size("ana"))])


def chip_gather(value, limit):
    chips = lax.axis_size("sim") // 2
    return jnp.concatenate([value] + exchange_chips([value] * chips, limit), axis=0)


def with_other_core(value):
    return value, xor_permute(value, "sim", 1)


PANEL = 32

def eliminate(work_ref, members, aside):
    tiles = work_ref.shape[1] // 128
    groups = PANEL // 8
    sub = lax.broadcasted_iota(jnp.int32, (8, 128), 0)

    def panel_step(k, carry):
        aside(k)
        start = pl.multiple_of(k * PANEL, PANEL)
        at = pl.multiple_of((k * PANEL) // 128 * 128, 128)
        diag = work_ref[pl.ds(start, PANEL), pl.ds(at, 128)]
        diag = pltpu.roll(diag, (128 - (k * PANEL) % 128) % 128, 1)
        rows = work_ref[pl.ds(start, PANEL), :]
        x = [[rows[8 * g:8 * g + 8, 128 * t:128 * t + 128] for t in range(tiles)] + [diag[8 * g:8 * g + 8]]
             for g in range(groups)]
        for b in range(groups):
            cols = {g: [jnp.broadcast_to(x[g][tiles][:, 8 * b + j:8 * b + j + 1], (8, 128)) for j in range(8)]
                    for g in range(b, groups)}
            pivots = jnp.ones((8, 128), jnp.float32)
            for r in range(8):
                pivot = jnp.broadcast_to(cols[b][r][r:r + 1], (8, 128))
                pivots = jnp.where(sub == r, pivot, pivots)
                inverse = 1.0 / pivot
                raw = [jnp.broadcast_to(v[r:r + 1], (8, 128)) for v in x[b]]
                craw = [jnp.broadcast_to(cols[b][j][r:r + 1], (8, 128)) if j > r else None for j in range(8)]
                for g in range(b, groups):
                    coef = cols[g][r] * inverse
                    if g == b:
                        coef = jnp.where(sub > r, coef, 0.0)
                    x[g] = [v - coef * w for v, w in zip(x[g], raw)]
                    cols[g] = [cols[g][j] - coef * craw[j] if j > r else cols[g][j] for j in range(8)]
            x[b] = [v * lax.rsqrt(pivots) for v in x[b]]
        done = jnp.concatenate([jnp.concatenate(v[:tiles], axis=1) for v in x], axis=0)
        lane = lax.broadcasted_iota(jnp.int32, (PANEL, members), 1)
        lower = jnp.where(lane >= start + PANEL, done[:, :members], 0.0)
        lh, lm, ll = thirds(lower)
        dh, dm, dl = thirds(done)
        left = jnp.concatenate([lh, lh, lm, lh, ll, lm], axis=0)
        right = jnp.concatenate([dh, dm, dh, dl, dh, dm], axis=0)
        work_ref[...] = work_ref[...] - mm(left, right, ((0,), (0,)), None)
        work_ref[pl.ds(start, PANEL), :] = done
        return carry

    lax.fori_loop(0, members // PANEL, panel_step, 0)


def ordered(index_ref, mine_ref, other_ref, out_ref, chips):
    half = mine_ref.shape[0]
    rows = half // chips
    for k in range(chips):
        at = (index_ref[2] ^ k) * rows
        piece = slice(k * rows, (k + 1) * rows)
        out_ref[pl.ds(pl.multiple_of(index_ref[1] * half + at, rows), rows), :] = mine_ref[piece, :]
        out_ref[pl.ds(pl.multiple_of((1 - index_ref[1]) * half + at, rows), rows), :] = other_ref[piece, :]


def solve_kernel(index_ref, sums_ref, sums2_ref, gram_ref, gram2_ref, rot_ref, high_hbm, low_hbm, turned_hbm, *rest, count, chips, ranks):
    pieces, rest = rest[:ranks], rest[ranks:]
    out_hbm, coords_ref, work_ref, all_ref, basis_ref, high_ref, low_ref, snap_ref, rem_high, rem_low, out_ref, sem, out_sem = rest
    rank, members = coords_ref.shape
    each = members // ranks
    copies = [pltpu.make_async_copy(high_hbm, high_ref, sem.at[0]), pltpu.make_async_copy(low_hbm, low_ref, sem.at[1])]
    for k, piece in enumerate(pieces):
        at = pl.multiple_of((index_ref[0] ^ index_ref[FIRST + k]) * each, each)
        copies.append(pltpu.make_async_copy(piece, snap_ref.at[:, pl.ds(at, each), :], sem.at[2 + k]))
    turned = pltpu.make_async_copy(turned_hbm, out_ref, out_sem)
    for copy in copies + [turned]:
        copy.start()
    ordered(index_ref, sums_ref, sums2_ref, all_ref, chips)
    ordered(index_ref, gram_ref, gram2_ref, basis_ref, chips)
    row = lax.broadcasted_iota(jnp.int32, (members, members), 0)
    col = lax.broadcasted_iota(jnp.int32, (members, members), 1)
    eye = row == col
    inner = all_ref[:, rank:]
    diag = jnp.where(eye, inner, 0.0)
    across = lax.rsqrt(jnp.sum(diag, axis=0, keepdims=True) / count + EPS)
    along = lax.rsqrt(jnp.sum(diag, axis=1, keepdims=True) / count + EPS)
    coef = all_ref[:, :rank] * (along / count)
    correct = 2.0 * coef - mm(coef, basis_ref[...], ((1,), (0,))) / count
    work_ref[:, :members] = inner * (along / count) * across - mm(correct, coef, ((1,), (1,)))
    work_ref[:, members:] = jnp.where(eye, 1.0, 0.0)
    all_ref[:, :rank] = coef
    for copy in copies:
        copy.wait()
    lines, _, width = snap_ref.shape
    block = lines // (members // PANEL)

    def remainder(k):
        at = pl.ds(pl.multiple_of(k * (block * width), block * width), block * width)
        taken = mm3((high_ref[at, :], low_ref[at, :]), halves(all_ref[:, :rank]), ((1,), (1,)))
        panel = jnp.concatenate([snap_ref[k * block + i].T for i in range(block)], axis=0) * across
        rem_high[at, :], rem_low[at, :] = halves(panel - taken)

    eliminate(work_ref, members, remainder)
    coefs, tops, bottoms = halves(all_ref[:, :rank]), halves(rot_ref[:rank, :]), halves(rot_ref[rank:, :])
    mix_high, mix_low = halves(mm3(halves(work_ref[:, members:]), bottoms, ((0,), (0,))))
    turned.wait()
    step = 2 * block
    for first in range(0, lines, step):
        at = slice(first * width, (first + step) * width)
        done = mm3((rem_high[at, :], rem_low[at, :]), (mix_high, mix_low), ((1,), (0,)))
        out_ref[first:first + step] += done.reshape(step, width, rank)
        pltpu.make_async_copy(out_ref.at[pl.ds(first, step)], out_hbm.at[pl.ds(first, step)], out_sem).start()
    upper = jnp.where(row <= col, work_ref[:, :members], 0.0)
    coords = (mm3(coefs, tops, ((1,), (0,))) + mm3(halves(upper), bottoms, ((0,), (0,)))) * math.sqrt(rank)
    coords_ref[...] = coords.T
    pltpu.make_async_copy(out_ref, out_hbm, out_sem).wait()


def solve(index, sums, gram, rotation, high, low, turned, pieces, count, chips):
    rows, rank = high.shape
    members = rotation.shape[0] - rank
    ranks = len(pieces)
    lines, each, width = pieces[0].shape
    half = jnp.bfloat16
    return pl.pallas_call(
        functools.partial(solve_kernel, count=float(count), chips=chips, ranks=ranks),
        in_specs=[SCALARS] + [pl.BlockSpec(memory_space=pltpu.VMEM)] * 5 + [pl.BlockSpec(memory_space=pl.ANY)] * (3 + ranks),
        out_specs=[pl.BlockSpec(memory_space=pltpu.HBM), pl.BlockSpec(memory_space=pltpu.VMEM)],
        out_shape=[pltpu.HBM((lines, width, rank), jnp.float32), shape(rank, members)],
        scratch_shapes=[pltpu.VMEM((members, 2 * members), jnp.float32),
                        pltpu.VMEM((members, rank + members), jnp.float32),
                        pltpu.VMEM((rank, rank), jnp.float32),
                        pltpu.VMEM((rows, rank), half), pltpu.VMEM((rows, rank), half),
                        pltpu.VMEM((lines, members, width), jnp.float32),
                        pltpu.VMEM((rows, members), half), pltpu.VMEM((rows, members), half),
                        pltpu.VMEM((lines, width, rank), jnp.float32),
                        pltpu.SemaphoreType.DMA((2 + ranks,)), pltpu.SemaphoreType.DMA],
        compiler_params=params(36),
        name="solve",
    )(index, *sums, *gram, rotation, high, low, in_hbm(turned.reshape(lines, width, rank)), *pieces)


def per_device(initial_disp, initial_vel, stiffness, basis, rotation):
    ranks, sims = lax.axis_size("ana"), lax.axis_size("sim")
    ana, sim = lax.axis_index("ana"), lax.axis_index("sim")
    lines, width, rank = basis.shape
    count = lines * width * sims * ranks
    chips = sims // 2
    core = sim % 2
    near, far = list(range(1, ranks // 2)), list(range(ranks // 2, ranks))
    orders = (near + far[::-1] + [0], far[::-1] + near + [0])
    masks = jnp.where(core == 0, jnp.array(orders[0]), jnp.array(orders[1]))
    first_index = jnp.stack([ana, core, sim // 2])
    index = jnp.concatenate([first_index, masks]).astype(jnp.int32)

    last, first = edges(initial_disp, initial_vel, stiffness)
    up = [(i, i + 1) for i in range(sims - 1)]
    before = lax.ppermute(last, "sim", up)
    after = lax.ppermute(first, "sim", [(j, i) for i, j in up])
    late_disp, late_vel, _ = lax.optimization_barrier((initial_disp, initial_vel, last[0, 0, 0]))
    disp, vel = to_lines(late_disp, late_vel)
    before, after, disp = lax.optimization_barrier((before, after, disp))

    pieces = list(evolve(index, disp, vel, stiffness, before, after, ranks))
    order, pieces = lax.optimization_barrier((index, pieces))
    for slot in range(ranks - 1):
        pairs = [(s * ranks + a, s * ranks + (a ^ orders[s % 2][slot])) for s in range(sims) for a in range(ranks)]
        pieces[slot] = lax.ppermute(pieces[slot], ("sim", "ana"), pairs)

    def meanwhile(_, carry):
        at, *_ = carry
        send, keep, high, low, turned = basis_parts(at, basis, rotation)
        return at + (at >> 20), ana_sum_by_pairs(chip_scatter(at, send, keep, 2), bits[:-1]), high, low, turned

    bits = [2 ** i for i in range(ranks.bit_length() - 1)]
    empty = room(*[shape(lines * width, rank, dtype=t) for t in (jnp.bfloat16, jnp.bfloat16, jnp.float32)])
    order, gram, high, low, turned = lax.fori_loop(
        0, 1 + (ana >> 20), meanwhile, (order, jnp.zeros((rank // sims, rank), jnp.float32), *empty))
    gram = ana_sum_by_pairs(gram, bits[-1:])

    send, keep = products(order, high, low, pieces)
    sums = chip_scatter(order, send, keep, chips)
    sums, gram = lax.optimization_barrier((sums, gram))
    gram = chip_gather(gram, chips)
    sums = ana_sum(sums)
    sums = with_other_core(chip_gather(sums, chips))
    gram = with_other_core(gram)
    return tuple(solve(index, sums, gram, rotation, high, low, turned, pieces, count, chips))


def solution(mesh):
    in_specs = (
        P("ana", "sim", None),
        P("ana", "sim", None),
        P("sim", None),
        P(("sim", "ana"), None, None),
        P(),
    )
    out_specs = (P(("sim", "ana"), None, None), P())
    return jax.shard_map(
        per_device, mesh=mesh, in_specs=in_specs, out_specs=out_specs, check_vma=False
    )
```

```python
import functools
import math

import jax
import jax.numpy as jnp
from jax import lax
from jax.experimental import pallas as pl
from jax.experimental.pallas import tpu as pltpu
from jax.sharding import PartitionSpec as P

STEPS = 4
EPS = 1e-06
MIB = 1024 * 1024
HI = lax.Precision.HIGHEST
FIRST = 3
SCALARS = pl.BlockSpec(memory_space=pltpu.SMEM)


def mm(left, right, dims, precision=HI):
    return lax.dot_general(left, right, (dims, ((), ())), precision=precision, preferred_element_type=jnp.float32)


def shape(*dims, dtype=jnp.float32):
    return jax.ShapeDtypeStruct(dims, dtype)


def params(mib):
    return pltpu.CompilerParams(vmem_limit_bytes=mib * MIB)


def in_hbm(value):
    return pltpu.with_memory_space_constraint(value, pltpu.HBM)


def halves(value):
    high = value.astype(jnp.bfloat16)
    return high, (value - high.astype(jnp.float32)).astype(jnp.bfloat16)


def thirds(value):
    high, _ = halves(value)
    rest = value - high.astype(jnp.float32)
    return (high,) + halves(rest)


def mm3(left, right, dims):
    (lh, ll), (rh, rl) = left, right
    (over,), (under,) = dims
    return mm(jnp.concatenate([ll, lh, lh], axis=over), jnp.concatenate([rh, rl, rh], axis=under), dims, None)


def xor_permute(value, axis, mask):
    size = lax.axis_size(axis)
    return lax.ppermute(value, axis, [(i, i ^ mask) for i in range(size)])


def edges_kernel(stiff_ref, disp_low, vel_low, disp_high, vel_high, last_ref, first_ref):
    w = STEPS
    lines = stiff_ref.shape[0]
    for ref, disp, vel, at, start in ((last_ref, disp_high, vel_high, 8 - w, lines - w), (first_ref, disp_low, vel_low, 0, 0)):
        for i in range(w):
            ref[i] = disp[:, at + i, :]
            ref[w + i] = vel[:, at + i, :]
        ref[2 * w] = jnp.zeros_like(ref[2 * w])
        ref[2 * w, :w, :] = stiff_ref[start:start + w, :]


def edges(disp, vel, stiff):
    members, lines, width = disp.shape
    w = STEPS
    low = pl.BlockSpec((members, 8, width), lambda i: (0, 0, 0))
    high = pl.BlockSpec((members, 8, width), lambda i: (0, lines // 8 - 1, 0))
    edge = pl.BlockSpec((2 * w + 1, members, width), lambda i: (0, 0, 0))
    return pl.pallas_call(
        edges_kernel,
        grid=(1,),
        in_specs=[pl.BlockSpec((lines, width), lambda i: (0, 0)), low, low, high, high],
        out_specs=[edge, edge],
        out_shape=[shape(2 * w + 1, members, width)] * 2,
        compiler_params=params(6),
        name="edges",
    )(in_hbm(stiff), in_hbm(disp), in_hbm(vel), in_hbm(disp), in_hbm(vel))


def to_lines_kernel(disp_ref, vel_ref, disp_out, vel_out):
    lines, group, _ = disp_out.shape
    for line in range(lines):
        disp_out[line] = disp_ref[pl.ds(line, group, stride=lines), :]
        vel_out[line] = vel_ref[pl.ds(line, group, stride=lines), :]


def to_lines(disp, vel):
    members, lines, width = disp.shape
    group = 16
    flat = pl.BlockSpec((group * lines, width), lambda i: (i, 0))
    out = pl.BlockSpec((lines, group, width), lambda i: (0, i, 0))
    return pl.pallas_call(
        to_lines_kernel,
        grid=(members // group,),
        in_specs=[flat, flat],
        out_specs=[out, out],
        out_shape=[shape(lines, members, width)] * 2,
        compiler_params=params(8),
        name="to_lines",
    )(in_hbm(disp.reshape(members * lines, width)), in_hbm(vel.reshape(members * lines, width)))


def evolve_kernel(index_ref, disp_ref, vel_ref, stiff_ref, before_ref, after_ref, *rest, slots):
    outs, (even_ref, odd_ref, speed_ref, pad_ref, all_ref, sem) = rest[:slots], rest[slots:]
    lines, members, width = disp_ref.shape
    w = STEPS
    full = lines + 2 * w
    size = lines // slots
    lane = lax.broadcasted_iota(jnp.int32, (8, width), 1)
    pad_ref[w:2 * w, :] = before_ref[2 * w, :w, :]
    pad_ref[8:8 + lines, :] = stiff_ref[...]
    pad_ref[8 + lines:8 + lines + w, :] = after_ref[2 * w, :w, :]

    def group_step(g, carry):
        at = pl.ds(pl.multiple_of(g * 8, 8), 8)
        for i in range(w):
            even_ref[i], speed_ref[i] = before_ref[i, at, :], before_ref[w + i, at, :]
            even_ref[w + lines + i], speed_ref[w + lines + i] = after_ref[i, at, :], after_ref[w + i, at, :]
        for i in range(lines):
            even_ref[w + i], speed_ref[w + i] = disp_ref[i, at, :], vel_ref[i, at, :]
        now, then = even_ref, odd_ref
        for step in range(1, w + 1):
            for i in range(step, full - step):
                u = now[i]
                right = jnp.where(lane == width - 1, 0.0, pltpu.roll(u, width - 1, 1))
                left = jnp.where(lane == 0, 0.0, pltpu.roll(u, 1, 1))
                around = (now[i + 1] + now[i - 1]) + (right + left)
                stiff = jnp.broadcast_to(pad_ref[8 - w + i:8 - w + i + 1, :], (8, width))
                speed = speed_ref[i] + stiff * (around + u * (0.5 / (1.0 + u * u) - 4.5))
                if step < w:
                    then[i], speed_ref[i] = u + speed, speed
                else:
                    all_ref[i - w, at, :] = u + speed
            now, then = then, now
        for slot, out in enumerate(outs):
            pltpu.make_async_copy(all_ref.at[block(slot), at], out.at[:, at], sem.at[slot]).start()
        return carry

    def block(slot):
        return pl.ds((index_ref[0] ^ index_ref[FIRST + slot]) * size, size)

    lax.fori_loop(0, members // 8, group_step, 0)
    for slot, out in enumerate(outs):
        pltpu.make_async_copy(all_ref.at[block(slot)], out, sem.at[slot]).wait()


def evolve(index, disp, vel, stiff, before, after, slots):
    lines, members, width = disp.shape
    line = pltpu.VMEM((lines + 2 * STEPS, 8, width), jnp.float32)
    return pl.pallas_call(
        functools.partial(evolve_kernel, slots=slots),
        in_specs=[SCALARS] + [pl.BlockSpec(memory_space=pltpu.VMEM)] * 5,
        out_shape=[pltpu.HBM((lines // slots, members, width), jnp.float32)] * slots,
        out_specs=[pl.BlockSpec(memory_space=pltpu.HBM)] * slots,
        scratch_shapes=[line, line, line, pltpu.VMEM((lines + 16, width), jnp.float32),
                        pltpu.VMEM((lines, members, width), jnp.float32), pltpu.SemaphoreType.DMA((slots,))],
        compiler_params=params(8),
        name="evolve",
    )(index, disp, vel, stiff, before, after)


def room(*arrays):
    return pl.pallas_call(
        lambda *refs: None,
        out_specs=[pl.BlockSpec(memory_space=pl.ANY)] * len(arrays),
        out_shape=[pltpu.HBM(a.shape, a.dtype) for a in arrays],
        name="room",
    )()


def tiles_of(rank):
    pairs = [(i, j) for i in range(rank // 128) for j in range(i, rank // 128)]
    return [(slice(128 * i, 128 * i + 128), slice(128 * j, 128 * j + 128),
             slice(128 * (t // 2), 128 * (t // 2) + 128), slice(128 * (t % 2), 128 * (t % 2) + 128))
            for t, (i, j) in enumerate(pairs)]


def packed_rows(rank):
    return len(tiles_of(rank)) * 64


def basis_kernel(index_ref, rot_ref, basis_ref, send_ref, keep_ref, high_ref, low_ref, turned_ref, sum_ref, mixed_ref, pack_ref):
    lines, width, rank = basis_ref.shape
    step = pl.program_id(0)

    @pl.when(step == 0)
    def _():
        sum_ref[...] = jnp.zeros_like(sum_ref)
        mixed_ref[...] = jnp.zeros_like(mixed_ref)

    high, low = halves(basis_ref[...].reshape(lines * width, rank))
    high_ref[...] = high
    low_ref[...] = low
    sum_ref[...] += mm(high, high, ((0,), (0,)), None)
    mixed_ref[...] += mm(high, low, ((0,), (0,)), None)
    turned_ref[...] = mm3((high, low), halves(rot_ref[...]), ((1,), (0,)))

    @pl.when(step == pl.num_programs(0) - 1)
    def _():
        sum_ref[...] += mixed_ref[...] + mixed_ref[...].T
        half = keep_ref.shape[0]
        core = index_ref[1]
        for row, col, to_row, to_col in tiles_of(rank):
            pack_ref[to_row, to_col] = sum_ref[row, col]
        keep_ref[...] = pack_ref[pl.ds(pl.multiple_of(core * half, 8), half), :]
        send_ref[...] = pack_ref[pl.ds(pl.multiple_of((1 - core) * half, 8), half), :]


def basis_parts(index, basis, rotation):
    lines, width, rank = basis.shape
    block = 4
    packed = packed_rows(rank)
    half = pl.BlockSpec((packed // 2, 256), lambda i: (0, 0))
    rows = pl.BlockSpec((block * width, rank), lambda i: (i, 0))
    return pl.pallas_call(
        basis_kernel,
        grid=(lines // block,),
        in_specs=[SCALARS, pl.BlockSpec((rank, rank), lambda i: (0, 0)), pl.BlockSpec((block, width, rank), lambda i: (i, 0, 0))],
        out_specs=[half, half, rows, rows, rows],
        out_shape=[shape(packed // 2, 256)] * 2 + [pltpu.HBM((lines * width, rank), jnp.bfloat16)] * 2
        + [pltpu.HBM((lines * width, rank), jnp.float32)],
        scratch_shapes=[pltpu.VMEM((rank, rank), jnp.float32)] * 2 + [pltpu.VMEM((packed, 256), jnp.float32)],
        compiler_params=params(24),
        name="basis_parts",
    )(index, in_hbm(rotation), in_hbm(basis))


def products_kernel(index_ref, high_ref, low_ref, *rest):
    pieces, (send_ref, keep_ref, snap_ref, sum_ref, mixed_ref) = rest[:-5], rest[-5:]
    lines, members, width = pieces[0].shape
    rank = high_ref.shape[-1]
    step = pl.program_id(0)
    for k, piece in enumerate(pieces):
        at = pl.multiple_of((index_ref[0] ^ index_ref[FIRST + k]) * members, members)
        for line in range(lines):
            snap_ref[pl.ds(at, members), line * width:(line + 1) * width] = piece[line]

    @pl.when(step == 0)
    def _():
        sum_ref[...] = jnp.zeros_like(sum_ref)
        mixed_ref[...] = jnp.zeros_like(mixed_ref)

    snap = halves(snap_ref[...])
    sum_ref[:, :rank] += mm3(snap, (high_ref[...], low_ref[...]), ((1,), (0,)))
    sum_ref[:, rank:] += mm(snap[0], snap[0], ((1,), (1,)), None)
    mixed_ref[...] += mm(snap[0], snap[1], ((1,), (1,)), None)

    @pl.when(step == pl.num_programs(0) - 1)
    def _():
        sum_ref[:, rank:] += mixed_ref[...] + mixed_ref[...].T
        half = keep_ref.shape[0]
        core = index_ref[1]
        keep_ref[...] = sum_ref[pl.ds(pl.multiple_of(core * half, half), half), :]
        send_ref[...] = sum_ref[pl.ds(pl.multiple_of((1 - core) * half, half), half), :]


def products(index, high, low, pieces):
    rank = high.shape[1]
    lines, members, width = pieces[0].shape
    total = members * len(pieces)
    block = 4
    half = pl.BlockSpec((total // 2, rank + total), lambda i: (0, 0))
    return pl.pallas_call(
        products_kernel,
        grid=(lines // block,),
        in_specs=[SCALARS] + [pl.BlockSpec((block * width, rank), lambda i: (i, 0))] * 2
        + [pl.BlockSpec((block, members, width), lambda i: (i, 0, 0))] * len(pieces),
        out_specs=[half, half],
        out_shape=[shape(total // 2, rank + total)] * 2,
        scratch_shapes=[pltpu.VMEM((total, block * width), jnp.float32), pltpu.VMEM((total, rank + total), jnp.float32),
                        pltpu.VMEM((total, total), jnp.float32)],
        compiler_params=params(14),
        name="products",
    )(index, in_hbm(high), in_hbm(low), *pieces)


def split_kernel(index_ref, keep_ref, got_ref, *outs):
    rows = outs[0].shape[0]
    for k, out in enumerate(outs):
        at = pl.ds(pl.multiple_of((index_ref[2] ^ k) * rows, 8), rows)
        out[...] = keep_ref[at, :] + got_ref[at, :]


def split(index, keep, got, chips):
    rows, cols = keep.shape
    return pl.pallas_call(
        split_kernel,
        in_specs=[SCALARS] + [pl.BlockSpec(memory_space=pltpu.VMEM)] * 2,
        out_shape=[shape(rows // chips, cols)] * chips,
        compiler_params=params(4),
        name="split",
    )(index, keep, got)


def tree_sum(values):
    while len(values) > 1:
        values = [a + b for a, b in zip(values[::2], values[1::2])]
    return values[0]


def ana_sum_by_pairs(value, bits):
    for bit in bits:
        value = value + xor_permute(value, "ana", bit)
    return value


def exchange_chips(pieces, limit):
    found = []
    for k in range(1, len(pieces)):
        piece = pieces[k]
        if k > limit:
            piece, found[k - limit - 1] = lax.optimization_barrier((piece, found[k - limit - 1]))
        found.append(xor_permute(piece, "sim", 2 * k))
    return found


def chip_scatter(index, send, keep, limit):
    chips = lax.axis_size("sim") // 2
    got = xor_permute(send, "sim", 1)
    pieces = split(index, keep, got, chips)
    return tree_sum([pieces[0]] + exchange_chips(pieces, limit))


def ana_sum(value):
    return tree_sum([value] + [xor_permute(value, "ana", k) for k in range(1, lax.axis_size("ana"))])


def chip_gather(value, limit):
    chips = lax.axis_size("sim") // 2
    return jnp.concatenate([value] + exchange_chips([value] * chips, limit), axis=0)


def with_other_core(value):
    return value, xor_permute(value, "sim", 1)


PANEL = 32

def eliminate(work_ref, members, aside):
    tiles = work_ref.shape[1] // 128
    groups = PANEL // 8
    sub = lax.broadcasted_iota(jnp.int32, (8, 128), 0)

    def panel_step(k, carry):
        aside(k)
        start = pl.multiple_of(k * PANEL, PANEL)
        at = pl.multiple_of((k * PANEL) // 128 * 128, 128)
        diag = work_ref[pl.ds(start, PANEL), pl.ds(at, 128)]
        diag = pltpu.roll(diag, (128 - (k * PANEL) % 128) % 128, 1)
        rows = work_ref[pl.ds(start, PANEL), :]
        x = [[rows[8 * g:8 * g + 8, 128 * t:128 * t + 128] for t in range(tiles)] + [diag[8 * g:8 * g + 8]]
             for g in range(groups)]
        for b in range(groups):
            cols = {g: [jnp.broadcast_to(x[g][tiles][:, 8 * b + j:8 * b + j + 1], (8, 128)) for j in range(8)]
                    for g in range(b, groups)}
            pivots = jnp.ones((8, 128), jnp.float32)
            for r in range(8):
                pivot = jnp.broadcast_to(cols[b][r][r:r + 1], (8, 128))
                pivots = jnp.where(sub == r, pivot, pivots)
                inverse = 1.0 / pivot
                raw = [jnp.broadcast_to(v[r:r + 1], (8, 128)) for v in x[b]]
                craw = [jnp.broadcast_to(cols[b][j][r:r + 1], (8, 128)) if j > r else None for j in range(8)]
                for g in range(b, groups):
                    coef = cols[g][r] * inverse
                    if g == b:
                        coef = jnp.where(sub > r, coef, 0.0)
                    x[g] = [v - coef * w for v, w in zip(x[g], raw)]
                    cols[g] = [cols[g][j] - coef * craw[j] if j > r else cols[g][j] for j in range(8)]
            x[b] = [v * lax.rsqrt(pivots) for v in x[b]]
        done = jnp.concatenate([jnp.concatenate(v[:tiles], axis=1) for v in x], axis=0)
        lane = lax.broadcasted_iota(jnp.int32, (PANEL, members), 1)
        lower = jnp.where(lane >= start + PANEL, done[:, :members], 0.0)
        lh, lm, ll = thirds(lower)
        dh, dm, dl = thirds(done)
        left = jnp.concatenate([lh, lh, lm, lh, ll, lm], axis=0)
        right = jnp.concatenate([dh, dm, dh, dl, dh, dm], axis=0)
        work_ref[...] = work_ref[...] - mm(left, right, ((0,), (0,)), None)
        work_ref[pl.ds(start, PANEL), :] = done
        return carry

    lax.fori_loop(0, members // PANEL, panel_step, 0)


def ordered(index_ref, mine_ref, other_ref, out_ref, chips):
    half = mine_ref.shape[0]
    rows = half // chips
    for k in range(chips):
        at = (index_ref[2] ^ k) * rows
        piece = slice(k * rows, (k + 1) * rows)
        out_ref[pl.ds(pl.multiple_of(index_ref[1] * half + at, 8), rows), :] = mine_ref[piece, :]
        out_ref[pl.ds(pl.multiple_of((1 - index_ref[1]) * half + at, 8), rows), :] = other_ref[piece, :]


def solve_kernel(index_ref, sums_ref, sums2_ref, gram_ref, gram2_ref, rot_ref, high_hbm, low_hbm, turned_hbm, *rest, count, chips, ranks):
    pieces, rest = rest[:ranks], rest[ranks:]
    out_hbm, coords_ref, work_ref, all_ref, basis_ref, high_ref, low_ref, snap_ref, rem_high, rem_low, out_ref, pack_ref, sem, out_sem = rest
    rank, members = coords_ref.shape
    each = members // ranks
    copies = [pltpu.make_async_copy(high_hbm, high_ref, sem.at[0]), pltpu.make_async_copy(low_hbm, low_ref, sem.at[1])]
    for k, piece in enumerate(pieces):
        at = pl.multiple_of((index_ref[0] ^ index_ref[FIRST + k]) * each, each)
        copies.append(pltpu.make_async_copy(piece, snap_ref.at[:, pl.ds(at, each), :], sem.at[2 + k]))
    turned = pltpu.make_async_copy(turned_hbm, out_ref, out_sem)
    for copy in copies + [turned]:
        copy.start()
    ordered(index_ref, sums_ref, sums2_ref, all_ref, chips)
    ordered(index_ref, gram_ref, gram2_ref, pack_ref, chips)
    for from_row, from_col, at_row, at_col in tiles_of(rank):
        tile = pack_ref[at_row, at_col]
        basis_ref[from_row, from_col] = tile
        if from_row != from_col:
            basis_ref[from_col, from_row] = tile.T
    row = lax.broadcasted_iota(jnp.int32, (members, members), 0)
    col = lax.broadcasted_iota(jnp.int32, (members, members), 1)
    eye = row == col
    inner = all_ref[:, rank:]
    diag = jnp.where(eye, inner, 0.0)
    across = lax.rsqrt(jnp.sum(diag, axis=0, keepdims=True) / count + EPS)
    along = lax.rsqrt(jnp.sum(diag, axis=1, keepdims=True) / count + EPS)
    coef = all_ref[:, :rank] * (along / count)
    correct = 2.0 * coef - mm(coef, basis_ref[...], ((1,), (0,))) / count
    work_ref[:, :members] = inner * (along / count) * across - mm(correct, coef, ((1,), (1,)))
    work_ref[:, members:] = jnp.where(eye, 1.0, 0.0)
    all_ref[:, :rank] = coef
    for copy in copies:
        copy.wait()
    lines, _, width = snap_ref.shape
    block = lines // (members // PANEL)

    def remainder(k):
        at = pl.ds(pl.multiple_of(k * (block * width), block * width), block * width)
        taken = mm3((high_ref[at, :], low_ref[at, :]), halves(all_ref[:, :rank]), ((1,), (1,)))
        panel = jnp.concatenate([snap_ref[k * block + i].T for i in range(block)], axis=0) * across
        rem_high[at, :], rem_low[at, :] = halves(panel - taken)

    eliminate(work_ref, members, remainder)
    coefs, tops, bottoms = halves(all_ref[:, :rank]), halves(rot_ref[:rank, :]), halves(rot_ref[rank:, :])
    mix_high, mix_low = halves(mm3(halves(work_ref[:, members:]), bottoms, ((0,), (0,))))
    turned.wait()
    step = 2 * block
    for first in range(0, lines, step):
        at = slice(first * width, (first + step) * width)
        done = mm3((rem_high[at, :], rem_low[at, :]), (mix_high, mix_low), ((1,), (0,)))
        out_ref[first:first + step] += done.reshape(step, width, rank)
        pltpu.make_async_copy(out_ref.at[pl.ds(first, step)], out_hbm.at[pl.ds(first, step)], out_sem).start()
    upper = jnp.where(row <= col, work_ref[:, :members], 0.0)
    coords = (mm3(coefs, tops, ((1,), (0,))) + mm3(halves(upper), bottoms, ((0,), (0,)))) * math.sqrt(rank)
    coords_ref[...] = coords.T
    pltpu.make_async_copy(out_ref, out_hbm, out_sem).wait()


def solve(index, sums, gram, rotation, high, low, turned, pieces, count, chips):
    rows, rank = high.shape
    members = rotation.shape[0] - rank
    ranks = len(pieces)
    lines, each, width = pieces[0].shape
    half = jnp.bfloat16
    return pl.pallas_call(
        functools.partial(solve_kernel, count=float(count), chips=chips, ranks=ranks),
        in_specs=[SCALARS] + [pl.BlockSpec(memory_space=pltpu.VMEM)] * 5 + [pl.BlockSpec(memory_space=pl.ANY)] * (3 + ranks),
        out_specs=[pl.BlockSpec(memory_space=pltpu.HBM), pl.BlockSpec(memory_space=pltpu.VMEM)],
        out_shape=[pltpu.HBM((lines, width, rank), jnp.float32), shape(rank, members)],
        scratch_shapes=[pltpu.VMEM((members, 2 * members), jnp.float32),
                        pltpu.VMEM((members, rank + members), jnp.float32),
                        pltpu.VMEM((rank, rank), jnp.float32),
                        pltpu.VMEM((rows, rank), half), pltpu.VMEM((rows, rank), half),
                        pltpu.VMEM((lines, members, width), jnp.float32),
                        pltpu.VMEM((rows, members), half), pltpu.VMEM((rows, members), half),
                        pltpu.VMEM((lines, width, rank), jnp.float32),
                        pltpu.VMEM((packed_rows(rank), 256), jnp.float32),
                        pltpu.SemaphoreType.DMA((2 + ranks,)), pltpu.SemaphoreType.DMA],
        compiler_params=params(36),
        name="solve",
    )(index, *sums, *gram, rotation, high, low, in_hbm(turned.reshape(lines, width, rank)), *pieces)


def per_device(initial_disp, initial_vel, stiffness, basis, rotation):
    ranks, sims = lax.axis_size("ana"), lax.axis_size("sim")
    ana, sim = lax.axis_index("ana"), lax.axis_index("sim")
    lines, width, rank = basis.shape
    count = lines * width * sims * ranks
    chips = sims // 2
    core = sim % 2
    near, far = list(range(1, ranks // 2)), list(range(ranks // 2, ranks))
    orders = (near + far[::-1] + [0], far[::-1] + near + [0])
    masks = jnp.where(core == 0, jnp.array(orders[0]), jnp.array(orders[1]))
    first_index = jnp.stack([ana, core, sim // 2])
    index = jnp.concatenate([first_index, masks]).astype(jnp.int32)

    last, first = edges(initial_disp, initial_vel, stiffness)
    up = [(i, i + 1) for i in range(sims - 1)]
    before = lax.ppermute(last, "sim", up)
    after = lax.ppermute(first, "sim", [(j, i) for i, j in up])
    late_disp, late_vel, _ = lax.optimization_barrier((initial_disp, initial_vel, last[0, 0, 0]))
    disp, vel = to_lines(late_disp, late_vel)
    before, after, disp = lax.optimization_barrier((before, after, disp))

    pieces = list(evolve(index, disp, vel, stiffness, before, after, ranks))
    order, pieces = lax.optimization_barrier((index, pieces))
    for slot in range(ranks - 1):
        pairs = [(s * ranks + a, s * ranks + (a ^ orders[s % 2][slot])) for s in range(sims) for a in range(ranks)]
        pieces[slot] = lax.ppermute(pieces[slot], ("sim", "ana"), pairs)

    def meanwhile(_, carry):
        at, *_ = carry
        send, keep, high, low, turned = basis_parts(at, basis, rotation)
        return at + (at >> 20), ana_sum_by_pairs(chip_scatter(at, send, keep, 2), bits[:-1]), high, low, turned

    bits = [2 ** i for i in range(ranks.bit_length() - 1)]
    empty = room(*[shape(lines * width, rank, dtype=t) for t in (jnp.bfloat16, jnp.bfloat16, jnp.float32)])
    order, gram, high, low, turned = lax.fori_loop(
        0, 1 + (ana >> 20), meanwhile, (order, jnp.zeros((packed_rows(rank) // sims, 256), jnp.float32), *empty))
    gram = ana_sum_by_pairs(gram, bits[-1:])

    send, keep = products(order, high, low, pieces)
    sums = chip_scatter(order, send, keep, chips)
    sums, gram = lax.optimization_barrier((sums, gram))
    gram = chip_gather(gram, chips)
    sums = ana_sum(sums)
    sums = with_other_core(chip_gather(sums, chips))
    gram = with_other_core(gram)
    return tuple(solve(index, sums, gram, rotation, high, low, turned, pieces, count, chips))


def solution(mesh):
    in_specs = (
        P("ana", "sim", None),
        P("ana", "sim", None),
        P("sim", None),
        P(("sim", "ana"), None, None),
        P(),
    )
    out_specs = (P(("sim", "ana"), None, None), P())
    return jax.shard_map(
        per_device, mesh=mesh, in_specs=in_specs, out_specs=out_specs, check_vma=False
    )
```

```python
import functools
import math

import jax
import jax.numpy as jnp
from jax import lax
from jax.experimental import pallas as pl
from jax.experimental.pallas import tpu as pltpu
from jax.sharding import PartitionSpec as P

STEPS = 4
EPS = 1e-06
MIB = 1024 * 1024
HI = lax.Precision.HIGHEST
FIRST = 3
SCALARS = pl.BlockSpec(memory_space=pltpu.SMEM)


def mm(left, right, dims, precision=HI):
    return lax.dot_general(left, right, (dims, ((), ())), precision=precision, preferred_element_type=jnp.float32)


def shape(*dims, dtype=jnp.float32):
    return jax.ShapeDtypeStruct(dims, dtype)


def params(mib):
    return pltpu.CompilerParams(vmem_limit_bytes=mib * MIB)


def in_hbm(value):
    return pltpu.with_memory_space_constraint(value, pltpu.HBM)


def halves(value):
    high = value.astype(jnp.bfloat16)
    return high, (value - high.astype(jnp.float32)).astype(jnp.bfloat16)


def thirds(value):
    high, _ = halves(value)
    rest = value - high.astype(jnp.float32)
    return (high,) + halves(rest)


def mm3(left, right, dims):
    (lh, ll), (rh, rl) = left, right
    (over,), (under,) = dims
    return mm(jnp.concatenate([ll, lh, lh], axis=over), jnp.concatenate([rh, rl, rh], axis=under), dims, None)


def xor_permute(value, axis, mask):
    size = lax.axis_size(axis)
    return lax.ppermute(value, axis, [(i, i ^ mask) for i in range(size)])


def edges_kernel(stiff_ref, disp_low, vel_low, disp_high, vel_high, last_ref, first_ref):
    w = STEPS
    lines = stiff_ref.shape[0]
    for ref, disp, vel, at, start in ((last_ref, disp_high, vel_high, 8 - w, lines - w), (first_ref, disp_low, vel_low, 0, 0)):
        for i in range(w):
            ref[i] = disp[:, at + i, :]
            ref[w + i] = vel[:, at + i, :]
        ref[2 * w] = jnp.zeros_like(ref[2 * w])
        ref[2 * w, :w, :] = stiff_ref[start:start + w, :]


def edges(disp, vel, stiff):
    members, lines, width = disp.shape
    w = STEPS
    low = pl.BlockSpec((members, 8, width), lambda i: (0, 0, 0))
    high = pl.BlockSpec((members, 8, width), lambda i: (0, lines // 8 - 1, 0))
    edge = pl.BlockSpec((2 * w + 1, members, width), lambda i: (0, 0, 0))
    return pl.pallas_call(
        edges_kernel,
        grid=(1,),
        in_specs=[pl.BlockSpec((lines, width), lambda i: (0, 0)), low, low, high, high],
        out_specs=[edge, edge],
        out_shape=[shape(2 * w + 1, members, width)] * 2,
        compiler_params=params(6),
        name="edges",
    )(in_hbm(stiff), in_hbm(disp), in_hbm(vel), in_hbm(disp), in_hbm(vel))


def to_lines_kernel(disp_ref, vel_ref, disp_out, vel_out):
    lines, group, _ = disp_out.shape
    for line in range(lines):
        disp_out[line] = disp_ref[pl.ds(line, group, stride=lines), :]
        vel_out[line] = vel_ref[pl.ds(line, group, stride=lines), :]


def to_lines(disp, vel):
    members, lines, width = disp.shape
    group = 16
    flat = pl.BlockSpec((group * lines, width), lambda i: (i, 0))
    out = pl.BlockSpec((lines, group, width), lambda i: (0, i, 0))
    return pl.pallas_call(
        to_lines_kernel,
        grid=(members // group,),
        in_specs=[flat, flat],
        out_specs=[out, out],
        out_shape=[shape(lines, members, width)] * 2,
        compiler_params=params(8),
        name="to_lines",
    )(in_hbm(disp.reshape(members * lines, width)), in_hbm(vel.reshape(members * lines, width)))


def evolve_kernel(index_ref, disp_ref, vel_ref, stiff_ref, before_ref, after_ref, *rest, slots):
    outs, (even_ref, odd_ref, speed_ref, pad_ref, all_ref, sem) = rest[:slots], rest[slots:]
    lines, members, width = disp_ref.shape
    w = STEPS
    full = lines + 2 * w
    size = lines // slots
    lane = lax.broadcasted_iota(jnp.int32, (8, width), 1)
    pad_ref[w:2 * w, :] = before_ref[2 * w, :w, :]
    pad_ref[8:8 + lines, :] = stiff_ref[...]
    pad_ref[8 + lines:8 + lines + w, :] = after_ref[2 * w, :w, :]

    def group_step(g, carry):
        at = pl.ds(pl.multiple_of(g * 8, 8), 8)
        for i in range(w):
            even_ref[i], speed_ref[i] = before_ref[i, at, :], before_ref[w + i, at, :]
            even_ref[w + lines + i], speed_ref[w + lines + i] = after_ref[i, at, :], after_ref[w + i, at, :]
        for i in range(lines):
            even_ref[w + i], speed_ref[w + i] = disp_ref[i, at, :], vel_ref[i, at, :]
        now, then = even_ref, odd_ref
        for step in range(1, w + 1):
            for i in range(step, full - step):
                u = now[i]
                right = jnp.where(lane == width - 1, 0.0, pltpu.roll(u, width - 1, 1))
                left = jnp.where(lane == 0, 0.0, pltpu.roll(u, 1, 1))
                around = (now[i + 1] + now[i - 1]) + (right + left)
                stiff = jnp.broadcast_to(pad_ref[8 - w + i:8 - w + i + 1, :], (8, width))
                speed = speed_ref[i] + stiff * (around + u * (0.5 / (1.0 + u * u) - 4.5))
                if step < w:
                    then[i], speed_ref[i] = u + speed, speed
                else:
                    all_ref[i - w, at, :] = u + speed
            now, then = then, now
        for slot, out in enumerate(outs):
            pltpu.make_async_copy(all_ref.at[block(slot), at], out.at[:, at], sem.at[slot]).start()
        return carry

    def block(slot):
        return pl.ds((index_ref[0] ^ index_ref[FIRST + slot]) * size, size)

    lax.fori_loop(0, members // 8, group_step, 0)
    for slot, out in enumerate(outs):
        pltpu.make_async_copy(all_ref.at[block(slot)], out, sem.at[slot]).wait()


def evolve(index, disp, vel, stiff, before, after, slots):
    lines, members, width = disp.shape
    line = pltpu.VMEM((lines + 2 * STEPS, 8, width), jnp.float32)
    return pl.pallas_call(
        functools.partial(evolve_kernel, slots=slots),
        in_specs=[SCALARS] + [pl.BlockSpec(memory_space=pltpu.VMEM)] * 5,
        out_shape=[pltpu.HBM((lines // slots, members, width), jnp.float32)] * slots,
        out_specs=[pl.BlockSpec(memory_space=pltpu.HBM)] * slots,
        scratch_shapes=[line, line, line, pltpu.VMEM((lines + 16, width), jnp.float32),
                        pltpu.VMEM((lines, members, width), jnp.float32), pltpu.SemaphoreType.DMA((slots,))],
        compiler_params=params(8),
        name="evolve",
    )(index, disp, vel, stiff, before, after)


def room(*arrays):
    return pl.pallas_call(
        lambda *refs: None,
        out_specs=[pl.BlockSpec(memory_space=pl.ANY)] * len(arrays),
        out_shape=[pltpu.HBM(a.shape, a.dtype) for a in arrays],
        name="room",
    )()


def basis_kernel(index_ref, rot_ref, basis_ref, send_ref, keep_ref, high_ref, low_ref, turned_ref, sum_ref, mixed_ref):
    lines, width, rank = basis_ref.shape
    step = pl.program_id(0)

    @pl.when(step == 0)
    def _():
        sum_ref[...] = jnp.zeros_like(sum_ref)
        mixed_ref[...] = jnp.zeros_like(mixed_ref)

    high, low = halves(basis_ref[...].reshape(lines * width, rank))
    high_ref[...] = high
    low_ref[...] = low
    sum_ref[...] += mm(high, high, ((0,), (0,)), None)
    mixed_ref[...] += mm(high, low, ((0,), (0,)), None)
    turned_ref[...] = mm3((high, low), halves(rot_ref[...]), ((1,), (0,)))

    @pl.when(step == pl.num_programs(0) - 1)
    def _():
        sum_ref[...] += mixed_ref[...] + mixed_ref[...].T
        half = keep_ref.shape[0]
        core = index_ref[1]
        keep_ref[...] = sum_ref[pl.ds(pl.multiple_of(core * half, half), half), :]
        send_ref[...] = sum_ref[pl.ds(pl.multiple_of((1 - core) * half, half), half), :]


def basis_parts(index, basis, rotation):
    lines, width, rank = basis.shape
    block = 4
    half = pl.BlockSpec((rank // 2, rank), lambda i: (0, 0))
    rows = pl.BlockSpec((block * width, rank), lambda i: (i, 0))
    return pl.pallas_call(
        basis_kernel,
        grid=(lines // block,),
        in_specs=[SCALARS, pl.BlockSpec((rank, rank), lambda i: (0, 0)), pl.BlockSpec((block, width, rank), lambda i: (i, 0, 0))],
        out_specs=[half, half, rows, rows, rows],
        out_shape=[shape(rank // 2, rank)] * 2 + [pltpu.HBM((lines * width, rank), jnp.bfloat16)] * 2
        + [pltpu.HBM((lines * width, rank), jnp.float32)],
        scratch_shapes=[pltpu.VMEM((rank, rank), jnp.float32)] * 2,
        compiler_params=params(24),
        name="basis_parts",
    )(index, in_hbm(rotation), in_hbm(basis))


def products_kernel(index_ref, high_ref, low_ref, *rest):
    pieces, (send_ref, keep_ref, snap_ref, sum_ref, mixed_ref) = rest[:-5], rest[-5:]
    lines, members, width = pieces[0].shape
    rank = high_ref.shape[-1]
    step = pl.program_id(0)
    for k, piece in enumerate(pieces):
        at = pl.multiple_of((index_ref[0] ^ index_ref[FIRST + k]) * members, members)
        for line in range(lines):
            snap_ref[pl.ds(at, members), line * width:(line + 1) * width] = piece[line]

    @pl.when(step == 0)
    def _():
        sum_ref[...] = jnp.zeros_like(sum_ref)
        mixed_ref[...] = jnp.zeros_like(mixed_ref)

    snap = halves(snap_ref[...])
    sum_ref[:, :rank] += mm3(snap, (high_ref[...], low_ref[...]), ((1,), (0,)))
    sum_ref[:, rank:] += mm(snap[0], snap[0], ((1,), (1,)), None)
    mixed_ref[...] += mm(snap[0], snap[1], ((1,), (1,)), None)

    @pl.when(step == pl.num_programs(0) - 1)
    def _():
        sum_ref[:, rank:] += mixed_ref[...] + mixed_ref[...].T
        half = keep_ref.shape[0]
        core = index_ref[1]
        keep_ref[...] = sum_ref[pl.ds(pl.multiple_of(core * half, half), half), :]
        send_ref[...] = sum_ref[pl.ds(pl.multiple_of((1 - core) * half, half), half), :]


def products(index, high, low, pieces):
    rank = high.shape[1]
    lines, members, width = pieces[0].shape
    total = members * len(pieces)
    block = 4
    half = pl.BlockSpec((total // 2, rank + total), lambda i: (0, 0))
    return pl.pallas_call(
        products_kernel,
        grid=(lines // block,),
        in_specs=[SCALARS] + [pl.BlockSpec((block * width, rank), lambda i: (i, 0))] * 2
        + [pl.BlockSpec((block, members, width), lambda i: (i, 0, 0))] * len(pieces),
        out_specs=[half, half],
        out_shape=[shape(total // 2, rank + total)] * 2,
        scratch_shapes=[pltpu.VMEM((total, block * width), jnp.float32), pltpu.VMEM((total, rank + total), jnp.float32),
                        pltpu.VMEM((total, total), jnp.float32)],
        compiler_params=params(14),
        name="products",
    )(index, in_hbm(high), in_hbm(low), *pieces)


def split_kernel(index_ref, keep_ref, got_ref, *outs):
    rows = outs[0].shape[0]
    for k, out in enumerate(outs):
        at = pl.ds(pl.multiple_of((index_ref[2] ^ k) * rows, rows), rows)
        out[...] = keep_ref[at, :] + got_ref[at, :]


def split(index, keep, got, chips):
    rows, cols = keep.shape
    return pl.pallas_call(
        split_kernel,
        in_specs=[SCALARS] + [pl.BlockSpec(memory_space=pltpu.VMEM)] * 2,
        out_shape=[shape(rows // chips, cols)] * chips,
        compiler_params=params(4),
        name="split",
    )(index, keep, got)


def tree_sum(values):
    while len(values) > 1:
        values = [a + b for a, b in zip(values[::2], values[1::2])]
    return values[0]


def ana_sum_by_pairs(value, bits):
    for bit in bits:
        value = value + xor_permute(value, "ana", bit)
    return value


def exchange_chips(pieces, limit):
    found = []
    for k in range(1, len(pieces)):
        piece = pieces[k]
        if k > limit:
            piece, found[k - limit - 1] = lax.optimization_barrier((piece, found[k - limit - 1]))
        found.append(xor_permute(piece, "sim", 2 * k))
    return found


def chip_scatter(index, send, keep, limit):
    chips = lax.axis_size("sim") // 2
    got = xor_permute(send, "sim", 1)
    pieces = split(index, keep, got, chips)
    return tree_sum([pieces[0]] + exchange_chips(pieces, limit))


def ana_sum(value):
    return tree_sum([value] + [xor_permute(value, "ana", k) for k in range(1, lax.axis_size("ana"))])


def chip_gather(value, limit):
    chips = lax.axis_size("sim") // 2
    return jnp.concatenate([value] + exchange_chips([value] * chips, limit), axis=0)


def with_other_core(value):
    return value, xor_permute(value, "sim", 1)


PANEL = 32

def eliminate(work_ref, members, aside):
    tiles = work_ref.shape[1] // 128
    groups = PANEL // 8
    sub = lax.broadcasted_iota(jnp.int32, (8, 128), 0)

    def panel_step(k, carry):
        aside(k)
        start = pl.multiple_of(k * PANEL, PANEL)
        at = pl.multiple_of((k * PANEL) // 128 * 128, 128)
        diag = work_ref[pl.ds(start, PANEL), pl.ds(at, 128)]
        diag = pltpu.roll(diag, (128 - (k * PANEL) % 128) % 128, 1)
        rows = work_ref[pl.ds(start, PANEL), :]
        x = [[rows[8 * g:8 * g + 8, 128 * t:128 * t + 128] for t in range(tiles)] + [diag[8 * g:8 * g + 8]]
             for g in range(groups)]
        for b in range(groups):
            cols = {g: [jnp.broadcast_to(x[g][tiles][:, 8 * b + j:8 * b + j + 1], (8, 128)) for j in range(8)]
                    for g in range(b, groups)}
            pivots = jnp.ones((8, 128), jnp.float32)
            for r in range(8):
                pivot = jnp.broadcast_to(cols[b][r][r:r + 1], (8, 128))
                pivots = jnp.where(sub == r, pivot, pivots)
                inverse = 1.0 / pivot
                raw = [jnp.broadcast_to(v[r:r + 1], (8, 128)) for v in x[b]]
                craw = [jnp.broadcast_to(cols[b][j][r:r + 1], (8, 128)) if j > r else None for j in range(8)]
                for g in range(b, groups):
                    coef = cols[g][r] * inverse
                    if g == b:
                        coef = jnp.where(sub > r, coef, 0.0)
                    x[g] = [v - coef * w for v, w in zip(x[g], raw)]
                    cols[g] = [cols[g][j] - coef * craw[j] if j > r else cols[g][j] for j in range(8)]
            x[b] = [v * lax.rsqrt(pivots) for v in x[b]]
        done = jnp.concatenate([jnp.concatenate(v[:tiles], axis=1) for v in x], axis=0)
        lane = lax.broadcasted_iota(jnp.int32, (PANEL, members), 1)
        lower = jnp.where(lane >= start + PANEL, done[:, :members], 0.0)
        lh, lm, ll = thirds(lower)
        dh, dm, dl = thirds(done)
        left = jnp.concatenate([lh, lh, lm, lh, ll, lm], axis=0)
        right = jnp.concatenate([dh, dm, dh, dl, dh, dm], axis=0)
        work_ref[...] = work_ref[...] - mm(left, right, ((0,), (0,)), None)
        work_ref[pl.ds(start, PANEL), :] = done
        return carry

    lax.fori_loop(0, members // PANEL, panel_step, 0)


def ordered(index_ref, mine_ref, other_ref, out_ref, chips):
    half = mine_ref.shape[0]
    rows = half // chips
    for k in range(chips):
        at = (index_ref[2] ^ k) * rows
        piece = slice(k * rows, (k + 1) * rows)
        out_ref[pl.ds(pl.multiple_of(index_ref[1] * half + at, rows), rows), :] = mine_ref[piece, :]
        out_ref[pl.ds(pl.multiple_of((1 - index_ref[1]) * half + at, rows), rows), :] = other_ref[piece, :]


def solve_kernel(index_ref, sums_ref, sums2_ref, gram_ref, gram2_ref, rot_ref, high_hbm, low_hbm, turned_hbm, *rest, count, chips, ranks):
    pieces, rest = rest[:ranks], rest[ranks:]
    out_hbm, coords_ref, work_ref, all_ref, basis_ref, high_ref, low_ref, snap_ref, rem_high, rem_low, out_ref, sem, out_sem = rest
    rank, members = coords_ref.shape
    each = members // ranks
    copies = [pltpu.make_async_copy(high_hbm, high_ref, sem.at[0]), pltpu.make_async_copy(low_hbm, low_ref, sem.at[1])]
    for k, piece in enumerate(pieces):
        at = pl.multiple_of((index_ref[0] ^ index_ref[FIRST + k]) * each, each)
        copies.append(pltpu.make_async_copy(piece, snap_ref.at[:, pl.ds(at, each), :], sem.at[2 + k]))
    turned = pltpu.make_async_copy(turned_hbm, out_ref, out_sem)
    for copy in copies + [turned]:
        copy.start()
    ordered(index_ref, sums_ref, sums2_ref, all_ref, chips)
    ordered(index_ref, gram_ref, gram2_ref, basis_ref, chips)
    row = lax.broadcasted_iota(jnp.int32, (members, members), 0)
    col = lax.broadcasted_iota(jnp.int32, (members, members), 1)
    eye = row == col
    inner = all_ref[:, rank:]
    diag = jnp.where(eye, inner, 0.0)
    across = lax.rsqrt(jnp.sum(diag, axis=0, keepdims=True) / count + EPS)
    along = lax.rsqrt(jnp.sum(diag, axis=1, keepdims=True) / count + EPS)
    coef = all_ref[:, :rank] * (along / count)
    correct = 2.0 * coef - mm(coef, basis_ref[...], ((1,), (0,))) / count
    work_ref[:, :members] = inner * (along / count) * across - mm(correct, coef, ((1,), (1,)))
    work_ref[:, members:] = jnp.where(eye, 1.0, 0.0)
    all_ref[:, :rank] = coef
    for copy in copies:
        copy.wait()
    lines, _, width = snap_ref.shape
    block = lines // (members // PANEL)

    def remainder(k):
        at = pl.ds(pl.multiple_of(k * (block * width), block * width), block * width)
        taken = mm3((high_ref[at, :], low_ref[at, :]), halves(all_ref[:, :rank]), ((1,), (1,)))
        panel = jnp.concatenate([snap_ref[k * block + i].T for i in range(block)], axis=0) * across
        rem_high[at, :], rem_low[at, :] = halves(panel - taken)

    eliminate(work_ref, members, remainder)
    coefs, tops, bottoms = halves(all_ref[:, :rank]), halves(rot_ref[:rank, :]), halves(rot_ref[rank:, :])
    mix_high, mix_low = halves(mm3(halves(work_ref[:, members:]), bottoms, ((0,), (0,))))
    turned.wait()
    step = 2 * block
    for first in range(0, lines, step):
        at = slice(first * width, (first + step) * width)
        done = mm3((rem_high[at, :], rem_low[at, :]), (mix_high, mix_low), ((1,), (0,)))
        out_ref[first:first + step] += done.reshape(step, width, rank)
        pltpu.make_async_copy(out_ref.at[pl.ds(first, step)], out_hbm.at[pl.ds(first, step)], out_sem).start()
    upper = jnp.where(row <= col, work_ref[:, :members], 0.0)
    coords = (mm3(coefs, tops, ((1,), (0,))) + mm3(halves(upper), bottoms, ((0,), (0,)))) * math.sqrt(rank)
    coords_ref[...] = coords.T
    pltpu.make_async_copy(out_ref, out_hbm, out_sem).wait()


def solve(index, sums, gram, rotation, high, low, turned, pieces, count, chips):
    rows, rank = high.shape
    members = rotation.shape[0] - rank
    ranks = len(pieces)
    lines, each, width = pieces[0].shape
    half = jnp.bfloat16
    return pl.pallas_call(
        functools.partial(solve_kernel, count=float(count), chips=chips, ranks=ranks),
        in_specs=[SCALARS] + [pl.BlockSpec(memory_space=pltpu.VMEM)] * 5 + [pl.BlockSpec(memory_space=pl.ANY)] * (3 + ranks),
        out_specs=[pl.BlockSpec(memory_space=pltpu.HBM), pl.BlockSpec(memory_space=pltpu.VMEM)],
        out_shape=[pltpu.HBM((lines, width, rank), jnp.float32), shape(rank, members)],
        scratch_shapes=[pltpu.VMEM((members, 2 * members), jnp.float32),
                        pltpu.VMEM((members, rank + members), jnp.float32),
                        pltpu.VMEM((rank, rank), jnp.float32),
                        pltpu.VMEM((rows, rank), half), pltpu.VMEM((rows, rank), half),
                        pltpu.VMEM((lines, members, width), jnp.float32),
                        pltpu.VMEM((rows, members), half), pltpu.VMEM((rows, members), half),
                        pltpu.VMEM((lines, width, rank), jnp.float32),
                        pltpu.SemaphoreType.DMA((2 + ranks,)), pltpu.SemaphoreType.DMA],
        compiler_params=params(36),
        name="solve",
    )(index, *sums, *gram, rotation, high, low, in_hbm(turned.reshape(lines, width, rank)), *pieces)


def per_device(initial_disp, initial_vel, stiffness, basis, rotation):
    ranks, sims = lax.axis_size("ana"), lax.axis_size("sim")
    ana, sim = lax.axis_index("ana"), lax.axis_index("sim")
    lines, width, rank = basis.shape
    count = lines * width * sims * ranks
    chips = sims // 2
    core = sim % 2
    slots = list(range(1, ranks)) + [0]
    masks = jnp.array(slots)
    first_index = jnp.stack([ana, core, sim // 2])
    index = jnp.concatenate([first_index, masks]).astype(jnp.int32)

    last, first = edges(initial_disp, initial_vel, stiffness)
    up = [(i, i + 1) for i in range(sims - 1)]
    before = lax.ppermute(last, "sim", up)
    after = lax.ppermute(first, "sim", [(j, i) for i, j in up])
    late_disp, late_vel, _ = lax.optimization_barrier((initial_disp, initial_vel, last[0, 0, 0]))
    disp, vel = to_lines(late_disp, late_vel)
    before, after, disp = lax.optimization_barrier((before, after, disp))

    pieces = list(evolve(index, disp, vel, stiffness, before, after, ranks))
    order, pieces = lax.optimization_barrier((index, pieces))
    for slot in range(ranks - 1):
        pieces[slot] = xor_permute(pieces[slot], "ana", slots[slot])

    def meanwhile(_, carry):
        at, *_ = carry
        send, keep, high, low, turned = basis_parts(at, basis, rotation)
        return at + (at >> 20), ana_sum_by_pairs(chip_scatter(at, send, keep, 2), bits[:-1]), high, low, turned

    bits = [2 ** i for i in range(ranks.bit_length() - 1)]
    empty = room(*[shape(lines * width, rank, dtype=t) for t in (jnp.bfloat16, jnp.bfloat16, jnp.float32)])
    order, gram, high, low, turned = lax.fori_loop(
        0, 1 + (ana >> 20), meanwhile, (order, jnp.zeros((rank // sims, rank), jnp.float32), *empty))
    gram = ana_sum_by_pairs(gram, bits[-1:])

    send, keep = products(order, high, low, pieces)
    sums = chip_scatter(order, send, keep, chips)
    sums, gram = lax.optimization_barrier((sums, gram))
    gram = chip_gather(gram, chips)
    sums = ana_sum(sums)
    sums = with_other_core(chip_gather(sums, chips))
    gram = with_other_core(gram)
    return tuple(solve(index, sums, gram, rotation, high, low, turned, pieces, count, chips))


def solution(mesh):
    in_specs = (
        P("ana", "sim", None),
        P("ana", "sim", None),
        P("sim", None),
        P(("sim", "ana"), None, None),
        P(),
    )
    out_specs = (P(("sim", "ana"), None, None), P())
    return jax.shard_map(
        per_device, mesh=mesh, in_specs=in_specs, out_specs=out_specs, check_vma=False
    )
```

```python
import functools
import math

import jax
import jax.numpy as jnp
from jax import lax
from jax.experimental import pallas as pl
from jax.experimental.pallas import tpu as pltpu
from jax.sharding import PartitionSpec as P

STEPS = 4
EPS = 1e-06
MIB = 1024 * 1024
HI = lax.Precision.HIGHEST
FIRST = 3
SCALARS = pl.BlockSpec(memory_space=pltpu.SMEM)


def mm(left, right, dims, precision=HI):
    return lax.dot_general(left, right, (dims, ((), ())), precision=precision, preferred_element_type=jnp.float32)


def shape(*dims, dtype=jnp.float32):
    return jax.ShapeDtypeStruct(dims, dtype)


def params(mib):
    return pltpu.CompilerParams(vmem_limit_bytes=mib * MIB)


def in_hbm(value):
    return pltpu.with_memory_space_constraint(value, pltpu.HBM)


def halves(value):
    high = value.astype(jnp.bfloat16)
    return high, (value - high.astype(jnp.float32)).astype(jnp.bfloat16)


def thirds(value):
    high, _ = halves(value)
    rest = value - high.astype(jnp.float32)
    return (high,) + halves(rest)


def mm3(left, right, dims):
    (lh, ll), (rh, rl) = left, right
    (over,), (under,) = dims
    return mm(jnp.concatenate([ll, lh, lh], axis=over), jnp.concatenate([rh, rl, rh], axis=under), dims, None)


def xor_permute(value, axis, mask):
    size = lax.axis_size(axis)
    return lax.ppermute(value, axis, [(i, i ^ mask) for i in range(size)])


def edges_kernel(stiff_ref, disp_low, vel_low, disp_high, vel_high, last_ref, first_ref):
    w = STEPS
    lines = stiff_ref.shape[0]
    for ref, disp, vel, at, start in ((last_ref, disp_high, vel_high, 8 - w, lines - w), (first_ref, disp_low, vel_low, 0, 0)):
        skip = 1 if ref is last_ref else 0
        for i in range(w):
            ref[i] = disp[:, at + i, :]
        for i in range(w - 1):
            ref[w + i] = vel[:, at + skip + i, :]
        ref[2 * w - 1] = jnp.zeros_like(ref[2 * w - 1])
        ref[2 * w - 1, :w, :] = stiff_ref[start:start + w, :]


def edges(disp, vel, stiff):
    members, lines, width = disp.shape
    w = STEPS
    low = pl.BlockSpec((members, 8, width), lambda i: (0, 0, 0))
    high = pl.BlockSpec((members, 8, width), lambda i: (0, lines // 8 - 1, 0))
    edge = pl.BlockSpec((2 * w, members, width), lambda i: (0, 0, 0))
    return pl.pallas_call(
        edges_kernel,
        grid=(1,),
        in_specs=[pl.BlockSpec((lines, width), lambda i: (0, 0)), low, low, high, high],
        out_specs=[edge, edge],
        out_shape=[shape(2 * w, members, width)] * 2,
        compiler_params=params(6),
        name="edges",
    )(in_hbm(stiff), in_hbm(disp), in_hbm(vel), in_hbm(disp), in_hbm(vel))


def to_lines_kernel(disp_ref, vel_ref, disp_out, vel_out):
    lines, group, _ = disp_out.shape
    for line in range(lines):
        disp_out[line] = disp_ref[pl.ds(line, group, stride=lines), :]
        vel_out[line] = vel_ref[pl.ds(line, group, stride=lines), :]


def to_lines(disp, vel):
    members, lines, width = disp.shape
    group = 16
    flat = pl.BlockSpec((group * lines, width), lambda i: (i, 0))
    out = pl.BlockSpec((lines, group, width), lambda i: (0, i, 0))
    return pl.pallas_call(
        to_lines_kernel,
        grid=(members // group,),
        in_specs=[flat, flat],
        out_specs=[out, out],
        out_shape=[shape(lines, members, width)] * 2,
        compiler_params=params(8),
        name="to_lines",
    )(in_hbm(disp.reshape(members * lines, width)), in_hbm(vel.reshape(members * lines, width)))


def evolve_kernel(index_ref, disp_ref, vel_ref, stiff_ref, before_ref, after_ref, *rest, slots):
    outs, (even_ref, odd_ref, speed_ref, pad_ref, all_ref, sem) = rest[:slots], rest[slots:]
    lines, members, width = disp_ref.shape
    w = STEPS
    full = lines + 2 * w
    size = lines // slots
    lane = lax.broadcasted_iota(jnp.int32, (8, width), 1)
    pad_ref[w:2 * w, :] = before_ref[2 * w - 1, :w, :]
    pad_ref[8:8 + lines, :] = stiff_ref[...]
    pad_ref[8 + lines:8 + lines + w, :] = after_ref[2 * w - 1, :w, :]

    def group_step(g, carry):
        at = pl.ds(pl.multiple_of(g * 8, 8), 8)
        for i in range(w):
            even_ref[i], even_ref[w + lines + i] = before_ref[i, at, :], after_ref[i, at, :]
        for i in range(w - 1):
            speed_ref[1 + i], speed_ref[w + lines + i] = before_ref[w + i, at, :], after_ref[w + i, at, :]
        for i in range(lines):
            even_ref[w + i], speed_ref[w + i] = disp_ref[i, at, :], vel_ref[i, at, :]
        now, then = even_ref, odd_ref
        for step in range(1, w + 1):
            for i in range(step, full - step):
                u = now[i]
                right = jnp.where(lane == width - 1, 0.0, pltpu.roll(u, width - 1, 1))
                left = jnp.where(lane == 0, 0.0, pltpu.roll(u, 1, 1))
                around = (now[i + 1] + now[i - 1]) + (right + left)
                stiff = jnp.broadcast_to(pad_ref[8 - w + i:8 - w + i + 1, :], (8, width))
                speed = speed_ref[i] + stiff * (around + u * (0.5 / (1.0 + u * u) - 4.5))
                if step < w:
                    then[i], speed_ref[i] = u + speed, speed
                else:
                    all_ref[i - w, at, :] = u + speed
            now, then = then, now
        for slot, out in enumerate(outs):
            pltpu.make_async_copy(all_ref.at[block(slot), at], out.at[:, at], sem.at[slot]).start()
        return carry

    def block(slot):
        return pl.ds((index_ref[0] ^ index_ref[FIRST + slot]) * size, size)

    lax.fori_loop(0, members // 8, group_step, 0)
    for slot, out in enumerate(outs):
        pltpu.make_async_copy(all_ref.at[block(slot)], out, sem.at[slot]).wait()


def evolve(index, disp, vel, stiff, before, after, slots):
    lines, members, width = disp.shape
    line = pltpu.VMEM((lines + 2 * STEPS, 8, width), jnp.float32)
    return pl.pallas_call(
        functools.partial(evolve_kernel, slots=slots),
        in_specs=[SCALARS] + [pl.BlockSpec(memory_space=pltpu.VMEM)] * 5,
        out_shape=[pltpu.HBM((lines // slots, members, width), jnp.float32)] * slots,
        out_specs=[pl.BlockSpec(memory_space=pltpu.HBM)] * slots,
        scratch_shapes=[line, line, line, pltpu.VMEM((lines + 16, width), jnp.float32),
                        pltpu.VMEM((lines, members, width), jnp.float32), pltpu.SemaphoreType.DMA((slots,))],
        compiler_params=params(8),
        name="evolve",
    )(index, disp, vel, stiff, before, after)


def room(*arrays):
    return pl.pallas_call(
        lambda *refs: None,
        out_specs=[pl.BlockSpec(memory_space=pl.ANY)] * len(arrays),
        out_shape=[pltpu.HBM(a.shape, a.dtype) for a in arrays],
        name="room",
    )()


def basis_kernel(index_ref, rot_ref, basis_ref, send_ref, keep_ref, high_ref, low_ref, turned_ref, sum_ref, mixed_ref):
    lines, width, rank = basis_ref.shape
    step = pl.program_id(0)

    @pl.when(step == 0)
    def _():
        sum_ref[...] = jnp.zeros_like(sum_ref)
        mixed_ref[...] = jnp.zeros_like(mixed_ref)

    high, low = halves(basis_ref[...].reshape(lines * width, rank))
    high_ref[...] = high
    low_ref[...] = low
    sum_ref[...] += mm(high, high, ((0,), (0,)), None)
    mixed_ref[...] += mm(high, low, ((0,), (0,)), None)
    turned_ref[...] = mm3((high, low), halves(rot_ref[...]), ((1,), (0,)))

    @pl.when(step == pl.num_programs(0) - 1)
    def _():
        sum_ref[...] += mixed_ref[...] + mixed_ref[...].T
        half = keep_ref.shape[0]
        core = index_ref[1]
        keep_ref[...] = sum_ref[pl.ds(pl.multiple_of(core * half, half), half), :]
        send_ref[...] = sum_ref[pl.ds(pl.multiple_of((1 - core) * half, half), half), :]


def basis_parts(index, basis, rotation):
    lines, width, rank = basis.shape
    block = 4
    half = pl.BlockSpec((rank // 2, rank), lambda i: (0, 0))
    rows = pl.BlockSpec((block * width, rank), lambda i: (i, 0))
    return pl.pallas_call(
        basis_kernel,
        grid=(lines // block,),
        in_specs=[SCALARS, pl.BlockSpec((rank, rank), lambda i: (0, 0)), pl.BlockSpec((block, width, rank), lambda i: (i, 0, 0))],
        out_specs=[half, half, rows, rows, rows],
        out_shape=[shape(rank // 2, rank)] * 2 + [pltpu.HBM((lines * width, rank), jnp.bfloat16)] * 2
        + [pltpu.HBM((lines * width, rank), jnp.float32)],
        scratch_shapes=[pltpu.VMEM((rank, rank), jnp.float32)] * 2,
        compiler_params=params(24),
        name="basis_parts",
    )(index, in_hbm(rotation), in_hbm(basis))


def products_kernel(index_ref, high_ref, low_ref, *rest):
    pieces, (send_ref, keep_ref, snap_ref, sum_ref, mixed_ref) = rest[:-5], rest[-5:]
    lines, members, width = pieces[0].shape
    rank = high_ref.shape[-1]
    step = pl.program_id(0)
    for k, piece in enumerate(pieces):
        at = pl.multiple_of((index_ref[0] ^ index_ref[FIRST + k]) * members, members)
        for line in range(lines):
            snap_ref[pl.ds(at, members), line * width:(line + 1) * width] = piece[line]

    @pl.when(step == 0)
    def _():
        sum_ref[...] = jnp.zeros_like(sum_ref)
        mixed_ref[...] = jnp.zeros_like(mixed_ref)

    snap = halves(snap_ref[...])
    sum_ref[:, :rank] += mm3(snap, (high_ref[...], low_ref[...]), ((1,), (0,)))
    sum_ref[:, rank:] += mm(snap[0], snap[0], ((1,), (1,)), None)
    mixed_ref[...] += mm(snap[0], snap[1], ((1,), (1,)), None)

    @pl.when(step == pl.num_programs(0) - 1)
    def _():
        sum_ref[:, rank:] += mixed_ref[...] + mixed_ref[...].T
        half = keep_ref.shape[0]
        core = index_ref[1]
        keep_ref[...] = sum_ref[pl.ds(pl.multiple_of(core * half, half), half), :]
        send_ref[...] = sum_ref[pl.ds(pl.multiple_of((1 - core) * half, half), half), :]


def products(index, high, low, pieces):
    rank = high.shape[1]
    lines, members, width = pieces[0].shape
    total = members * len(pieces)
    block = 8
    half = pl.BlockSpec((total // 2, rank + total), lambda i: (0, 0))
    return pl.pallas_call(
        products_kernel,
        grid=(lines // block,),
        in_specs=[SCALARS] + [pl.BlockSpec((block * width, rank), lambda i: (i, 0))] * 2
        + [pl.BlockSpec((block, members, width), lambda i: (i, 0, 0))] * len(pieces),
        out_specs=[half, half],
        out_shape=[shape(total // 2, rank + total)] * 2,
        scratch_shapes=[pltpu.VMEM((total, block * width), jnp.float32), pltpu.VMEM((total, rank + total), jnp.float32),
                        pltpu.VMEM((total, total), jnp.float32)],
        compiler_params=params(22),
        name="products",
    )(index, in_hbm(high), in_hbm(low), *pieces)


def split_kernel(index_ref, keep_ref, got_ref, *outs):
    rows = outs[0].shape[0]
    for k, out in enumerate(outs):
        at = pl.ds(pl.multiple_of((index_ref[2] ^ k) * rows, rows), rows)
        out[...] = keep_ref[at, :] + got_ref[at, :]


def split(index, keep, got, chips):
    rows, cols = keep.shape
    return pl.pallas_call(
        split_kernel,
        in_specs=[SCALARS] + [pl.BlockSpec(memory_space=pltpu.VMEM)] * 2,
        out_shape=[shape(rows // chips, cols)] * chips,
        compiler_params=params(4),
        name="split",
    )(index, keep, got)


def tree_sum(values):
    while len(values) > 1:
        values = [a + b for a, b in zip(values[::2], values[1::2])]
    return values[0]


def ana_sum_by_pairs(value, bits):
    for bit in bits:
        value = value + xor_permute(value, "ana", bit)
    return value


def exchange_chips(pieces, limit):
    found = []
    for k in range(1, len(pieces)):
        piece = pieces[k]
        if k > limit:
            piece, found[k - limit - 1] = lax.optimization_barrier((piece, found[k - limit - 1]))
        found.append(xor_permute(piece, "sim", 2 * k))
    return found


def chip_scatter(index, send, keep, limit):
    chips = lax.axis_size("sim") // 2
    got = xor_permute(send, "sim", 1)
    pieces = split(index, keep, got, chips)
    return tree_sum([pieces[0]] + exchange_chips(pieces, limit))


def ana_sum(value):
    return tree_sum([value] + [xor_permute(value, "ana", k) for k in range(1, lax.axis_size("ana"))])


def chip_gather(value, limit):
    chips = lax.axis_size("sim") // 2
    return jnp.concatenate([value] + exchange_chips([value] * chips, limit), axis=0)


def with_other_core(value):
    return value, xor_permute(value, "sim", 1)


PANEL = 32

def eliminate(work_ref, members, aside):
    tiles = work_ref.shape[1] // 128
    groups = PANEL // 8
    sub = lax.broadcasted_iota(jnp.int32, (8, 128), 0)

    def panel_step(k, carry):
        aside(k)
        start = pl.multiple_of(k * PANEL, PANEL)
        at = pl.multiple_of((k * PANEL) // 128 * 128, 128)
        diag = work_ref[pl.ds(start, PANEL), pl.ds(at, 128)]
        diag = pltpu.roll(diag, (128 - (k * PANEL) % 128) % 128, 1)
        rows = work_ref[pl.ds(start, PANEL), :]
        x = [[rows[8 * g:8 * g + 8, 128 * t:128 * t + 128] for t in range(tiles)] + [diag[8 * g:8 * g + 8]]
             for g in range(groups)]
        for b in range(groups):
            cols = {g: [jnp.broadcast_to(x[g][tiles][:, 8 * b + j:8 * b + j + 1], (8, 128)) for j in range(8)]
                    for g in range(b, groups)}
            pivots = jnp.ones((8, 128), jnp.float32)
            for r in range(8):
                pivot = jnp.broadcast_to(cols[b][r][r:r + 1], (8, 128))
                pivots = jnp.where(sub == r, pivot, pivots)
                inverse = 1.0 / pivot
                raw = [jnp.broadcast_to(v[r:r + 1], (8, 128)) for v in x[b]]
                craw = [jnp.broadcast_to(cols[b][j][r:r + 1], (8, 128)) if j > r else None for j in range(8)]
                for g in range(b, groups):
                    coef = cols[g][r] * inverse
                    if g == b:
                        coef = jnp.where(sub > r, coef, 0.0)
                    x[g] = [v - coef * w for v, w in zip(x[g], raw)]
                    cols[g] = [cols[g][j] - coef * craw[j] if j > r else cols[g][j] for j in range(8)]
            x[b] = [v * lax.rsqrt(pivots) for v in x[b]]
        done = jnp.concatenate([jnp.concatenate(v[:tiles], axis=1) for v in x], axis=0)
        lane = lax.broadcasted_iota(jnp.int32, (PANEL, members), 1)
        lower = jnp.where(lane >= start + PANEL, done[:, :members], 0.0)
        lh, lm, ll = thirds(lower)
        dh, dm, dl = thirds(done)
        left = jnp.concatenate([lh, lh, lm, lh, ll, lm], axis=0)
        right = jnp.concatenate([dh, dm, dh, dl, dh, dm], axis=0)
        work_ref[...] = work_ref[...] - mm(left, right, ((0,), (0,)), None)
        work_ref[pl.ds(start, PANEL), :] = done
        return carry

    lax.fori_loop(0, members // PANEL, panel_step, 0)


def ordered(index_ref, mine_ref, other_ref, out_ref, chips):
    half = mine_ref.shape[0]
    rows = half // chips
    for k in range(chips):
        at = (index_ref[2] ^ k) * rows
        piece = slice(k * rows, (k + 1) * rows)
        out_ref[pl.ds(pl.multiple_of(index_ref[1] * half + at, rows), rows), :] = mine_ref[piece, :]
        out_ref[pl.ds(pl.multiple_of((1 - index_ref[1]) * half + at, rows), rows), :] = other_ref[piece, :]


def solve_kernel(index_ref, sums_ref, sums2_ref, gram_ref, gram2_ref, rot_ref, high_hbm, low_hbm, turned_hbm, *rest, count, chips, ranks):
    pieces, rest = rest[:ranks], rest[ranks:]
    out_hbm, coords_ref, work_ref, all_ref, basis_ref, high_ref, low_ref, snap_ref, rem_high, rem_low, out_ref, sem, out_sem = rest
    rank, members = coords_ref.shape
    each = members // ranks
    copies = [pltpu.make_async_copy(high_hbm, high_ref, sem.at[0]), pltpu.make_async_copy(low_hbm, low_ref, sem.at[1])]
    for k, piece in enumerate(pieces):
        at = pl.multiple_of((index_ref[0] ^ index_ref[FIRST + k]) * each, each)
        copies.append(pltpu.make_async_copy(piece, snap_ref.at[:, pl.ds(at, each), :], sem.at[2 + k]))
    turned = pltpu.make_async_copy(turned_hbm, out_ref, out_sem)
    for copy in copies + [turned]:
        copy.start()
    ordered(index_ref, sums_ref, sums2_ref, all_ref, chips)
    ordered(index_ref, gram_ref, gram2_ref, basis_ref, chips)
    row = lax.broadcasted_iota(jnp.int32, (members, members), 0)
    col = lax.broadcasted_iota(jnp.int32, (members, members), 1)
    eye = row == col
    inner = all_ref[:, rank:]
    diag = jnp.where(eye, inner, 0.0)
    across = lax.rsqrt(jnp.sum(diag, axis=0, keepdims=True) / count + EPS)
    along = lax.rsqrt(jnp.sum(diag, axis=1, keepdims=True) / count + EPS)
    coef = all_ref[:, :rank] * (along / count)
    correct = 2.0 * coef - mm(coef, basis_ref[...], ((1,), (0,))) / count
    work_ref[:, :members] = inner * (along / count) * across - mm(correct, coef, ((1,), (1,)))
    work_ref[:, members:] = jnp.where(eye, 1.0, 0.0)
    all_ref[:, :rank] = coef
    for copy in copies:
        copy.wait()
    lines, _, width = snap_ref.shape
    block = lines // (members // PANEL)

    def remainder(k):
        at = pl.ds(pl.multiple_of(k * (block * width), block * width), block * width)
        taken = mm3((high_ref[at, :], low_ref[at, :]), halves(all_ref[:, :rank]), ((1,), (1,)))
        panel = jnp.concatenate([snap_ref[k * block + i].T for i in range(block)], axis=0) * across
        rem_high[at, :], rem_low[at, :] = halves(panel - taken)

    eliminate(work_ref, members, remainder)
    coefs, tops, bottoms = halves(all_ref[:, :rank]), halves(rot_ref[:rank, :]), halves(rot_ref[rank:, :])
    mix_high, mix_low = halves(mm3(halves(work_ref[:, members:]), bottoms, ((0,), (0,))))
    turned.wait()
    step = 2 * block
    for first in range(0, lines, step):
        at = slice(first * width, (first + step) * width)
        done = mm3((rem_high[at, :], rem_low[at, :]), (mix_high, mix_low), ((1,), (0,)))
        out_ref[first:first + step] += done.reshape(step, width, rank)
        pltpu.make_async_copy(out_ref.at[pl.ds(first, step)], out_hbm.at[pl.ds(first, step)], out_sem).start()
    upper = jnp.where(row <= col, work_ref[:, :members], 0.0)
    coords = (mm3(coefs, tops, ((1,), (0,))) + mm3(halves(upper), bottoms, ((0,), (0,)))) * math.sqrt(rank)
    coords_ref[...] = coords.T
    pltpu.make_async_copy(out_ref, out_hbm, out_sem).wait()


def solve(index, sums, gram, rotation, high, low, turned, pieces, count, chips):
    rows, rank = high.shape
    members = rotation.shape[0] - rank
    ranks = len(pieces)
    lines, each, width = pieces[0].shape
    half = jnp.bfloat16
    return pl.pallas_call(
        functools.partial(solve_kernel, count=float(count), chips=chips, ranks=ranks),
        in_specs=[SCALARS] + [pl.BlockSpec(memory_space=pltpu.VMEM)] * 5 + [pl.BlockSpec(memory_space=pl.ANY)] * (3 + ranks),
        out_specs=[pl.BlockSpec(memory_space=pltpu.HBM), pl.BlockSpec(memory_space=pltpu.VMEM)],
        out_shape=[pltpu.HBM((lines, width, rank), jnp.float32), shape(rank, members)],
        scratch_shapes=[pltpu.VMEM((members, 2 * members), jnp.float32),
                        pltpu.VMEM((members, rank + members), jnp.float32),
                        pltpu.VMEM((rank, rank), jnp.float32),
                        pltpu.VMEM((rows, rank), half), pltpu.VMEM((rows, rank), half),
                        pltpu.VMEM((lines, members, width), jnp.float32),
                        pltpu.VMEM((rows, members), half), pltpu.VMEM((rows, members), half),
                        pltpu.VMEM((lines, width, rank), jnp.float32),
                        pltpu.SemaphoreType.DMA((2 + ranks,)), pltpu.SemaphoreType.DMA],
        compiler_params=params(36),
        name="solve",
    )(index, *sums, *gram, rotation, high, low, in_hbm(turned.reshape(lines, width, rank)), *pieces)


def per_device(initial_disp, initial_vel, stiffness, basis, rotation):
    ranks, sims = lax.axis_size("ana"), lax.axis_size("sim")
    ana, sim = lax.axis_index("ana"), lax.axis_index("sim")
    lines, width, rank = basis.shape
    count = lines * width * sims * ranks
    chips = sims // 2
    core = sim % 2
    slots = list(range(1, ranks)) + [0]
    masks = jnp.array(slots)
    first_index = jnp.stack([ana, core, sim // 2])
    index = jnp.concatenate([first_index, masks]).astype(jnp.int32)

    last, first = edges(initial_disp, initial_vel, stiffness)
    up = [(i, i + 1) for i in range(sims - 1)]
    before = lax.ppermute(last, "sim", up)
    after = lax.ppermute(first, "sim", [(j, i) for i, j in up])
    late_disp, late_vel, _ = lax.optimization_barrier((initial_disp, initial_vel, last[0, 0, 0]))
    disp, vel = to_lines(late_disp, late_vel)
    before, after, disp = lax.optimization_barrier((before, after, disp))

    pieces = list(evolve(index, disp, vel, stiffness, before, after, ranks))
    order, pieces = lax.optimization_barrier((index, pieces))
    for slot in range(ranks - 1):
        pieces[slot] = xor_permute(pieces[slot], "ana", slots[slot])

    def meanwhile(_, carry):
        at, *_ = carry
        send, keep, high, low, turned = basis_parts(at, basis, rotation)
        return at + (at >> 20), ana_sum_by_pairs(chip_scatter(at, send, keep, 2), bits[:-1]), high, low, turned

    bits = [2 ** i for i in range(ranks.bit_length() - 1)]
    empty = room(*[shape(lines * width, rank, dtype=t) for t in (jnp.bfloat16, jnp.bfloat16, jnp.float32)])
    order, gram, high, low, turned = lax.fori_loop(
        0, 1 + (ana >> 20), meanwhile, (order, jnp.zeros((rank // sims, rank), jnp.float32), *empty))
    gram = ana_sum_by_pairs(gram, bits[-1:])

    send, keep = products(order, high, low, pieces)
    sums = chip_scatter(order, send, keep, chips)
    sums, gram = lax.optimization_barrier((sums, gram))
    gram = chip_gather(gram, chips)
    sums = ana_sum(sums)
    sums = with_other_core(chip_gather(sums, chips))
    gram = with_other_core(gram)
    return tuple(solve(index, sums, gram, rotation, high, low, turned, pieces, count, chips))


def solution(mesh):
    in_specs = (
        P("ana", "sim", None),
        P("ana", "sim", None),
        P("sim", None),
        P(("sim", "ana"), None, None),
        P(),
    )
    out_specs = (P(("sim", "ana"), None, None), P())
    return jax.shard_map(
        per_device, mesh=mesh, in_specs=in_specs, out_specs=out_specs, check_vma=False
    )
```

```python
import functools
import math

import jax
import jax.numpy as jnp
from jax import lax
from jax.experimental import pallas as pl
from jax.experimental.pallas import tpu as pltpu
from jax.sharding import PartitionSpec as P

STEPS = 4
EPS = 1e-06
MIB = 1024 * 1024
HI = lax.Precision.HIGHEST
FIRST = 3
SCALARS = pl.BlockSpec(memory_space=pltpu.SMEM)


def mm(left, right, dims, precision=HI):
    return lax.dot_general(left, right, (dims, ((), ())), precision=precision, preferred_element_type=jnp.float32)


def shape(*dims, dtype=jnp.float32):
    return jax.ShapeDtypeStruct(dims, dtype)


def params(mib):
    return pltpu.CompilerParams(vmem_limit_bytes=mib * MIB)


def in_hbm(value):
    return pltpu.with_memory_space_constraint(value, pltpu.HBM)


def halves(value):
    high = value.astype(jnp.bfloat16)
    return high, (value - high.astype(jnp.float32)).astype(jnp.bfloat16)


def thirds(value):
    high, _ = halves(value)
    rest = value - high.astype(jnp.float32)
    return (high,) + halves(rest)


def mm3(left, right, dims):
    (lh, ll), (rh, rl) = left, right
    (over,), (under,) = dims
    return mm(jnp.concatenate([ll, lh, lh], axis=over), jnp.concatenate([rh, rl, rh], axis=under), dims, None)


def xor_permute(value, axis, mask):
    size = lax.axis_size(axis)
    return lax.ppermute(value, axis, [(i, i ^ mask) for i in range(size)])


def edges_kernel(stiff_ref, disp_low, vel_low, disp_high, vel_high, last_ref, first_ref):
    w = STEPS
    lines = stiff_ref.shape[0]
    for ref, disp, vel, at, start in ((last_ref, disp_high, vel_high, 8 - w, lines - w), (first_ref, disp_low, vel_low, 0, 0)):
        skip = 1 if ref is last_ref else 0
        for i in range(w):
            ref[i] = disp[:, at + i, :]
        for i in range(w - 1):
            ref[w + i] = vel[:, at + skip + i, :]
        ref[2 * w - 1] = jnp.zeros_like(ref[2 * w - 1])
        ref[2 * w - 1, :w, :] = stiff_ref[start:start + w, :]


def edges(disp, vel, stiff):
    members, lines, width = disp.shape
    w = STEPS
    low = pl.BlockSpec((members, 8, width), lambda i: (0, 0, 0))
    high = pl.BlockSpec((members, 8, width), lambda i: (0, lines // 8 - 1, 0))
    edge = pl.BlockSpec((2 * w, members, width), lambda i: (0, 0, 0))
    return pl.pallas_call(
        edges_kernel,
        grid=(1,),
        in_specs=[pl.BlockSpec((lines, width), lambda i: (0, 0)), low, low, high, high],
        out_specs=[edge, edge],
        out_shape=[shape(2 * w, members, width)] * 2,
        compiler_params=params(6),
        name="edges",
    )(in_hbm(stiff), in_hbm(disp), in_hbm(vel), in_hbm(disp), in_hbm(vel))


def to_lines_kernel(disp_ref, vel_ref, disp_out, vel_out):
    lines, group, _ = disp_out.shape
    for line in range(lines):
        disp_out[line] = disp_ref[pl.ds(line, group, stride=lines), :]
        vel_out[line] = vel_ref[pl.ds(line, group, stride=lines), :]


def to_lines(disp, vel):
    members, lines, width = disp.shape
    group = 16
    flat = pl.BlockSpec((group * lines, width), lambda i: (i, 0))
    out = pl.BlockSpec((lines, group, width), lambda i: (0, i, 0))
    return pl.pallas_call(
        to_lines_kernel,
        grid=(members // group,),
        in_specs=[flat, flat],
        out_specs=[out, out],
        out_shape=[shape(lines, members, width)] * 2,
        compiler_params=params(8),
        name="to_lines",
    )(in_hbm(disp.reshape(members * lines, width)), in_hbm(vel.reshape(members * lines, width)))


def evolve_kernel(index_ref, disp_ref, vel_ref, stiff_ref, before_ref, after_ref, *rest, slots):
    outs, (even_ref, odd_ref, speed_ref, pad_ref, all_ref, sem) = rest[:slots], rest[slots:]
    lines, members, width = disp_ref.shape
    w = STEPS
    full = lines + 2 * w
    size = lines // slots
    lane = lax.broadcasted_iota(jnp.int32, (8, width), 1)
    pad_ref[w:2 * w, :] = before_ref[2 * w - 1, :w, :]
    pad_ref[8:8 + lines, :] = stiff_ref[...]
    pad_ref[8 + lines:8 + lines + w, :] = after_ref[2 * w - 1, :w, :]

    def group_step(g, carry):
        at = pl.ds(pl.multiple_of(g * 8, 8), 8)
        for i in range(w):
            even_ref[i], even_ref[w + lines + i] = before_ref[i, at, :], after_ref[i, at, :]
        for i in range(w - 1):
            speed_ref[1 + i], speed_ref[w + lines + i] = before_ref[w + i, at, :], after_ref[w + i, at, :]
        for i in range(lines):
            even_ref[w + i], speed_ref[w + i] = disp_ref[i, at, :], vel_ref[i, at, :]
        now, then = even_ref, odd_ref
        for step in range(1, w + 1):
            for i in range(step, full - step):
                u = now[i]
                right = jnp.where(lane == width - 1, 0.0, pltpu.roll(u, width - 1, 1))
                left = jnp.where(lane == 0, 0.0, pltpu.roll(u, 1, 1))
                around = (now[i + 1] + now[i - 1]) + (right + left)
                stiff = jnp.broadcast_to(pad_ref[8 - w + i:8 - w + i + 1, :], (8, width))
                speed = speed_ref[i] + stiff * (around + u * (0.5 / (1.0 + u * u) - 4.5))
                if step < w:
                    then[i], speed_ref[i] = u + speed, speed
                else:
                    all_ref[i - w, at, :] = u + speed
            now, then = then, now
        for slot, out in enumerate(outs):
            pltpu.make_async_copy(all_ref.at[block(slot), at], out.at[:, at], sem.at[slot]).start()
        return carry

    def block(slot):
        return pl.ds((index_ref[0] ^ index_ref[FIRST + slot]) * size, size)

    lax.fori_loop(0, members // 8, group_step, 0)
    for slot, out in enumerate(outs):
        pltpu.make_async_copy(all_ref.at[block(slot)], out, sem.at[slot]).wait()


def evolve(index, disp, vel, stiff, before, after, slots):
    lines, members, width = disp.shape
    line = pltpu.VMEM((lines + 2 * STEPS, 8, width), jnp.float32)
    return pl.pallas_call(
        functools.partial(evolve_kernel, slots=slots),
        in_specs=[SCALARS] + [pl.BlockSpec(memory_space=pltpu.VMEM)] * 5,
        out_shape=[pltpu.HBM((lines // slots, members, width), jnp.float32)] * slots,
        out_specs=[pl.BlockSpec(memory_space=pltpu.HBM)] * slots,
        scratch_shapes=[line, line, line, pltpu.VMEM((lines + 16, width), jnp.float32),
                        pltpu.VMEM((lines, members, width), jnp.float32), pltpu.SemaphoreType.DMA((slots,))],
        compiler_params=params(8),
        name="evolve",
    )(index, disp, vel, stiff, before, after)


def room(*arrays):
    return pl.pallas_call(
        lambda *refs: None,
        out_specs=[pl.BlockSpec(memory_space=pl.ANY)] * len(arrays),
        out_shape=[pltpu.HBM(a.shape, a.dtype) for a in arrays],
        name="room",
    )()


def basis_kernel(index_ref, rot_ref, basis_ref, send_ref, keep_ref, high_ref, low_ref, turned_ref, sum_ref, mixed_ref):
    lines, width, rank = basis_ref.shape
    step = pl.program_id(0)

    @pl.when(step == 0)
    def _():
        sum_ref[...] = jnp.zeros_like(sum_ref)
        mixed_ref[...] = jnp.zeros_like(mixed_ref)

    high, low = halves(basis_ref[...].reshape(lines * width, rank))
    high_ref[...] = high
    low_ref[...] = low
    sum_ref[...] += mm(high, high, ((0,), (0,)), None)
    mixed_ref[...] += mm(high, low, ((0,), (0,)), None)
    turned_ref[...] = mm3((high, low), halves(rot_ref[...]), ((1,), (0,)))

    @pl.when(step == pl.num_programs(0) - 1)
    def _():
        sum_ref[...] += mixed_ref[...] + mixed_ref[...].T
        half = keep_ref.shape[0]
        core = index_ref[1]
        keep_ref[...] = sum_ref[pl.ds(pl.multiple_of(core * half, half), half), :]
        send_ref[...] = sum_ref[pl.ds(pl.multiple_of((1 - core) * half, half), half), :]


def basis_parts(index, basis, rotation):
    lines, width, rank = basis.shape
    block = 4
    half = pl.BlockSpec((rank // 2, rank), lambda i: (0, 0))
    rows = pl.BlockSpec((block * width, rank), lambda i: (i, 0))
    return pl.pallas_call(
        basis_kernel,
        grid=(lines // block,),
        in_specs=[SCALARS, pl.BlockSpec((rank, rank), lambda i: (0, 0)), pl.BlockSpec((block, width, rank), lambda i: (i, 0, 0))],
        out_specs=[half, half, rows, rows, rows],
        out_shape=[shape(rank // 2, rank)] * 2 + [pltpu.HBM((lines * width, rank), jnp.bfloat16)] * 2
        + [pltpu.HBM((lines * width, rank), jnp.float32)],
        scratch_shapes=[pltpu.VMEM((rank, rank), jnp.float32)] * 2,
        compiler_params=params(24),
        name="basis_parts",
    )(index, in_hbm(rotation), in_hbm(basis))


def products_kernel(index_ref, high_ref, low_ref, *rest):
    pieces, (send_ref, keep_ref, snap_ref, sum_ref, mixed_ref) = rest[:-5], rest[-5:]
    lines, members, width = pieces[0].shape
    rank = high_ref.shape[-1]
    step = pl.program_id(0)
    for k, piece in enumerate(pieces):
        at = pl.multiple_of((index_ref[0] ^ index_ref[FIRST + k]) * members, members)
        for line in range(lines):
            snap_ref[pl.ds(at, members), line * width:(line + 1) * width] = piece[line]

    @pl.when(step == 0)
    def _():
        sum_ref[...] = jnp.zeros_like(sum_ref)
        mixed_ref[...] = jnp.zeros_like(mixed_ref)

    snap = halves(snap_ref[...])
    sum_ref[:, :rank] += mm3(snap, (high_ref[...], low_ref[...]), ((1,), (0,)))
    sum_ref[:, rank:] += mm(snap[0], snap[0], ((1,), (1,)), None)
    mixed_ref[...] += mm(snap[0], snap[1], ((1,), (1,)), None)

    @pl.when(step == pl.num_programs(0) - 1)
    def _():
        sum_ref[:, rank:] += mixed_ref[...] + mixed_ref[...].T
        half = keep_ref.shape[0]
        core = index_ref[1]
        keep_ref[...] = sum_ref[pl.ds(pl.multiple_of(core * half, half), half), :]
        send_ref[...] = sum_ref[pl.ds(pl.multiple_of((1 - core) * half, half), half), :]


def products(index, high, low, pieces):
    rank = high.shape[1]
    lines, members, width = pieces[0].shape
    total = members * len(pieces)
    block = 8
    half = pl.BlockSpec((total // 2, rank + total), lambda i: (0, 0))
    return pl.pallas_call(
        products_kernel,
        grid=(lines // block,),
        in_specs=[SCALARS] + [pl.BlockSpec((block * width, rank), lambda i: (i, 0))] * 2
        + [pl.BlockSpec((block, members, width), lambda i: (i, 0, 0))] * len(pieces),
        out_specs=[half, half],
        out_shape=[shape(total // 2, rank + total)] * 2,
        scratch_shapes=[pltpu.VMEM((total, block * width), jnp.float32), pltpu.VMEM((total, rank + total), jnp.float32),
                        pltpu.VMEM((total, total), jnp.float32)],
        compiler_params=params(22),
        name="products",
    )(index, in_hbm(high), in_hbm(low), *pieces)


def split_kernel(index_ref, keep_ref, got_ref, *outs):
    rows = outs[0].shape[0]
    for k, out in enumerate(outs):
        at = pl.ds(pl.multiple_of((index_ref[2] ^ k) * rows, rows), rows)
        out[...] = keep_ref[at, :] + got_ref[at, :]


def split(index, keep, got, chips):
    rows, cols = keep.shape
    return pl.pallas_call(
        split_kernel,
        in_specs=[SCALARS] + [pl.BlockSpec(memory_space=pltpu.VMEM)] * 2,
        out_shape=[shape(rows // chips, cols)] * chips,
        compiler_params=params(4),
        name="split",
    )(index, keep, got)


def tree_sum(values):
    while len(values) > 1:
        values = [a + b for a, b in zip(values[::2], values[1::2])]
    return values[0]


def ana_sum_by_pairs(value, bits):
    for bit in bits:
        value = value + xor_permute(value, "ana", bit)
    return value


def exchange_chips(pieces, limit):
    found = []
    for k in range(1, len(pieces)):
        piece = pieces[k]
        if k > limit:
            piece, found[k - limit - 1] = lax.optimization_barrier((piece, found[k - limit - 1]))
        found.append(xor_permute(piece, "sim", 2 * k))
    return found


def chip_scatter(index, send, keep, limit):
    chips = lax.axis_size("sim") // 2
    got = xor_permute(send, "sim", 1)
    pieces = split(index, keep, got, chips)
    return tree_sum([pieces[0]] + exchange_chips(pieces, limit))


def ana_sum(value):
    return tree_sum([value] + [xor_permute(value, "ana", k) for k in range(1, lax.axis_size("ana"))])


def chip_gather(value, limit):
    chips = lax.axis_size("sim") // 2
    return jnp.concatenate([value] + exchange_chips([value] * chips, limit), axis=0)


def with_other_core(value):
    return value, xor_permute(value, "sim", 1)


PANEL = 32

def eliminate(work_ref, members, aside):
    tiles = work_ref.shape[1] // 128
    groups = PANEL // 8
    sub = lax.broadcasted_iota(jnp.int32, (8, 128), 0)

    def panel_step(k, carry):
        aside(k)
        start = pl.multiple_of(k * PANEL, PANEL)
        at = pl.multiple_of((k * PANEL) // 128 * 128, 128)
        diag = work_ref[pl.ds(start, PANEL), pl.ds(at, 128)]
        diag = pltpu.roll(diag, (128 - (k * PANEL) % 128) % 128, 1)
        rows = work_ref[pl.ds(start, PANEL), :]
        x = [[rows[8 * g:8 * g + 8, 128 * t:128 * t + 128] for t in range(tiles)] + [diag[8 * g:8 * g + 8]]
             for g in range(groups)]
        for b in range(groups):
            cols = {g: [jnp.broadcast_to(x[g][tiles][:, 8 * b + j:8 * b + j + 1], (8, 128)) for j in range(8)]
                    for g in range(b, groups)}
            pivots = jnp.ones((8, 128), jnp.float32)
            for r in range(8):
                pivot = jnp.broadcast_to(cols[b][r][r:r + 1], (8, 128))
                pivots = jnp.where(sub == r, pivot, pivots)
                inverse = 1.0 / pivot
                raw = [jnp.broadcast_to(v[r:r + 1], (8, 128)) for v in x[b]]
                craw = [jnp.broadcast_to(cols[b][j][r:r + 1], (8, 128)) if j > r else None for j in range(8)]
                for g in range(b, groups):
                    coef = cols[g][r] * inverse
                    if g == b:
                        coef = jnp.where(sub > r, coef, 0.0)
                    x[g] = [v - coef * w for v, w in zip(x[g], raw)]
                    cols[g] = [cols[g][j] - coef * craw[j] if j > r else cols[g][j] for j in range(8)]
            x[b] = [v * lax.rsqrt(pivots) for v in x[b]]
        done = jnp.concatenate([jnp.concatenate(v[:tiles], axis=1) for v in x], axis=0)
        lane = lax.broadcasted_iota(jnp.int32, (PANEL, members), 1)
        lower = jnp.where(lane >= start + PANEL, done[:, :members], 0.0)
        lh, lm, ll = thirds(lower)
        dh, dm, dl = thirds(done)
        left = jnp.concatenate([lh, lh, lm, lh, ll, lm], axis=0)
        right = jnp.concatenate([dh, dm, dh, dl, dh, dm], axis=0)
        work_ref[...] = work_ref[...] - mm(left, right, ((0,), (0,)), None)
        work_ref[pl.ds(start, PANEL), :] = done
        return carry

    lax.fori_loop(0, members // PANEL, panel_step, 0)


def ordered(index_ref, mine_ref, other_ref, out_ref, chips):
    half = mine_ref.shape[0]
    rows = half // chips
    for k in range(chips):
        at = (index_ref[2] ^ k) * rows
        piece = slice(k * rows, (k + 1) * rows)
        out_ref[pl.ds(pl.multiple_of(index_ref[1] * half + at, rows), rows), :] = mine_ref[piece, :]
        out_ref[pl.ds(pl.multiple_of((1 - index_ref[1]) * half + at, rows), rows), :] = other_ref[piece, :]


def solve_kernel(index_ref, sums_ref, sums2_ref, gram_ref, gram2_ref, rot_ref, high_hbm, low_hbm, turned_hbm, *rest, count, chips, ranks):
    pieces, rest = rest[:ranks], rest[ranks:]
    out_hbm, coords_ref, work_ref, all_ref, basis_ref, high_ref, low_ref, snap_ref, rem_high, rem_low, out_ref, sem, out_sem = rest
    rank, members = coords_ref.shape
    each = members // ranks
    copies = [pltpu.make_async_copy(high_hbm, high_ref, sem.at[0]), pltpu.make_async_copy(low_hbm, low_ref, sem.at[1])]
    for k, piece in enumerate(pieces):
        at = pl.multiple_of((index_ref[0] ^ index_ref[FIRST + k]) * each, each)
        copies.append(pltpu.make_async_copy(piece, snap_ref.at[:, pl.ds(at, each), :], sem.at[2 + k]))
    turned = pltpu.make_async_copy(turned_hbm, out_ref, out_sem)
    for copy in copies + [turned]:
        copy.start()
    ordered(index_ref, sums_ref, sums2_ref, all_ref, chips)
    ordered(index_ref, gram_ref, gram2_ref, basis_ref, chips)
    row = lax.broadcasted_iota(jnp.int32, (members, members), 0)
    col = lax.broadcasted_iota(jnp.int32, (members, members), 1)
    eye = row == col
    inner = all_ref[:, rank:]
    diag = jnp.where(eye, inner, 0.0)
    across = lax.rsqrt(jnp.sum(diag, axis=0, keepdims=True) / count + EPS)
    along = lax.rsqrt(jnp.sum(diag, axis=1, keepdims=True) / count + EPS)
    coef = all_ref[:, :rank] * (along / count)
    correct = 2.0 * coef - mm(coef, basis_ref[...], ((1,), (0,))) / count
    work_ref[:, :members] = inner * (along / count) * across - mm(correct, coef, ((1,), (1,)))
    work_ref[:, members:] = jnp.where(eye, 1.0, 0.0)
    all_ref[:, :rank] = coef
    for copy in copies:
        copy.wait()
    lines, _, width = snap_ref.shape
    block = lines // (members // PANEL)

    def remainder(k):
        at = pl.ds(pl.multiple_of(k * (block * width), block * width), block * width)
        taken = mm3((high_ref[at, :], low_ref[at, :]), halves(all_ref[:, :rank]), ((1,), (1,)))
        panel = jnp.concatenate([snap_ref[k * block + i].T for i in range(block)], axis=0) * across
        rem_high[at, :], rem_low[at, :] = halves(panel - taken)

    eliminate(work_ref, members, remainder)
    coefs, tops, bottoms = halves(all_ref[:, :rank]), halves(rot_ref[:rank, :]), halves(rot_ref[rank:, :])
    mix_high, mix_low = halves(mm3(halves(work_ref[:, members:]), bottoms, ((0,), (0,))))
    turned.wait()
    step = 2 * block
    for first in range(0, lines, step):
        at = slice(first * width, (first + step) * width)
        done = mm3((rem_high[at, :], rem_low[at, :]), (mix_high, mix_low), ((1,), (0,)))
        out_ref[first:first + step] += done.reshape(step, width, rank)
        pltpu.make_async_copy(out_ref.at[pl.ds(first, step)], out_hbm.at[pl.ds(first, step)], out_sem).start()
    upper = jnp.where(row <= col, work_ref[:, :members], 0.0)
    coords = (mm3(coefs, tops, ((1,), (0,))) + mm3(halves(upper), bottoms, ((0,), (0,)))) * math.sqrt(rank)
    coords_ref[...] = coords.T
    pltpu.make_async_copy(out_ref, out_hbm, out_sem).wait()


def solve(index, sums, gram, rotation, high, low, turned, pieces, count, chips):
    rows, rank = high.shape
    members = rotation.shape[0] - rank
    ranks = len(pieces)
    lines, each, width = pieces[0].shape
    half = jnp.bfloat16
    return pl.pallas_call(
        functools.partial(solve_kernel, count=float(count), chips=chips, ranks=ranks),
        in_specs=[SCALARS] + [pl.BlockSpec(memory_space=pltpu.VMEM)] * 5 + [pl.BlockSpec(memory_space=pl.ANY)] * (3 + ranks),
        out_specs=[pl.BlockSpec(memory_space=pltpu.HBM), pl.BlockSpec(memory_space=pltpu.VMEM)],
        out_shape=[pltpu.HBM((lines, width, rank), jnp.float32), shape(rank, members)],
        scratch_shapes=[pltpu.VMEM((members, 2 * members), jnp.float32),
                        pltpu.VMEM((members, rank + members), jnp.float32),
                        pltpu.VMEM((rank, rank), jnp.float32),
                        pltpu.VMEM((rows, rank), half), pltpu.VMEM((rows, rank), half),
                        pltpu.VMEM((lines, members, width), jnp.float32),
                        pltpu.VMEM((rows, members), half), pltpu.VMEM((rows, members), half),
                        pltpu.VMEM((lines, width, rank), jnp.float32),
                        pltpu.SemaphoreType.DMA((2 + ranks,)), pltpu.SemaphoreType.DMA],
        compiler_params=params(36),
        name="solve",
    )(index, *sums, *gram, rotation, high, low, in_hbm(turned.reshape(lines, width, rank)), *pieces)


def per_device(initial_disp, initial_vel, stiffness, basis, rotation):
    ranks, sims = lax.axis_size("ana"), lax.axis_size("sim")
    ana, sim = lax.axis_index("ana"), lax.axis_index("sim")
    lines, width, rank = basis.shape
    count = lines * width * sims * ranks
    chips = sims // 2
    core = sim % 2
    slots = list(range(1, ranks)) + [0]
    masks = jnp.array(slots)
    first_index = jnp.stack([ana, core, sim // 2])
    index = jnp.concatenate([first_index, masks]).astype(jnp.int32)

    last, first = edges(initial_disp, initial_vel, stiffness)
    up = [(i, i + 1) for i in range(sims - 1)]
    before = lax.ppermute(last, "sim", up)
    after = lax.ppermute(first, "sim", [(j, i) for i, j in up])
    late_disp, late_vel, _ = lax.optimization_barrier((initial_disp, initial_vel, last[0, 0, 0]))
    disp, vel = to_lines(late_disp, late_vel)
    before, after, disp = lax.optimization_barrier((before, after, disp))

    pieces = list(evolve(index, disp, vel, stiffness, before, after, ranks))
    order, pieces = lax.optimization_barrier((index, pieces))
    for slot in range(ranks - 1):
        pieces[slot] = xor_permute(pieces[slot], "ana", slots[slot])

    def meanwhile(_, carry):
        at, *_ = carry
        send, keep, high, low, turned = basis_parts(at, basis, rotation)
        return at + (at >> 20), ana_sum_by_pairs(chip_scatter(at, send, keep, 2), bits[:-1]), high, low, turned

    bits = [2 ** i for i in range(ranks.bit_length() - 1)]
    empty = room(*[shape(lines * width, rank, dtype=t) for t in (jnp.bfloat16, jnp.bfloat16, jnp.float32)])
    order, gram, high, low, turned = lax.fori_loop(
        0, 1 + (ana >> 20), meanwhile, (order, jnp.zeros((rank // sims, rank), jnp.float32), *empty))
    gram_rest = xor_permute(gram, "ana", bits[-1])

    send, keep = products(order, high, low, pieces)
    sums = chip_scatter(order, send, keep, chips)
    sums, gram, gram_rest = lax.optimization_barrier((sums, gram, gram_rest))
    gram = chip_gather(gram + gram_rest, chips)
    sums = ana_sum(sums)
    sums = with_other_core(chip_gather(sums, chips))
    gram = with_other_core(gram)
    return tuple(solve(index, sums, gram, rotation, high, low, turned, pieces, count, chips))


def solution(mesh):
    in_specs = (
        P("ana", "sim", None),
        P("ana", "sim", None),
        P("sim", None),
        P(("sim", "ana"), None, None),
        P(),
    )
    out_specs = (P(("sim", "ana"), None, None), P())
    return jax.shard_map(
        per_device, mesh=mesh, in_specs=in_specs, out_specs=out_specs, check_vma=False
    )
```
